128 devices in a mesh: member: 16 (over z, x_lo, core), tensor: 8 (over y, x_hi).
Axes of the slice: x: 4 (x_hi: 2, x_lo: 2; x = x_hi * 2 + x_lo), y: 4, z: 4, core: 2. Of those that a mesh axis runs over, the one named last changes fastest.
Arguments:
- query: bfloat16 [8192, 8192], P('member', 'tensor'), may hold values from -100 to 100
- keys: bfloat16 [8192, 1024], P('member', 'tensor'), may hold values from -6 to 6
- values: bfloat16 [8192, 1024], P('member', 'tensor'), may hold values from -12 to 12
- residual: bfloat16 [8192, 8192], P('member', 'tensor'), may hold values from -6 to 6
- out_weight: bfloat16 [8192, 8192], P('tensor', 'member'), may hold values from -0.0625 to 0.0625
- norm_gain: float32 [8192], replicated, may hold values from 0.1 to 1.9
- cand_len: int32 [64], P('member'), may hold values from 32 to 128, as said below
- head_w1: bfloat16 [16, 8192, 4096], P('member', None, 'tensor'), may hold values from -0.0625 to 0.0625
- head_b1: float32 [16, 4096], P('member', 'tensor'), may hold values from -3 to 3
- head_w2: bfloat16 [16, 4096, 4096], P('member', 'tensor'), may hold values from -0.09375 to 0.09375
- head_b2: float32 [16, 4096], P('member'), may hold values from -3 to 3
- head_w3: bfloat16 [16, 4096], P('member'), may hold values from -0.09375 to 0.09375
- head_b3: float32 [16], P('member'), may hold values from -4 to 4
Outputs:
- trunk_out: bfloat16 [8192, 8192], P('member', 'tensor')
- scores: float32 [16, 64], P('member')
The draws below stay inside these ranges and needn't reach their ends.
Inputs may be any that keep to these rules, and one draw needn't show every extreme that they name: Token slots of candidate c at places cand_len[c] and beyond are padding: excluded as keys, and the slot at place cand_len[c] - 1 is the one that is scored.
All inputs are finite; a program needn't handle non-finite values.
Results may differ from the reference program's by a relative error of at most 0.014.
Values may be sent and summed in bfloat16 or wider, within the bound.
No kernel may reach another device: no remote copies, remote signals or barrier semaphores. Data moves between devices by JAX's collectives and lax.ppermute only.
A program may use at most 192 MiB of HBM per device.

```python
import jax
import jax.numpy as jnp
from jax import lax

D = 8192
QUERY_HEADS = 64
KEY_VALUE_HEADS = 8
HEAD_WIDTH = 128
HID = 4096
SEQUENCE_SLOTS = 128
CANDIDATE_TOTAL = 64
TOKEN_SLOTS = 8192
HEADS = 16
N_TENSOR = 8


def query_key_pair(key):
    initial_keys = jnp.clip(jax.random.normal(jax.random.fold_in(key, 101), (TOKEN_SLOTS, KEY_VALUE_HEADS * HEAD_WIDTH), jnp.float32), -5.0, 5.0)
    base_query = jnp.clip(jax.random.normal(jax.random.fold_in(key, 202), (TOKEN_SLOTS, QUERY_HEADS * HEAD_WIDTH), jnp.float32), -5.0, 5.0)
    return (base_query, initial_keys)


def draw_query(key, part):
    return query_key_pair(key)[0].astype(jnp.bfloat16)


def draw_keys(key, part):
    return query_key_pair(key)[1].astype(jnp.bfloat16)


def draw_cand_len(key, part):
    drawn = jax.random.randint(jax.random.fold_in(key, 404), (CANDIDATE_TOTAL,), SEQUENCE_SLOTS // 4, SEQUENCE_SLOTS + 1)
    places = jnp.arange(CANDIDATE_TOTAL)
    drawn = jnp.where(places == 0, SEQUENCE_SLOTS // 4, drawn)
    drawn = jnp.where(places == 1, SEQUENCE_SLOTS, drawn)
    return drawn.astype(jnp.int32)


def shard_levels(key, extent, shards, low, high):
    def one(dim, blocks):
        heights = jax.random.uniform(jax.random.fold_in(jax.random.fold_in(key, 6), dim), (blocks,), jnp.float32, low / len(shards), high / len(shards))
        return jnp.repeat(jnp.exp(heights), extent[dim] // blocks).reshape((-1,) + (1,) * (len(extent) - dim - 1))

    level = one(*shards[0])
    for cut in shards[1:]:
        level = level * one(*cut)
    return level


def bell_draw(stream_key, extent, scale, bound, split=(), held_as=jnp.bfloat16):
    entries = jax.random.normal(stream_key, extent, jnp.float32) * scale
    if len(split) > 0:
        entries = shard_levels(stream_key, extent, split, -0.22, 0.18) * entries
    return jnp.clip(entries, min=-bound, max=bound).astype(held_as)


def setup_inputs(seed: int = 0) -> dict:
    streams_of = jax.random.split(jax.random.key(seed), 14)
    query = draw_query(jax.random.fold_in(streams_of[13], 71), 0)
    keys = draw_keys(jax.random.fold_in(streams_of[13], 71), 0)
    values = bell_draw(streams_of[2], (TOKEN_SLOTS, KEY_VALUE_HEADS * HEAD_WIDTH), 2.0, 12.0, ((0, 16), (1, 8)))
    residual = bell_draw(streams_of[3], (TOKEN_SLOTS, D), 1.0, 6.0, ((0, 16), (1, 8)))
    out_weight = bell_draw(streams_of[4], (QUERY_HEADS * HEAD_WIDTH, D), (QUERY_HEADS * HEAD_WIDTH) ** -0.5, 0.0625, ((0, 8), (1, 16)))
    norm_gain = jnp.clip(1.0 + 0.18 * jax.random.normal(streams_of[5], (D,), jnp.float32), 0.1, 1.9)
    cand_len = draw_cand_len(jax.random.fold_in(streams_of[13], 71), 0)
    head_w1 = bell_draw(streams_of[7], (HEADS, D, HID), D ** -0.5, 0.0625, ((0, 16), (2, 8)))
    head_b1 = bell_draw(streams_of[8], (HEADS, HID), 0.5, 3.0, ((0, 16), (1, 8)), jnp.float32)
    head_w2 = bell_draw(streams_of[9], (HEADS, HID, HID), HID ** -0.5, 0.09375, ((0, 16), (1, 8)))
    head_b2 = bell_draw(streams_of[10], (HEADS, HID), 0.5, 3.0, ((0, 16),), jnp.float32)
    head_w3 = bell_draw(streams_of[11], (HEADS, HID), HID ** -0.5, 0.09375, ((0, 16),))
    head_b3 = bell_draw(streams_of[12], (HEADS,), 1.0, 4.0, ((0, 16),), jnp.float32)
    return {"query": query, "keys": keys, "values": values, "residual": residual, "out_weight": out_weight, "norm_gain": norm_gain, "cand_len": cand_len, "head_w1": head_w1, "head_b1": head_b1, "head_w2": head_w2, "head_b2": head_b2, "head_w3": head_w3, "head_b3": head_b3}


def reference(query, keys, values, residual, out_weight, norm_gain, cand_len, head_w1, head_b1, head_w2, head_b2, head_w3, head_b3):
    group_width = QUERY_HEADS // KEY_VALUE_HEADS
    query_tiles = query.astype(jnp.float32).reshape(CANDIDATE_TOTAL, SEQUENCE_SLOTS, KEY_VALUE_HEADS, group_width, HEAD_WIDTH)
    key_tiles = keys.astype(jnp.float32).reshape(CANDIDATE_TOTAL, SEQUENCE_SLOTS, KEY_VALUE_HEADS, HEAD_WIDTH)
    value_tiles = values.astype(jnp.float32).reshape(CANDIDATE_TOTAL, SEQUENCE_SLOTS, KEY_VALUE_HEADS, HEAD_WIDTH)
    logits = jnp.einsum('cskgd,ctkd->ckgst', query_tiles, key_tiles) * HEAD_WIDTH ** (-0.5)
    places = jnp.arange(SEQUENCE_SLOTS, dtype=jnp.int32)
    allowed = (places[None, :, None] >= places[None, None, :]) & (places[None, None, :] < cand_len[:, None, None])
    allowed = allowed[:, None, None]
    logits = jnp.where(allowed, logits, jnp.float32(-1e+30))
    row_max = lax.optimization_barrier(jnp.max(logits, axis=-1, keepdims=True))
    probs = jnp.where(allowed, jnp.exp(logits - row_max), jnp.float32(0.0))
    totals = lax.optimization_barrier(jnp.sum(probs, axis=-1, keepdims=True))
    attn_weights = (probs / totals).astype(jnp.bfloat16)
    attn_out = jnp.einsum('ckgst,ctkd->cskgd', attn_weights.astype(jnp.float32), value_tiles)
    attn_out = attn_out.astype(jnp.bfloat16).reshape(TOKEN_SLOTS, QUERY_HEADS * HEAD_WIDTH)
    col_width = QUERY_HEADS * HEAD_WIDTH // N_TENSOR
    summed = jnp.zeros((TOKEN_SLOTS, D), jnp.float32)
    for shard in range(N_TENSOR):
        piece_sum = jnp.dot(attn_out[:, shard * col_width:(shard + 1) * col_width], out_weight[shard * col_width:(shard + 1) * col_width], preferred_element_type=jnp.float32)
        summed = summed + piece_sum.astype(jnp.bfloat16).astype(jnp.float32)
    trunk_out = (summed + residual.astype(jnp.float32)).astype(jnp.bfloat16)
    last_rows = jnp.arange(CANDIDATE_TOTAL, dtype=jnp.int32) * SEQUENCE_SLOTS + cand_len - 1
    pooled = jnp.take(trunk_out, last_rows, axis=0).astype(jnp.float32)
    mean_square = lax.optimization_barrier(jnp.mean(pooled * pooled, axis=-1, keepdims=True)) + 1e-05
    features = (pooled * lax.rsqrt(mean_square) * norm_gain).astype(jnp.bfloat16)
    score_rows = []
    for member_head in range(HEADS):
        first = jax.nn.silu(jnp.dot(features, head_w1[member_head], preferred_element_type=jnp.float32) + head_b1[member_head]).astype(jnp.bfloat16)
        second = jax.nn.silu(jnp.dot(first, head_w2[member_head], preferred_element_type=jnp.float32) + head_b2[member_head])
        score_rows.append(lax.optimization_barrier(jnp.sum(second * head_w3[member_head].astype(jnp.float32), axis=-1)) + head_b3[member_head])
    scores = jnp.stack(score_rows, axis=0)
    return (trunk_out, scores)
```

```python
import functools

import jax
import jax.numpy as jnp
from jax import lax
from jax.experimental import pallas as pl
from jax.experimental.pallas import tpu as pltpu
from jax.sharding import Mesh, PartitionSpec as P

HEAD_WIDTH = 128
SEQUENCE_SLOTS = 128
Z, XL, CORE, Y, XH = 4, 2, 2, 4, 2
MEMBER = ("z", "xl", "core")
TENSOR = ("y", "xh")
ALL = MEMBER + TENSOR


def flat(z, xl, core, y, xh):
    return (((z % Z) * XL + xl % XL) * CORE + core) * Y * XH + (y % Y) * XH + xh % XH


def weight_moves():
    return [
        (flat(z, xl, core, y, xh), flat(y - z, xh - xl, core, z, xl))
        for z in range(Z)
        for xl in range(XL)
        for core in range(CORE)
        for y in range(Y)
        for xh in range(XH)
    ]


def from_ahead(x, axis, size, step):
    return lax.ppermute(x, axis, [(i, (i - step) % size) for i in range(size)])


def attention(query, keys, values, cand_len):
    row_count = query.shape[0]
    cand_count = row_count // SEQUENCE_SLOTS
    heads_here = query.shape[1] // HEAD_WIDTH
    kv_here = keys.shape[1] // HEAD_WIDTH
    group_width = heads_here // kv_here
    query_tiles = query.reshape(cand_count, SEQUENCE_SLOTS, kv_here, group_width, HEAD_WIDTH)
    key_tiles = keys.reshape(cand_count, SEQUENCE_SLOTS, kv_here, HEAD_WIDTH)
    value_tiles = values.reshape(cand_count, SEQUENCE_SLOTS, kv_here, HEAD_WIDTH)
    logits = jnp.einsum(
        "cskgd,ctkd->ckgst", query_tiles, key_tiles, preferred_element_type=jnp.float32
    ) * HEAD_WIDTH ** (-0.5)
    places = jnp.arange(SEQUENCE_SLOTS, dtype=jnp.int32)
    allowed = (places[None, :, None] >= places[None, None, :]) & (
        places[None, None, :] < cand_len[:, None, None]
    )
    allowed = allowed[:, None, None]
    logits = jnp.where(allowed, logits, jnp.float32(-1e30))
    row_max = jnp.max(logits, axis=-1, keepdims=True)
    probs = jnp.where(allowed, jnp.exp(logits - row_max), jnp.float32(0.0))
    totals = jnp.sum(probs, axis=-1, keepdims=True)
    attn_weights = (probs / totals).astype(jnp.bfloat16)
    attn_out = jnp.einsum(
        "ckgst,ctkd->cskgd", attn_weights, value_tiles, preferred_element_type=jnp.float32
    )
    return attn_out.astype(jnp.bfloat16).reshape(row_count, heads_here * HEAD_WIDTH)


def trunk_kernel(*refs):
    acts, w_ref, residual_ref, out_ref = refs[:8], refs[8], refs[9], refs[10]
    total = residual_ref[...].astype(jnp.float32)
    for slot in range(8):
        total = total + jnp.dot(
            acts[slot][...], w_ref[slot, 0], preferred_element_type=jnp.float32
        )
    out_ref[...] = total.astype(jnp.bfloat16)


def trunk_matmul(acts, weights, residual):
    rows, depth = acts[0].shape
    half = weights.shape[-1]
    width = 256
    per = half // width
    whole = pl.BlockSpec((rows, depth), lambda j: (0, 0), pipeline_mode=pl.Buffered(1))
    tile = pl.BlockSpec((rows, width), lambda j: (0, j))
    return pl.pallas_call(
        trunk_kernel,
        grid=(CORE * per,),
        in_specs=[whole] * 8
        + [pl.BlockSpec((8, 1, depth, width), lambda j: (0, j // per, 0, j % per)), tile],
        out_specs=tile,
        out_shape=jax.ShapeDtypeStruct(residual.shape, jnp.bfloat16),
        compiler_params=pltpu.CompilerParams(vmem_limit_bytes=40 * 2**20),
        cost_estimate=pl.CostEstimate(
            flops=2 * rows * 8 * depth * CORE * half,
            bytes_accessed=2 * (8 * rows * depth + 8 * depth * CORE * half),
            transcendentals=0,
        ),
        name="trunk_matmul",
    )(*acts, weights, residual)


def norm_kernel(place_ref, p0, p1, p2, p3, gain_ref, out_ref):
    pieces = (p0, p1, p2, p3)
    z = place_ref[0]
    group = p0.shape[1] // Z
    width = p0.shape[2]
    per_z = p0.shape[0]
    scales = []
    for r in range(Z):
        square = jnp.zeros((group, 1), jnp.float32)
        for s in range(Z):
            for q in range(per_z):
                rows = pieces[s][q, pl.ds(((r - s) % Z) * group, group), :].astype(jnp.float32)
                square = square + jnp.sum(rows * rows, axis=-1, keepdims=True)
        scales.append(lax.rsqrt(square / (Z * per_z * width) + 1e-05))
    for s in range(Z):
        for q in range(per_z):
            start = pl.multiple_of((lax.rem(z + s, Z) * per_z + q) * width, width)
            gain = gain_ref[:, pl.ds(start, width)]
            for r in range(Z):
                rows = pieces[s][q, pl.ds(((r - s) % Z) * group, group), :].astype(jnp.float32)
                out_ref[pl.ds(r * group, group), pl.ds(start, width)] = (
                    rows * scales[r] * gain
                ).astype(jnp.bfloat16)


def normalize(pieces, gain, z):
    per_z, rows, width = pieces[0].shape
    total = Z * per_z * width
    return pl.pallas_call(
        norm_kernel,
        in_specs=[pl.BlockSpec(memory_space=pltpu.SMEM)]
        + [pl.BlockSpec(memory_space=pltpu.VMEM)] * 5,
        out_specs=pl.BlockSpec(memory_space=pltpu.VMEM),
        out_shape=jax.ShapeDtypeStruct((rows, total), jnp.bfloat16),
        cost_estimate=pl.CostEstimate(
            flops=8 * rows * total, bytes_accessed=4 * rows * total, transcendentals=rows
        ),
        name="normalize",
    )(z[None], *pieces, gain[None, :])


def local(
    query,
    keys,
    values,
    residual,
    out_weight,
    norm_gain,
    cand_len,
    head_w1,
    head_b1,
    head_w2,
    head_b2,
    head_w3,
    head_b3,
):
    z = lax.axis_index("z")
    xl = lax.axis_index("xl")
    core = lax.axis_index("core")
    y = lax.axis_index("y")
    xh = lax.axis_index("xh")
    cand_count = cand_len.shape[0]

    moved = lax.ppermute(out_weight, ALL, weight_moves())
    attn_out = attention(query, keys, values, cand_len)

    last_rows = jnp.arange(cand_count, dtype=jnp.int32) * SEQUENCE_SLOTS + cand_len - 1
    picked = jnp.concatenate(
        [jnp.take(attn_out, last_rows, axis=0), jnp.take(residual, last_rows, axis=0)], axis=1
    )
    near = lax.all_gather(picked, ("xl", "core"), axis=0, tiled=True)
    rows = jnp.concatenate([near] + [from_ahead(near, "z", Z, s) for s in (1, 2, 3)], axis=0)
    width = out_weight.shape[1]
    own = jnp.dot(rows[:, : attn_out.shape[1]], out_weight, preferred_element_type=jnp.float32)
    res = rows[:, attn_out.shape[1] :]
    res = jnp.where(core == 0, res[:, :width], res[:, width:]).astype(jnp.float32)
    own = jnp.where((y == z) & (xh == xl), own + res, own).astype(jnp.bfloat16)
    pair = jnp.stack([own, from_ahead(own, "xh", XH, 1)])
    parts = [pair] + [from_ahead(pair, "y", Y, s) for s in (1, 2, 3)]
    pooled = sum(jnp.sum(p.astype(jnp.float32), axis=0) for p in parts).astype(jnp.bfloat16)
    moved, bulk, _ = lax.optimization_barrier((moved, attn_out, pooled))
    near = lax.all_gather(pooled, ("xl", "core"), axis=0, tiled=False)
    pieces = [near] + [from_ahead(near, "z", Z, s) for s in (1, 2, 3)]
    features = normalize(pieces, norm_gain, z)
    first = jax.nn.silu(
        jnp.dot(features, head_w1[0], preferred_element_type=jnp.float32) + head_b1[0]
    ).astype(jnp.bfloat16)
    terms = jnp.dot(first, head_w2[0], preferred_element_type=jnp.float32).astype(jnp.bfloat16)
    count = terms.shape[0] // Y
    terms = lax.all_to_all(
        terms.reshape(Y, count, terms.shape[1]), "y", split_axis=0, concat_axis=0, tiled=True
    )
    half = jnp.sum(terms.astype(jnp.float32), axis=0).astype(jnp.bfloat16)
    other = from_ahead(half, "xh", XH, 1)
    second = jax.nn.silu(half.astype(jnp.float32) + other.astype(jnp.float32) + head_b2[0])
    mine = jnp.sum(second * head_w3[0].astype(jnp.float32), axis=-1) + head_b3[0]
    scores = lax.all_gather(mine, "y", axis=0, tiled=False)
    scores = jnp.roll(scores, z, axis=0).reshape(1, Y * count)

    weights = lax.all_gather(moved, MEMBER, axis=0, tiled=False)
    weights = weights.reshape((Z * XL, CORE) + out_weight.shape)
    acts = {}
    for e in range(XH):
        base = bulk if e == 0 else from_ahead(bulk, "xh", XH, 1)
        acts[0, e] = base
        for s in (1, 3, 2):
            acts[s, e] = from_ahead(base, "y", Y, s)
    ordered = [acts[s, e] for s in range(Y) for e in range(XH)]
    trunk_out = trunk_matmul(ordered, weights, residual)
    return (trunk_out, scores)


def solution(mesh):
    fine = Mesh(mesh.devices.reshape(Z, XL, CORE, Y, XH), ALL)
    in_specs = (
        P(MEMBER, TENSOR),
        P(MEMBER, TENSOR),
        P(MEMBER, TENSOR),
        P(MEMBER, TENSOR),
        P(TENSOR, MEMBER),
        P(),
        P(MEMBER),
        P(MEMBER, None, TENSOR),
        P(MEMBER, TENSOR),
        P(MEMBER, TENSOR, None),
        P(MEMBER, None),
        P(MEMBER, None),
        P(MEMBER),
    )
    out_specs = (P(MEMBER, TENSOR), P(MEMBER, None))
    return jax.shard_map(local, mesh=fine, in_specs=in_specs, out_specs=out_specs, check_vma=False)
```

```python
import functools

import jax
import jax.numpy as jnp
from jax import lax
from jax.experimental import pallas as pl
from jax.experimental.pallas import tpu as pltpu
from jax.sharding import Mesh, PartitionSpec as P

HEAD_WIDTH = 128
SEQUENCE_SLOTS = 128
Z, XL, CORE, Y, XH = 4, 2, 2, 4, 2
MEMBER = ("z", "xl", "core")
TENSOR = ("y", "xh")
ALL = MEMBER + TENSOR


def flat(z, xl, core, y, xh):
    return (((z % Z) * XL + xl % XL) * CORE + core) * Y * XH + (y % Y) * XH + xh % XH


def weight_moves():
    return [
        (flat(z, xl, core, y, xh), flat(y - z, xh - xl, core, z, xl))
        for z in range(Z)
        for xl in range(XL)
        for core in range(CORE)
        for y in range(Y)
        for xh in range(XH)
    ]


def from_ahead(x, axis, size, step):
    return lax.ppermute(x, axis, [(i, (i - step) % size) for i in range(size)])


def attention(query, keys, values, cand_len):
    row_count = query.shape[0]
    cand_count = row_count // SEQUENCE_SLOTS
    heads_here = query.shape[1] // HEAD_WIDTH
    kv_here = keys.shape[1] // HEAD_WIDTH
    group_width = heads_here // kv_here
    query_tiles = query.reshape(cand_count, SEQUENCE_SLOTS, kv_here, group_width, HEAD_WIDTH)
    key_tiles = keys.reshape(cand_count, SEQUENCE_SLOTS, kv_here, HEAD_WIDTH)
    value_tiles = values.reshape(cand_count, SEQUENCE_SLOTS, kv_here, HEAD_WIDTH)
    logits = jnp.einsum(
        "cskgd,ctkd->ckgst", query_tiles, key_tiles, preferred_element_type=jnp.float32
    ) * HEAD_WIDTH ** (-0.5)
    places = jnp.arange(SEQUENCE_SLOTS, dtype=jnp.int32)
    allowed = (places[None, :, None] >= places[None, None, :]) & (
        places[None, None, :] < cand_len[:, None, None]
    )
    allowed = allowed[:, None, None]
    logits = jnp.where(allowed, logits, jnp.float32(-1e30))
    row_max = jnp.max(logits, axis=-1, keepdims=True)
    probs = jnp.where(allowed, jnp.exp(logits - row_max), jnp.float32(0.0))
    totals = jnp.sum(probs, axis=-1, keepdims=True)
    attn_weights = (probs / totals).astype(jnp.bfloat16)
    attn_out = jnp.einsum(
        "ckgst,ctkd->cskgd", attn_weights, value_tiles, preferred_element_type=jnp.float32
    )
    return attn_out.astype(jnp.bfloat16).reshape(row_count, heads_here * HEAD_WIDTH)


def trunk_kernel(*refs):
    acts, w_ref, residual_ref, out_ref = refs[:8], refs[8], refs[9], refs[11]
    total = residual_ref[...].astype(jnp.float32)
    for slot in range(8):
        total = total + jnp.dot(
            acts[slot][...], w_ref[slot, 0], preferred_element_type=jnp.float32
        )
    out_ref[...] = total.astype(jnp.bfloat16)


def trunk_matmul(acts, weights, residual, token):
    rows, depth = acts[0].shape
    half = weights.shape[-1]
    width = 256
    per = half // width
    whole = pl.BlockSpec((rows, depth), lambda j: (0, 0), pipeline_mode=pl.Buffered(1))
    tile = pl.BlockSpec((rows, width), lambda j: (0, j))
    return pl.pallas_call(
        trunk_kernel,
        grid=(CORE * per,),
        in_specs=[whole] * 8
        + [pl.BlockSpec((8, 1, depth, width), lambda j: (0, j // per, 0, j % per)), tile]
        + [pl.BlockSpec(memory_space=pl.ANY)],
        out_specs=tile,
        out_shape=jax.ShapeDtypeStruct(residual.shape, jnp.bfloat16),
        compiler_params=pltpu.CompilerParams(vmem_limit_bytes=40 * 2**20),
        cost_estimate=pl.CostEstimate(
            flops=2 * rows * 8 * depth * CORE * half,
            bytes_accessed=2 * (8 * rows * depth + 8 * depth * CORE * half),
            transcendentals=0,
        ),
        name="trunk_matmul",
    )(*acts, weights, residual, token)


def norm_kernel(place_ref, p0, p1, p2, p3, gain_ref, out_ref):
    pieces = (p0, p1, p2, p3)
    z = place_ref[0]
    group = p0.shape[1] // Z
    width = p0.shape[2]
    per_z = p0.shape[0]
    scales = []
    for r in range(Z):
        square = jnp.zeros((group, 1), jnp.float32)
        for s in range(Z):
            for q in range(per_z):
                rows = pieces[s][q, pl.ds(((r - s) % Z) * group, group), :].astype(jnp.float32)
                square = square + jnp.sum(rows * rows, axis=-1, keepdims=True)
        scales.append(lax.rsqrt(square / (Z * per_z * width) + 1e-05))
    for s in range(Z):
        for q in range(per_z):
            start = pl.multiple_of((lax.rem(z + s, Z) * per_z + q) * width, width)
            gain = gain_ref[:, pl.ds(start, width)]
            for r in range(Z):
                rows = pieces[s][q, pl.ds(((r - s) % Z) * group, group), :].astype(jnp.float32)
                out_ref[pl.ds(r * group, group), pl.ds(start, width)] = (
                    rows * scales[r] * gain
                ).astype(jnp.bfloat16)


def normalize(pieces, gain, z):
    per_z, rows, width = pieces[0].shape
    total = Z * per_z * width
    return pl.pallas_call(
        norm_kernel,
        in_specs=[pl.BlockSpec(memory_space=pltpu.SMEM)]
        + [pl.BlockSpec(memory_space=pltpu.VMEM)] * 5,
        out_specs=pl.BlockSpec(memory_space=pltpu.VMEM),
        out_shape=jax.ShapeDtypeStruct((rows, total), jnp.bfloat16),
        cost_estimate=pl.CostEstimate(
            flops=8 * rows * total, bytes_accessed=4 * rows * total, transcendentals=rows
        ),
        name="normalize",
    )(z[None], *pieces, gain[None, :])


def local(
    query,
    keys,
    values,
    residual,
    out_weight,
    norm_gain,
    cand_len,
    head_w1,
    head_b1,
    head_w2,
    head_b2,
    head_w3,
    head_b3,
):
    z = lax.axis_index("z")
    xl = lax.axis_index("xl")
    core = lax.axis_index("core")
    y = lax.axis_index("y")
    xh = lax.axis_index("xh")
    cand_count = cand_len.shape[0]

    moved = lax.ppermute(out_weight, ALL, weight_moves())
    attn_out = attention(query, keys, values, cand_len)

    last_rows = jnp.arange(cand_count, dtype=jnp.int32) * SEQUENCE_SLOTS + cand_len - 1
    picked = jnp.concatenate(
        [jnp.take(attn_out, last_rows, axis=0), jnp.take(residual, last_rows, axis=0)], axis=1
    )
    near = lax.all_gather(picked, ("xl", "core"), axis=0, tiled=True)
    rows = jnp.concatenate([near] + [from_ahead(near, "z", Z, s) for s in (1, 2, 3)], axis=0)
    acts = {}
    moved, acts[0, 0], token = lax.optimization_barrier((moved, attn_out, rows))
    weights = lax.all_gather(moved, MEMBER, axis=0, tiled=False)
    weights = weights.reshape((Z * XL, CORE) + out_weight.shape)
    acts[1, 0] = from_ahead(acts[0, 0], "y", Y, 1)
    acts[3, 0] = from_ahead(acts[0, 0], "y", Y, 3)
    acts[0, 1] = from_ahead(acts[0, 0], "xh", XH, 1)
    width = out_weight.shape[1]
    own = jnp.dot(rows[:, : attn_out.shape[1]], out_weight, preferred_element_type=jnp.float32)
    res = rows[:, attn_out.shape[1] :]
    res = jnp.where(core == 0, res[:, :width], res[:, width:]).astype(jnp.float32)
    own = jnp.where((y == z) & (xh == xl), own + res, own).astype(jnp.bfloat16)
    pair = jnp.stack([own, from_ahead(own, "xh", XH, 1)])
    parts = [pair] + [from_ahead(pair, "y", Y, s) for s in (1, 2, 3)]
    pooled = sum(jnp.sum(p.astype(jnp.float32), axis=0) for p in parts).astype(jnp.bfloat16)
    pooled, acts[1, 0], acts[3, 0], acts[0, 1], acts[0, 0] = lax.optimization_barrier(
        (pooled, acts[1, 0], acts[3, 0], acts[0, 1], acts[0, 0])
    )
    acts[1, 1] = from_ahead(acts[0, 1], "y", Y, 1)
    acts[3, 1] = from_ahead(acts[0, 1], "y", Y, 3)
    near = lax.all_gather(pooled, ("xl", "core"), axis=0, tiled=False)
    pieces = [near] + [from_ahead(near, "z", Z, s) for s in (1, 2, 3)]
    features = normalize(pieces, norm_gain, z)
    features, acts[1, 1], acts[3, 1], acts[0, 0], acts[0, 1] = lax.optimization_barrier(
        (features, acts[1, 1], acts[3, 1], acts[0, 0], acts[0, 1])
    )
    acts[2, 0] = from_ahead(acts[0, 0], "y", Y, 2)
    acts[2, 1] = from_ahead(acts[0, 1], "y", Y, 2)
    first = jax.nn.silu(
        jnp.dot(features, head_w1[0], preferred_element_type=jnp.float32) + head_b1[0]
    ).astype(jnp.bfloat16)
    terms = jnp.dot(first, head_w2[0], preferred_element_type=jnp.float32).astype(jnp.bfloat16)
    count = terms.shape[0] // Y
    terms = lax.all_to_all(
        terms.reshape(Y, count, terms.shape[1]), "y", split_axis=0, concat_axis=0, tiled=True
    )
    half = jnp.sum(terms.astype(jnp.float32), axis=0).astype(jnp.bfloat16)
    other = from_ahead(half, "xh", XH, 1)
    second = jax.nn.silu(half.astype(jnp.float32) + other.astype(jnp.float32) + head_b2[0])
    mine = jnp.sum(second * head_w3[0].astype(jnp.float32), axis=-1) + head_b3[0]
    scores = lax.all_gather(mine, "y", axis=0, tiled=False)
    scores = jnp.roll(scores, z, axis=0).reshape(1, Y * count)

    ordered = [acts[s, e] for s in range(Y) for e in range(XH)]
    trunk_out = trunk_matmul(ordered, weights, residual, token)
    return (trunk_out, scores)


def solution(mesh):
    fine = Mesh(mesh.devices.reshape(Z, XL, CORE, Y, XH), ALL)
    in_specs = (
        P(MEMBER, TENSOR),
        P(MEMBER, TENSOR),
        P(MEMBER, TENSOR),
        P(MEMBER, TENSOR),
        P(TENSOR, MEMBER),
        P(),
        P(MEMBER),
        P(MEMBER, None, TENSOR),
        P(MEMBER, TENSOR),
        P(MEMBER, TENSOR, None),
        P(MEMBER, None),
        P(MEMBER, None),
        P(MEMBER),
    )
    out_specs = (P(MEMBER, TENSOR), P(MEMBER, None))
    return jax.shard_map(local, mesh=fine, in_specs=in_specs, out_specs=out_specs, check_vma=False)
```

```python
import itertools

import jax
import jax.numpy as jnp
from jax import lax
from jax.experimental import pallas as pl
from jax.experimental.pallas import tpu as pltpu
from jax.sharding import Mesh, PartitionSpec as P

HEAD_WIDTH = 128
SEQUENCE_SLOTS = 128
Z, XL, CORE, Y, XH = 4, 2, 2, 4, 2
MEMBER = ("z", "xl", "core")
TENSOR = ("y", "xh")
ALL = MEMBER + TENSOR


def flat(z, xl, core, y, xh):
    return (((z % Z) * XL + xl % XL) * CORE + core) * Y * XH + (y % Y) * XH + xh % XH


def places():
    return itertools.product(range(Z), range(XL), range(CORE), range(Y), range(XH))


def spread_moves(v):
    return [
        (flat(z, xl, core, y, xh), flat(z - y - v, xl, core, y, xh)) for z, xl, core, y, xh in places()
    ]


def column_moves(v):
    return [
        (flat(z, xl, core, y, xh), flat(z, xh - xl, core, y + z + v, xl))
        for z, xl, core, y, xh in places()
    ]


def from_ahead(x, axis, size, step):
    return lax.ppermute(x, axis, [(i, (i - step) % size) for i in range(size)])


def attention(query, keys, values, cand_len):
    row_count = query.shape[0]
    cand_count = row_count // SEQUENCE_SLOTS
    heads_here = query.shape[1] // HEAD_WIDTH
    kv_here = keys.shape[1] // HEAD_WIDTH
    group_width = heads_here // kv_here
    query_tiles = query.reshape(cand_count, SEQUENCE_SLOTS, kv_here, group_width, HEAD_WIDTH)
    key_tiles = keys.reshape(cand_count, SEQUENCE_SLOTS, kv_here, HEAD_WIDTH)
    value_tiles = values.reshape(cand_count, SEQUENCE_SLOTS, kv_here, HEAD_WIDTH)
    logits = jnp.einsum(
        "cskgd,ctkd->ckgst", query_tiles, key_tiles, preferred_element_type=jnp.float32
    ) * HEAD_WIDTH ** (-0.5)
    places = jnp.arange(SEQUENCE_SLOTS, dtype=jnp.int32)
    allowed = (places[None, :, None] >= places[None, None, :]) & (
        places[None, None, :] < cand_len[:, None, None]
    )
    allowed = allowed[:, None, None]
    logits = jnp.where(allowed, logits, jnp.float32(-1e30))
    row_max = jnp.max(logits, axis=-1, keepdims=True)
    probs = jnp.where(allowed, jnp.exp(logits - row_max), jnp.float32(0.0))
    totals = jnp.sum(probs, axis=-1, keepdims=True)
    attn_weights = (probs / totals).astype(jnp.bfloat16)
    attn_out = jnp.einsum(
        "ckgst,ctkd->cskgd", attn_weights, value_tiles, preferred_element_type=jnp.float32
    )
    return attn_out.astype(jnp.bfloat16).reshape(row_count, heads_here * HEAD_WIDTH)


def trunk_kernel(*refs):
    acts, w_ref, residual_ref, out_ref = refs[:8], refs[8], refs[9], refs[-1]
    total = residual_ref[...].astype(jnp.float32)
    for a in range(Y):
        for e in range(XH):
            block = jnp.concatenate(
                [w_ref[((-a - v) % Z) * XL + e, 0, v] for v in range(Z)], axis=0
            )
            total = total + jnp.dot(
                acts[a * XH + e][...], block, preferred_element_type=jnp.float32
            )
    out_ref[...] = total.astype(jnp.bfloat16)


def trunk_matmul(acts, weights, residual, tokens):
    rows, depth = acts[0].shape
    half = weights.shape[-1]
    width = 256
    per = half // width
    whole = pl.BlockSpec((rows, depth), lambda j: (0, 0), pipeline_mode=pl.Buffered(1))
    tile = pl.BlockSpec((rows, width), lambda j: (0, j))
    return pl.pallas_call(
        trunk_kernel,
        grid=(CORE * per,),
        in_specs=[whole] * 8
        + [
            pl.BlockSpec(
                (Z * XL, 1, Z, depth // Z, width), lambda j: (0, j // per, 0, 0, j % per)
            ),
            tile,
        ]
        + [pl.BlockSpec(memory_space=pl.ANY)] * len(tokens),
        out_specs=tile,
        out_shape=jax.ShapeDtypeStruct(residual.shape, jnp.bfloat16),
        compiler_params=pltpu.CompilerParams(vmem_limit_bytes=40 * 2**20),
        cost_estimate=pl.CostEstimate(
            flops=2 * rows * 8 * depth * CORE * half,
            bytes_accessed=2 * (8 * rows * depth + 8 * depth * CORE * half),
            transcendentals=0,
        ),
        name="trunk_matmul",
    )(*acts, weights, residual, *tokens)


def norm_kernel(place_ref, p0, p1, p2, p3, gain_ref, out_ref):
    pieces = (p0, p1, p2, p3)
    z = place_ref[0]
    group = p0.shape[1] // Z
    width = p0.shape[2]
    per_z = p0.shape[0]
    scales = []
    for r in range(Z):
        square = jnp.zeros((group, 1), jnp.float32)
        for s in range(Z):
            for q in range(per_z):
                rows = pieces[s][q, pl.ds(((r - s) % Z) * group, group), :].astype(jnp.float32)
                square = square + jnp.sum(rows * rows, axis=-1, keepdims=True)
        scales.append(lax.rsqrt(square / (Z * per_z * width) + 1e-05))
    for s in range(Z):
        for q in range(per_z):
            start = pl.multiple_of((lax.rem(z + s, Z) * per_z + q) * width, width)
            gain = gain_ref[:, pl.ds(start, width)]
            for r in range(Z):
                rows = pieces[s][q, pl.ds(((r - s) % Z) * group, group), :].astype(jnp.float32)
                out_ref[pl.ds(r * group, group), pl.ds(start, width)] = (
                    rows * scales[r] * gain
                ).astype(jnp.bfloat16)


def normalize(pieces, gain, z):
    per_z, rows, width = pieces[0].shape
    total = Z * per_z * width
    return pl.pallas_call(
        norm_kernel,
        in_specs=[pl.BlockSpec(memory_space=pltpu.SMEM)]
        + [pl.BlockSpec(memory_space=pltpu.VMEM)] * 5,
        out_specs=pl.BlockSpec(memory_space=pltpu.VMEM),
        out_shape=jax.ShapeDtypeStruct((rows, total), jnp.bfloat16),
        cost_estimate=pl.CostEstimate(
            flops=8 * rows * total, bytes_accessed=4 * rows * total, transcendentals=rows
        ),
        name="normalize",
    )(z[None], *pieces, gain[None, :])


def local(
    query,
    keys,
    values,
    residual,
    out_weight,
    norm_gain,
    cand_len,
    head_w1,
    head_b1,
    head_w2,
    head_b2,
    head_w3,
    head_b3,
):
    z = lax.axis_index("z")
    xl = lax.axis_index("xl")
    core = lax.axis_index("core")
    y = lax.axis_index("y")
    xh = lax.axis_index("xh")
    cand_count = cand_len.shape[0]

    quarter = out_weight.shape[0] // Z
    moved = [
        lax.ppermute(out_weight[v * quarter : (v + 1) * quarter], ALL, spread_moves(v))
        for v in range(Z)
    ]
    acts = {}
    acts[0, 0] = attention(query, keys, values, cand_len)

    last_rows = jnp.arange(cand_count, dtype=jnp.int32) * SEQUENCE_SLOTS + cand_len - 1
    picked = jnp.concatenate(
        [jnp.take(acts[0, 0], last_rows, axis=0), jnp.take(residual, last_rows, axis=0)], axis=1
    )
    depth = acts[0, 0].shape[1]
    near = lax.all_gather(picked, ("xl", "core"), axis=0, tiled=True)
    *moved, near = lax.optimization_barrier((*moved, near))
    moved = [lax.ppermute(m, ALL, column_moves(v)) for v, m in enumerate(moved)]
    rows = jnp.concatenate([near] + [from_ahead(near, "z", Z, s) for s in (1, 2, 3)], axis=0)
    width = out_weight.shape[1]
    own = jnp.dot(rows[:, :depth], out_weight, preferred_element_type=jnp.float32)
    res = rows[:, depth:]
    res = jnp.where(core == 0, res[:, :width], res[:, width:]).astype(jnp.float32)
    own = jnp.where((y == z) & (xh == xl), own + res, own).astype(jnp.bfloat16)
    pair = jnp.stack([own, from_ahead(own, "xh", XH, 1)])
    *moved, acts[0, 0], pair = lax.optimization_barrier((*moved, acts[0, 0], pair))
    weights = lax.all_gather(jnp.stack(moved), MEMBER, axis=0, tiled=False)
    weights = weights.reshape((Z * XL, CORE, Z, quarter, width))
    acts[0, 1] = from_ahead(acts[0, 0], "xh", XH, 1)
    parts = [pair] + [from_ahead(pair, "y", Y, s) for s in (1, 2, 3)]
    pooled = sum(jnp.sum(p.astype(jnp.float32), axis=0) for p in parts).astype(jnp.bfloat16)
    acts[0, 0], token = lax.optimization_barrier((acts[0, 0], pooled))
    acts[1, 0] = from_ahead(acts[0, 0], "y", Y, 1)
    acts[3, 0] = from_ahead(acts[0, 0], "y", Y, 3)
    near = lax.all_gather(pooled, ("xl", "core"), axis=0, tiled=False)
    acts[0, 0], acts[0, 1], near = lax.optimization_barrier((acts[0, 0], acts[0, 1], near))
    acts[1, 1] = from_ahead(acts[0, 1], "y", Y, 1)
    acts[3, 1] = from_ahead(acts[0, 1], "y", Y, 3)
    acts[2, 0] = from_ahead(acts[0, 0], "y", Y, 2)
    pieces = [near] + [from_ahead(near, "z", Z, s) for s in (1, 2, 3)]
    features = normalize(pieces, norm_gain, z)
    first = jax.nn.silu(
        jnp.dot(features, head_w1[0], preferred_element_type=jnp.float32) + head_b1[0]
    ).astype(jnp.bfloat16)
    terms = jnp.dot(first, head_w2[0], preferred_element_type=jnp.float32).astype(jnp.bfloat16)
    count = terms.shape[0] // Y
    terms = lax.all_to_all(
        terms.reshape(Y, count, terms.shape[1]), "y", split_axis=0, concat_axis=0, tiled=True
    )
    terms, acts[0, 1], acts[1, 0], acts[3, 0], acts[1, 1], acts[3, 1] = lax.optimization_barrier(
        (terms, acts[0, 1], acts[1, 0], acts[3, 0], acts[1, 1], acts[3, 1])
    )
    acts[2, 1] = from_ahead(acts[0, 1], "y", Y, 2)
    half = jnp.sum(terms.astype(jnp.float32), axis=0).astype(jnp.bfloat16)
    other = from_ahead(half, "xh", XH, 1)
    second = jax.nn.silu(half.astype(jnp.float32) + other.astype(jnp.float32) + head_b2[0])
    mine = jnp.sum(second * head_w3[0].astype(jnp.float32), axis=-1) + head_b3[0]
    scores = lax.all_gather(mine, "y", axis=0, tiled=False)
    scores = jnp.roll(scores, z, axis=0).reshape(1, Y * count)

    ordered = [acts[a, e] for a in range(Y) for e in range(XH)]
    trunk_out = trunk_matmul(ordered, weights, residual, (token,))
    return (trunk_out, scores)


def solution(mesh):
    fine = Mesh(mesh.devices.reshape(Z, XL, CORE, Y, XH), ALL)
    in_specs = (
        P(MEMBER, TENSOR),
        P(MEMBER, TENSOR),
        P(MEMBER, TENSOR),
        P(MEMBER, TENSOR),
        P(TENSOR, MEMBER),
        P(),
        P(MEMBER),
        P(MEMBER, None, TENSOR),
        P(MEMBER, TENSOR),
        P(MEMBER, TENSOR, None),
        P(MEMBER, None),
        P(MEMBER, None),
        P(MEMBER),
    )
    out_specs = (P(MEMBER, TENSOR), P(MEMBER, None))
    return jax.shard_map(local, mesh=fine, in_specs=in_specs, out_specs=out_specs, check_vma=False)
```

```python
import itertools

import jax
import jax.numpy as jnp
from jax import lax
from jax.experimental import pallas as pl
from jax.experimental.pallas import tpu as pltpu
from jax.sharding import Mesh, PartitionSpec as P

HEAD_WIDTH = 128
SEQUENCE_SLOTS = 128
Z, XL, CORE, Y, XH = 4, 2, 2, 4, 2
MEMBER = ("z", "xl", "core")
TENSOR = ("y", "xh")
ALL = MEMBER + TENSOR


def flat(z, xl, core, y, xh):
    return (((z % Z) * XL + xl % XL) * CORE + core) * Y * XH + (y % Y) * XH + xh % XH


def places():
    return itertools.product(range(Z), range(XL), range(CORE), range(Y), range(XH))


def spread_moves(v):
    return [
        (flat(z, xl, core, y, xh), flat(z - y - 2 * v, xl, core, y, xh))
        for z, xl, core, y, xh in places()
    ]


def column_moves(v):
    return [
        (flat(z, xl, core, y, xh), flat(z, xh - xl, core, y + z + 2 * v, xl))
        for z, xl, core, y, xh in places()
    ]


def from_ahead(x, axis, size, step):
    return lax.ppermute(x, axis, [(i, (i - step) % size) for i in range(size)])


def attention(query, keys, values, cand_len):
    row_count = query.shape[0]
    cand_count = row_count // SEQUENCE_SLOTS
    heads_here = query.shape[1] // HEAD_WIDTH
    kv_here = keys.shape[1] // HEAD_WIDTH
    group_width = heads_here // kv_here
    query_tiles = query.reshape(cand_count, SEQUENCE_SLOTS, kv_here, group_width, HEAD_WIDTH)
    key_tiles = keys.reshape(cand_count, SEQUENCE_SLOTS, kv_here, HEAD_WIDTH)
    value_tiles = values.reshape(cand_count, SEQUENCE_SLOTS, kv_here, HEAD_WIDTH)
    logits = jnp.einsum(
        "cskgd,ctkd->ckgst", query_tiles, key_tiles, preferred_element_type=jnp.float32
    ) * HEAD_WIDTH ** (-0.5)
    places = jnp.arange(SEQUENCE_SLOTS, dtype=jnp.int32)
    allowed = (places[None, :, None] >= places[None, None, :]) & (
        places[None, None, :] < cand_len[:, None, None]
    )
    allowed = allowed[:, None, None]
    logits = jnp.where(allowed, logits, jnp.float32(-1e30))
    row_max = jnp.max(logits, axis=-1, keepdims=True)
    probs = jnp.where(allowed, jnp.exp(logits - row_max), jnp.float32(0.0))
    totals = jnp.sum(probs, axis=-1, keepdims=True)
    attn_weights = (probs / totals).astype(jnp.bfloat16)
    attn_out = jnp.einsum(
        "ckgst,ctkd->cskgd", attn_weights, value_tiles, preferred_element_type=jnp.float32
    )
    return attn_out.astype(jnp.bfloat16).reshape(row_count, heads_here * HEAD_WIDTH)


def trunk_kernel(place_ref, acts_ref, *refs):
    residual_ref, out_ref = refs[20], refs[21]
    j = pl.program_id(0)

    def tile(blocks):
        total = residual_ref[...].astype(jnp.float32)
        for e in range(XL):
            for s in range(Z):
                for v in range(2):
                    if s == 2:
                        block = blocks[5 * e + 3 + v][...]
                    else:
                        block = blocks[5 * e + min(s, 2)][v]
                    depth = block.shape[0]
                    group = lax.rem(place_ref[0] + 2 * Y - s - 2 * v, Y) * XH + lax.rem(
                        place_ref[1] + e, XH
                    )
                    total = total + jnp.dot(
                        acts_ref[group, :, v * depth : (v + 1) * depth],
                        block,
                        preferred_element_type=jnp.float32,
                    )
        out_ref[...] = total.astype(jnp.bfloat16)

    @pl.when(j < 2)
    def _():
        tile(refs[:10])

    @pl.when(j >= 2)
    def _():
        tile(refs[10:20])


def trunk_matmul(place, acts, own, other, residual):
    groups, rows, depth = acts.shape
    half = residual.shape[1] // CORE
    width = half // 2

    def spec(w, index):
        shape = w.shape[:-1] + (width,)
        return pl.BlockSpec(shape, lambda j, p: (0,) * (len(shape) - 1) + (index(j),))

    tile = pl.BlockSpec(
        (rows, width), lambda j, p: (0, jnp.where(j < 2, p[2], 1 - p[2]) * 2 + lax.rem(j, 2))
    )
    return pl.pallas_call(
        trunk_kernel,
        grid_spec=pltpu.PrefetchScalarGridSpec(
            num_scalar_prefetch=1,
            grid=(4,),
            in_specs=[
                pl.BlockSpec(acts.shape, lambda j, p: (0, 0, 0), pipeline_mode=pl.Buffered(1))
            ]
            + [spec(w, lambda j: jnp.minimum(j, 1)) for w in own]
            + [spec(w, lambda j: jnp.maximum(j - 2, 0)) for w in other]
            + [tile],
            out_specs=tile,
        ),
        out_shape=jax.ShapeDtypeStruct(residual.shape, jnp.bfloat16),
        compiler_params=pltpu.CompilerParams(vmem_limit_bytes=44 * 2**20),
        cost_estimate=pl.CostEstimate(
            flops=2 * rows * groups * depth * CORE * half,
            bytes_accessed=2 * (groups * rows * depth + groups * depth * CORE * half),
            transcendentals=0,
        ),
        name="trunk_matmul",
    )(place, acts, *own, *other, residual)


def norm_kernel(place_ref, p0, p1, p2, p3, gain_ref, out_ref):
    pieces = (p0, p1, p2, p3)
    z = place_ref[0]
    group = p0.shape[1] // Z
    width = p0.shape[2]
    per_z = p0.shape[0]
    scales = []
    for r in range(Z):
        square = jnp.zeros((group, 1), jnp.float32)
        for s in range(Z):
            for q in range(per_z):
                rows = pieces[s][q, pl.ds(((r - s) % Z) * group, group), :].astype(jnp.float32)
                square = square + jnp.sum(rows * rows, axis=-1, keepdims=True)
        scales.append(lax.rsqrt(square / (Z * per_z * width) + 1e-05))
    for s in range(Z):
        for q in range(per_z):
            start = pl.multiple_of((lax.rem(z + s, Z) * per_z + q) * width, width)
            gain = gain_ref[:, pl.ds(start, width)]
            for r in range(Z):
                rows = pieces[s][q, pl.ds(((r - s) % Z) * group, group), :].astype(jnp.float32)
                out_ref[pl.ds(r * group, group), pl.ds(start, width)] = (
                    rows * scales[r] * gain
                ).astype(jnp.bfloat16)


def normalize(pieces, gain, z):
    per_z, rows, width = pieces[0].shape
    total = Z * per_z * width
    return pl.pallas_call(
        norm_kernel,
        in_specs=[pl.BlockSpec(memory_space=pltpu.SMEM)]
        + [pl.BlockSpec(memory_space=pltpu.VMEM)] * 5,
        out_specs=pl.BlockSpec(memory_space=pltpu.VMEM),
        out_shape=jax.ShapeDtypeStruct((rows, total), jnp.bfloat16),
        cost_estimate=pl.CostEstimate(
            flops=8 * rows * total, bytes_accessed=4 * rows * total, transcendentals=rows
        ),
        name="normalize",
    )(z[None], *pieces, gain[None, :])


def local(
    query,
    keys,
    values,
    residual,
    out_weight,
    norm_gain,
    cand_len,
    head_w1,
    head_b1,
    head_w2,
    head_b2,
    head_w3,
    head_b3,
):
    z = lax.axis_index("z")
    xl = lax.axis_index("xl")
    core = lax.axis_index("core")
    y = lax.axis_index("y")
    xh = lax.axis_index("xh")
    cand_count = cand_len.shape[0]

    lock = lax.optimization_barrier
    rows_half = out_weight.shape[0] // 2
    moved = [
        lax.ppermute(out_weight[v * rows_half : (v + 1) * rows_half], ALL, spread_moves(v))
        for v in range(2)
    ]
    attn_out = attention(query, keys, values, cand_len)
    acts = lax.all_gather(attn_out, TENSOR, axis=0, tiled=False)

    last_rows = jnp.arange(cand_count, dtype=jnp.int32) * SEQUENCE_SLOTS + cand_len - 1
    picked = jnp.concatenate(
        [jnp.take(attn_out, last_rows, axis=0), jnp.take(residual, last_rows, axis=0)], axis=1
    )
    depth = attn_out.shape[1]
    width = out_weight.shape[1]
    near = lax.all_gather(picked, ("xl", "core"), axis=0, tiled=True)
    near, *moved = lock((near, *moved))
    moved = [lax.ppermute(m, ALL, column_moves(v)) for v, m in enumerate(moved)]
    rows = jnp.concatenate([near] + [from_ahead(near, "z", Z, s) for s in (1, 2, 3)], axis=0)
    own = jnp.dot(rows[:, :depth], out_weight, preferred_element_type=jnp.float32)
    res = rows[:, depth:]
    res = jnp.where(core == 0, res[:, :width], res[:, width:]).astype(jnp.float32)
    own = jnp.where((y == z) & (xh == xl), own + res, own).astype(jnp.bfloat16)
    pair = jnp.stack([own, from_ahead(own, "xh", XH, 1)])
    pair, *moved = lock((pair, *moved))
    w, swapped = {}, {}
    w[0, 0] = jnp.stack(moved)
    w[1, 0] = from_ahead(w[0, 0], "z", Z, 1)
    w[3, 0] = from_ahead(w[0, 0], "z", Z, 3)
    swapped[0, 0] = from_ahead(w[0, 0], "core", CORE, 1)
    parts = [pair] + [from_ahead(pair, "y", Y, s) for s in (1, 2, 3)]
    pooled = sum(jnp.sum(p.astype(jnp.float32), axis=0) for p in parts).astype(jnp.bfloat16)
    near = lax.all_gather(pooled, ("xl", "core"), axis=0, tiled=False)
    near, w[0, 0], w[1, 0], w[3, 0], swapped[0, 0] = lock(
        (near, w[0, 0], w[1, 0], w[3, 0], swapped[0, 0])
    )
    w[0, 1] = from_ahead(w[0, 0], "xl", XL, 1)
    pieces = [near] + [from_ahead(near, "z", Z, s) for s in (1, 2, 3)]
    features = normalize(pieces, norm_gain, z)
    w[2, 0, 0] = from_ahead(w[1, 0][0], "z", Z, 1)
    w[2, 0, 1] = from_ahead(w[3, 0][1], "z", Z, 3)
    swapped[1, 0] = from_ahead(w[1, 0], "core", CORE, 1)
    swapped[3, 0] = from_ahead(w[3, 0], "core", CORE, 1)
    first = jax.nn.silu(
        jnp.dot(features, head_w1[0], preferred_element_type=jnp.float32) + head_b1[0]
    ).astype(jnp.bfloat16)
    terms = jnp.dot(first, head_w2[0], preferred_element_type=jnp.float32).astype(jnp.bfloat16)
    names = [(0, 1), (2, 0, 0), (2, 0, 1)]
    terms, swapped[1, 0], swapped[3, 0], *late = lock(
        (terms, swapped[1, 0], swapped[3, 0], *[w[n] for n in names])
    )
    w.update(zip(names, late))
    w[1, 1] = from_ahead(w[0, 1], "z", Z, 1)
    w[3, 1] = from_ahead(w[0, 1], "z", Z, 3)
    for n in names:
        swapped[n] = from_ahead(w[n], "core", CORE, 1)
    count = terms.shape[0] // Y
    terms = lax.all_to_all(
        terms.reshape(Y, count, terms.shape[1]), "y", split_axis=0, concat_axis=0, tiled=True
    )
    half = jnp.sum(terms.astype(jnp.float32), axis=0).astype(jnp.bfloat16)
    other = from_ahead(half, "xh", XH, 1)
    other, w[1, 1], w[3, 1], *late = lock((other, w[1, 1], w[3, 1], *[swapped[n] for n in names]))
    swapped.update(zip(names, late))
    w[2, 1, 0] = from_ahead(w[1, 1][0], "z", Z, 1)
    w[2, 1, 1] = from_ahead(w[3, 1][1], "z", Z, 3)
    for n in ((1, 1), (3, 1), (2, 1, 0), (2, 1, 1)):
        swapped[n] = from_ahead(w[n], "core", CORE, 1)
    second = jax.nn.silu(half.astype(jnp.float32) + other.astype(jnp.float32) + head_b2[0])
    mine = jnp.sum(second * head_w3[0].astype(jnp.float32), axis=-1) + head_b3[0]
    scores = lax.all_gather(mine, "y", axis=0, tiled=False)
    scores = jnp.roll(scores, z, axis=0).reshape(1, Y * count)

    order = [n for e in range(XL) for n in ((0, e), (1, e), (3, e), (2, e, 0), (2, e, 1))]
    place = jnp.stack([lax.rem(y - z + Y, Y), lax.rem(xh + xl, XH), core])
    trunk_out = trunk_matmul(
        place, acts, [w[n] for n in order], [swapped[n] for n in order], residual
    )
    return (trunk_out, scores)


def solution(mesh):
    fine = Mesh(mesh.devices.reshape(Z, XL, CORE, Y, XH), ALL)
    in_specs = (
        P(MEMBER, TENSOR),
        P(MEMBER, TENSOR),
        P(MEMBER, TENSOR),
        P(MEMBER, TENSOR),
        P(TENSOR, MEMBER),
        P(),
        P(MEMBER),
        P(MEMBER, None, TENSOR),
        P(MEMBER, TENSOR),
        P(MEMBER, TENSOR, None),
        P(MEMBER, None),
        P(MEMBER, None),
        P(MEMBER),
    )
    out_specs = (P(MEMBER, TENSOR), P(MEMBER, None))
    return jax.shard_map(local, mesh=fine, in_specs=in_specs, out_specs=out_specs, check_vma=False)
```

```python
import functools
import itertools

import jax
import jax.numpy as jnp
from jax import lax
from jax.experimental import pallas as pl
from jax.experimental.pallas import tpu as pltpu
from jax.sharding import Mesh, PartitionSpec as P

HEAD_WIDTH = 128
SEQUENCE_SLOTS = 128
Z, XL, CORE, Y, XH = 4, 2, 2, 4, 2
MEMBER = ("z", "xl", "core")
TENSOR = ("y", "xh")
ALL = MEMBER + TENSOR


def flat(z, xl, core, y, xh):
    return (((z % Z) * XL + xl % XL) * CORE + core) * Y * XH + (y % Y) * XH + xh % XH


def places():
    return itertools.product(range(Z), range(XL), range(CORE), range(Y), range(XH))


def spread_moves(v):
    return [
        (flat(z, xl, core, y, xh), flat(z - y - 2 * v, xl, core, y, xh))
        for z, xl, core, y, xh in places()
    ]


def column_moves(v):
    return [
        (flat(z, xl, core, y, xh), flat(z, xh - xl, core, y + z + 2 * v, xl))
        for z, xl, core, y, xh in places()
    ]


def from_ahead(x, axis, size, step):
    return lax.ppermute(x, axis, [(i, (i - step) % size) for i in range(size)])


def attention(query, keys, values, cand_len):
    row_count = query.shape[0]
    cand_count = row_count // SEQUENCE_SLOTS
    heads_here = query.shape[1] // HEAD_WIDTH
    kv_here = keys.shape[1] // HEAD_WIDTH
    group_width = heads_here // kv_here
    query_tiles = query.reshape(cand_count, SEQUENCE_SLOTS, kv_here, group_width, HEAD_WIDTH)
    key_tiles = keys.reshape(cand_count, SEQUENCE_SLOTS, kv_here, HEAD_WIDTH)
    value_tiles = values.reshape(cand_count, SEQUENCE_SLOTS, kv_here, HEAD_WIDTH)
    logits = jnp.einsum(
        "cskgd,ctkd->ckgst", query_tiles, key_tiles, preferred_element_type=jnp.float32
    ) * HEAD_WIDTH ** (-0.5)
    places = jnp.arange(SEQUENCE_SLOTS, dtype=jnp.int32)
    allowed = (places[None, :, None] >= places[None, None, :]) & (
        places[None, None, :] < cand_len[:, None, None]
    )
    allowed = allowed[:, None, None]
    logits = jnp.where(allowed, logits, jnp.float32(-1e30))
    row_max = jnp.max(logits, axis=-1, keepdims=True)
    probs = jnp.where(allowed, jnp.exp(logits - row_max), jnp.float32(0.0))
    totals = jnp.sum(probs, axis=-1, keepdims=True)
    attn_weights = (probs / totals).astype(jnp.bfloat16)
    attn_out = jnp.einsum(
        "ckgst,ctkd->cskgd", attn_weights, value_tiles, preferred_element_type=jnp.float32
    )
    return attn_out.astype(jnp.bfloat16).reshape(row_count, heads_here * HEAD_WIDTH)


def trunk_kernel(count, place_ref, *refs):
    acts, own, other = refs[:count], refs[count : 2 * count], refs[2 * count : 3 * count]
    base_ref, out_ref = refs[3 * count], refs[3 * count + 1]

    def tile(blocks):
        total = base_ref[...].astype(jnp.float32)
        for a, b in zip(acts, blocks):
            total = total + jnp.dot(a[...], b[...], preferred_element_type=jnp.float32)
        out_ref[...] = total.astype(out_ref.dtype)

    @pl.when(pl.program_id(0) < 2)
    def _():
        tile(own)

    @pl.when(pl.program_id(0) >= 2)
    def _():
        tile(other)


def trunk_part(place, acts, terms, base, dtype):
    rows = acts.shape[1]
    half = base.shape[1] // CORE
    width = half // 2
    depth = acts.shape[2] // 2

    def act_spec(s, e, v):
        def index(j, p):
            group = lax.rem(p[0] + 2 * Y - s - 2 * v, Y) * XH + lax.rem(p[1] + e, XH)
            return (group, 0, v)

        return pl.BlockSpec((None, rows, depth), index, pipeline_mode=pl.Buffered(1))

    def weight_spec(w, v, index):
        if w.ndim == 3:
            return pl.BlockSpec((None, depth, width), lambda j, p: (v, 0, index(j)))
        return pl.BlockSpec((depth, width), lambda j, p: (0, index(j)))

    tile = pl.BlockSpec(
        (rows, width), lambda j, p: (0, jnp.where(j < 2, p[2], 1 - p[2]) * 2 + lax.rem(j, 2))
    )
    count = len(terms)
    return pl.pallas_call(
        functools.partial(trunk_kernel, count),
        grid_spec=pltpu.PrefetchScalarGridSpec(
            num_scalar_prefetch=1,
            grid=(4,),
            in_specs=[act_spec(s, e, v) for s, e, v, _, _ in terms]
            + [weight_spec(w, v, lambda j: jnp.minimum(j, 1)) for _, _, v, w, _ in terms]
            + [weight_spec(w, v, lambda j: jnp.maximum(j - 2, 0)) for _, _, v, _, w in terms]
            + [tile],
            out_specs=tile,
        ),
        out_shape=jax.ShapeDtypeStruct(base.shape, dtype),
        compiler_params=pltpu.CompilerParams(vmem_limit_bytes=40 * 2**20),
        cost_estimate=pl.CostEstimate(
            flops=2 * rows * count * depth * CORE * half,
            bytes_accessed=2 * count * depth * (rows + CORE * half) + 8 * rows * CORE * half,
            transcendentals=0,
        ),
        name="trunk_part",
    )(place, *[pltpu.with_memory_space_constraint(acts, pltpu.HBM)] * count, *[t[3] for t in terms], *[t[4] for t in terms], base)


def norm_kernel(place_ref, p0, p1, p2, p3, gain_ref, out_ref):
    pieces = (p0, p1, p2, p3)
    z = place_ref[0]
    group = p0.shape[1] // Z
    width = p0.shape[2]
    per_z = p0.shape[0]
    scales = []
    for r in range(Z):
        square = jnp.zeros((group, 1), jnp.float32)
        for s in range(Z):
            for q in range(per_z):
                rows = pieces[s][q, pl.ds(((r - s) % Z) * group, group), :].astype(jnp.float32)
                square = square + jnp.sum(rows * rows, axis=-1, keepdims=True)
        scales.append(lax.rsqrt(square / (Z * per_z * width) + 1e-05))
    for s in range(Z):
        for q in range(per_z):
            start = pl.multiple_of((lax.rem(z + s, Z) * per_z + q) * width, width)
            gain = gain_ref[:, pl.ds(start, width)]
            for r in range(Z):
                rows = pieces[s][q, pl.ds(((r - s) % Z) * group, group), :].astype(jnp.float32)
                out_ref[pl.ds(r * group, group), pl.ds(start, width)] = (
                    rows * scales[r] * gain
                ).astype(jnp.bfloat16)


def normalize(pieces, gain, z):
    per_z, rows, width = pieces[0].shape
    total = Z * per_z * width
    return pl.pallas_call(
        norm_kernel,
        in_specs=[pl.BlockSpec(memory_space=pltpu.SMEM)]
        + [pl.BlockSpec(memory_space=pltpu.VMEM)] * 5,
        out_specs=pl.BlockSpec(memory_space=pltpu.VMEM),
        out_shape=jax.ShapeDtypeStruct((rows, total), jnp.bfloat16),
        cost_estimate=pl.CostEstimate(
            flops=8 * rows * total, bytes_accessed=4 * rows * total, transcendentals=rows
        ),
        name="normalize",
    )(z[None], *pieces, gain[None, :])


def local(
    query,
    keys,
    values,
    residual,
    out_weight,
    norm_gain,
    cand_len,
    head_w1,
    head_b1,
    head_w2,
    head_b2,
    head_w3,
    head_b3,
):
    z = lax.axis_index("z")
    xl = lax.axis_index("xl")
    core = lax.axis_index("core")
    y = lax.axis_index("y")
    xh = lax.axis_index("xh")
    cand_count = cand_len.shape[0]

    lock = lax.optimization_barrier
    place = jnp.stack([lax.rem(y - z + Y, Y), lax.rem(xh + xl, XH), core])
    rows_half = out_weight.shape[0] // 2
    moved = [
        lax.ppermute(out_weight[v * rows_half : (v + 1) * rows_half], ALL, spread_moves(v))
        for v in range(2)
    ]
    attn_out = attention(query, keys, values, cand_len)
    acts = lax.all_gather(attn_out, TENSOR, axis=0, tiled=False)

    attn_out, *moved = lock((attn_out, *moved))
    moved = [lax.ppermute(m, ALL, column_moves(v)) for v, m in enumerate(moved)]
    last_rows = jnp.arange(cand_count, dtype=jnp.int32) * SEQUENCE_SLOTS + cand_len - 1
    picked = jnp.concatenate(
        [jnp.take(attn_out, last_rows, axis=0), jnp.take(residual, last_rows, axis=0)], axis=1
    )
    depth = attn_out.shape[1]
    width = out_weight.shape[1]
    near = lax.all_gather(picked, ("xl", "core"), axis=0, tiled=True)
    rows = jnp.concatenate([near] + [from_ahead(near, "z", Z, s) for s in (1, 2, 3)], axis=0)
    rows, *moved = lock((rows, *moved))
    w, swapped = {}, {}
    w[0, 0] = jnp.stack(moved)
    w[1, 0] = from_ahead(w[0, 0], "z", Z, 1)
    w[3, 0] = from_ahead(w[0, 0], "z", Z, 3)
    own = jnp.dot(rows[:, :depth], out_weight, preferred_element_type=jnp.float32)
    res = rows[:, depth:]
    res = jnp.where(core == 0, res[:, :width], res[:, width:]).astype(jnp.float32)
    own = jnp.where((y == z) & (xh == xl), own + res, own).astype(jnp.bfloat16)
    pair = jnp.stack([own, from_ahead(own, "xh", XH, 1)])
    parts = [pair] + [from_ahead(pair, "y", Y, s) for s in (1, 2, 3)]
    pooled = sum(jnp.sum(p.astype(jnp.float32), axis=0) for p in parts).astype(jnp.bfloat16)
    near = lax.all_gather(pooled, ("xl", "core"), axis=0, tiled=False)
    near, w[1, 0], w[3, 0], w[0, 0] = lock((near, w[1, 0], w[3, 0], w[0, 0]))
    pieces = [near] + [from_ahead(near, "z", Z, s) for s in (1, 2, 3)]
    w[0, 1] = from_ahead(w[0, 0], "xl", XL, 1)
    swapped[0, 0] = from_ahead(w[0, 0], "core", CORE, 1)
    w[2, 0, 0] = from_ahead(w[1, 0][0], "z", Z, 1)
    w[2, 0, 1] = from_ahead(w[3, 0][1], "z", Z, 3)
    features = normalize(pieces, norm_gain, z)
    features, w[0, 1], swapped[0, 0] = lock((features, w[0, 1], swapped[0, 0]))
    w[1, 1] = from_ahead(w[0, 1], "z", Z, 1)
    w[3, 1] = from_ahead(w[0, 1], "z", Z, 3)
    for n in ((1, 0), (3, 0)):
        swapped[n] = from_ahead(w[n], "core", CORE, 1)
    first = jax.nn.silu(
        jnp.dot(features, head_w1[0], preferred_element_type=jnp.float32) + head_b1[0]
    ).astype(jnp.bfloat16)
    terms = jnp.dot(first, head_w2[0], preferred_element_type=jnp.float32).astype(jnp.bfloat16)
    terms, w[2, 0, 0], w[2, 0, 1], swapped[1, 0], swapped[3, 0] = lock(
        (terms, w[2, 0, 0], w[2, 0, 1], swapped[1, 0], swapped[3, 0])
    )
    for n in ((2, 0, 0), (2, 0, 1), (0, 1)):
        swapped[n] = from_ahead(w[n], "core", CORE, 1)
    count = terms.shape[0] // Y
    terms = lax.all_to_all(
        terms.reshape(Y, count, terms.shape[1]), "y", split_axis=0, concat_axis=0, tiled=True
    )

    def products(*names):
        for n in names:
            for v in (0, 1) if len(n) == 2 else n[2:]:
                yield (n[0], n[1], v, w[n], swapped[n])

    first_names = ((0, 0), (1, 0), (3, 0), (2, 0, 0), (2, 0, 1), (0, 1))
    trunk = trunk_part(place, acts, list(products(*first_names)), residual, jnp.float32)
    terms, w[1, 1], w[3, 1], trunk = lock((terms, w[1, 1], w[3, 1], trunk))
    w[2, 1, 0] = from_ahead(w[1, 1][0], "z", Z, 1)
    w[2, 1, 1] = from_ahead(w[3, 1][1], "z", Z, 3)
    for n in ((1, 1), (3, 1)):
        swapped[n] = from_ahead(w[n], "core", CORE, 1)
    half = jnp.sum(terms.astype(jnp.float32), axis=0).astype(jnp.bfloat16)
    other = from_ahead(half, "xh", XH, 1)
    trunk = trunk_part(place, acts, list(products((1, 1), (3, 1))), trunk, jnp.float32)
    other, trunk = lock((other, trunk))
    second = jax.nn.silu(half.astype(jnp.float32) + other.astype(jnp.float32) + head_b2[0])
    mine = jnp.sum(second * head_w3[0].astype(jnp.float32), axis=-1) + head_b3[0]
    scores = lax.all_gather(mine, "y", axis=0, tiled=False)
    scores, w[2, 1, 0], w[2, 1, 1] = lock((scores, w[2, 1, 0], w[2, 1, 1]))
    for n in ((2, 1, 0), (2, 1, 1)):
        swapped[n] = from_ahead(w[n], "core", CORE, 1)
    scores = jnp.roll(scores, z, axis=0).reshape(1, Y * count)
    trunk_out = trunk_part(
        place, acts, list(products((2, 1, 0), (2, 1, 1))), trunk, jnp.bfloat16
    )
    return (trunk_out, scores)


def solution(mesh):
    fine = Mesh(mesh.devices.reshape(Z, XL, CORE, Y, XH), ALL)
    in_specs = (
        P(MEMBER, TENSOR),
        P(MEMBER, TENSOR),
        P(MEMBER, TENSOR),
        P(MEMBER, TENSOR),
        P(TENSOR, MEMBER),
        P(),
        P(MEMBER),
        P(MEMBER, None, TENSOR),
        P(MEMBER, TENSOR),
        P(MEMBER, TENSOR, None),
        P(MEMBER, None),
        P(MEMBER, None),
        P(MEMBER),
    )
    out_specs = (P(MEMBER, TENSOR), P(MEMBER, None))
    return jax.shard_map(local, mesh=fine, in_specs=in_specs, out_specs=out_specs, check_vma=False)
```

```python
import functools
import itertools

import jax
import jax.numpy as jnp
from jax import lax
from jax.experimental import pallas as pl
from jax.experimental.pallas import tpu as pltpu
from jax.sharding import Mesh, PartitionSpec as P

HEAD_WIDTH = 128
SEQUENCE_SLOTS = 128
Z, XL, CORE, Y, XH = 4, 2, 2, 4, 2
MEMBER = ("z", "xl", "core")
TENSOR = ("y", "xh")
ALL = MEMBER + TENSOR


def flat(z, xl, core, y, xh):
    return (((z % Z) * XL + xl % XL) * CORE + core) * Y * XH + (y % Y) * XH + xh % XH


def places():
    return itertools.product(range(Z), range(XL), range(CORE), range(Y), range(XH))


def spread_moves(v):
    return [
        (flat(z, xl, core, y, xh), flat(z - y - 2 * v, xl, core, y, xh))
        for z, xl, core, y, xh in places()
    ]


def column_moves(v):
    return [
        (flat(z, xl, core, y, xh), flat(z, xh - xl, core, y + z + 2 * v, xl))
        for z, xl, core, y, xh in places()
    ]


def from_ahead(x, axis, size, step):
    return lax.ppermute(x, axis, [(i, (i - step) % size) for i in range(size)])


def attention(query, keys, values, cand_len):
    row_count = query.shape[0]
    cand_count = row_count // SEQUENCE_SLOTS
    heads_here = query.shape[1] // HEAD_WIDTH
    kv_here = keys.shape[1] // HEAD_WIDTH
    group_width = heads_here // kv_here
    query_tiles = query.reshape(cand_count, SEQUENCE_SLOTS, kv_here, group_width, HEAD_WIDTH)
    key_tiles = keys.reshape(cand_count, SEQUENCE_SLOTS, kv_here, HEAD_WIDTH)
    value_tiles = values.reshape(cand_count, SEQUENCE_SLOTS, kv_here, HEAD_WIDTH)
    logits = jnp.einsum(
        "cskgd,ctkd->ckgst", query_tiles, key_tiles, preferred_element_type=jnp.float32
    ) * HEAD_WIDTH ** (-0.5)
    places = jnp.arange(SEQUENCE_SLOTS, dtype=jnp.int32)
    allowed = (places[None, :, None] >= places[None, None, :]) & (
        places[None, None, :] < cand_len[:, None, None]
    )
    allowed = allowed[:, None, None]
    logits = jnp.where(allowed, logits, jnp.float32(-1e30))
    row_max = jnp.max(logits, axis=-1, keepdims=True)
    probs = jnp.where(allowed, jnp.exp(logits - row_max), jnp.float32(0.0))
    totals = jnp.sum(probs, axis=-1, keepdims=True)
    attn_weights = (probs / totals).astype(jnp.bfloat16)
    attn_out = jnp.einsum(
        "ckgst,ctkd->cskgd", attn_weights, value_tiles, preferred_element_type=jnp.float32
    )
    return attn_out.astype(jnp.bfloat16).reshape(row_count, heads_here * HEAD_WIDTH)


def trunk_kernel(picks, place_ref, here_ref, there_ref, *refs):
    count = len(picks)
    own, other = refs[:count], refs[count : 2 * count]
    base_ref, out_ref, acts, sems = refs[2 * count :]
    j = pl.program_id(0)

    def copies(source):
        for i, (s, v) in enumerate(picks):
            depth = acts.shape[2]
            group = lax.rem(place_ref[0] + 2 * Y - s - 2 * v, Y)
            yield pltpu.make_async_copy(
                source.at[group, :, pl.ds(v * depth, depth)], acts.at[i], sems.at[i]
            )

    @pl.when(j == 0)
    def _():
        @pl.when(place_ref[1] == 0)
        def _():
            for copy in copies(here_ref):
                copy.start()

        @pl.when(place_ref[1] == 1)
        def _():
            for copy in copies(there_ref):
                copy.start()

        for copy in copies(here_ref):
            copy.wait()

    def tile(blocks):
        total = base_ref[...].astype(jnp.float32)
        for i, block in enumerate(blocks):
            total = total + jnp.dot(acts[i], block[...], preferred_element_type=jnp.float32)
        out_ref[...] = total.astype(out_ref.dtype)

    @pl.when(j < 2)
    def _():
        tile(own)

    @pl.when(j >= 2)
    def _():
        tile(other)


def trunk_part(place, here, there, terms, base, dtype):
    rows = here.shape[1]
    half = base.shape[1] // CORE
    width = half // 2
    depth = here.shape[2] // 2

    def weight_spec(w, v, index):
        if w.ndim == 3:
            return pl.BlockSpec((None, depth, width), lambda j, p: (v, 0, index(j)))
        return pl.BlockSpec((depth, width), lambda j, p: (0, index(j)))

    tile = pl.BlockSpec(
        (rows, width), lambda j, p: (0, jnp.where(j < 2, p[2], 1 - p[2]) * 2 + lax.rem(j, 2))
    )
    count = len(terms)
    in_hbm = pltpu.with_memory_space_constraint
    return pl.pallas_call(
        functools.partial(trunk_kernel, [(s, v) for s, v, _, _ in terms]),
        grid_spec=pltpu.PrefetchScalarGridSpec(
            num_scalar_prefetch=1,
            grid=(4,),
            in_specs=[pl.BlockSpec(memory_space=pltpu.HBM)] * 2
            + [weight_spec(w, v, lambda j: jnp.minimum(j, 1)) for _, v, w, _ in terms]
            + [weight_spec(w, v, lambda j: jnp.maximum(j - 2, 0)) for _, v, _, w in terms]
            + [tile],
            out_specs=tile,
            scratch_shapes=[
                pltpu.VMEM((count, rows, depth), here.dtype),
                pltpu.SemaphoreType.DMA((count,)),
            ],
        ),
        out_shape=jax.ShapeDtypeStruct(base.shape, dtype),
        compiler_params=pltpu.CompilerParams(vmem_limit_bytes=32 * 2**20),
        cost_estimate=pl.CostEstimate(
            flops=2 * rows * count * depth * CORE * half,
            bytes_accessed=2 * count * depth * (rows + CORE * half) + 8 * rows * CORE * half,
            transcendentals=0,
        ),
        name="trunk_part",
    )(
        place,
        in_hbm(here, pltpu.HBM),
        in_hbm(there, pltpu.HBM),
        *[t[2] for t in terms],
        *[t[3] for t in terms],
        base,
    )


def norm_kernel(place_ref, p0, p1, p2, p3, gain_ref, out_ref):
    pieces = (p0, p1, p2, p3)
    z = place_ref[0]
    group = p0.shape[1] // Z
    width = p0.shape[2]
    per_z = p0.shape[0]
    scales = []
    for r in range(Z):
        square = jnp.zeros((group, 1), jnp.float32)
        for s in range(Z):
            for q in range(per_z):
                rows = pieces[s][q, pl.ds(((r - s) % Z) * group, group), :].astype(jnp.float32)
                square = square + jnp.sum(rows * rows, axis=-1, keepdims=True)
        scales.append(lax.rsqrt(square / (Z * per_z * width) + 1e-05))
    for s in range(Z):
        for q in range(per_z):
            start = pl.multiple_of((lax.rem(z + s, Z) * per_z + q) * width, width)
            gain = gain_ref[:, pl.ds(start, width)]
            for r in range(Z):
                rows = pieces[s][q, pl.ds(((r - s) % Z) * group, group), :].astype(jnp.float32)
                out_ref[pl.ds(r * group, group), pl.ds(start, width)] = (
                    rows * scales[r] * gain
                ).astype(jnp.bfloat16)


def normalize(pieces, gain, z):
    per_z, rows, width = pieces[0].shape
    total = Z * per_z * width
    return pl.pallas_call(
        norm_kernel,
        in_specs=[pl.BlockSpec(memory_space=pltpu.SMEM)]
        + [pl.BlockSpec(memory_space=pltpu.VMEM)] * 5,
        out_specs=pl.BlockSpec(memory_space=pltpu.VMEM),
        out_shape=jax.ShapeDtypeStruct((rows, total), jnp.bfloat16),
        cost_estimate=pl.CostEstimate(
            flops=8 * rows * total, bytes_accessed=4 * rows * total, transcendentals=rows
        ),
        name="normalize",
    )(z[None], *pieces, gain[None, :])


def local(
    query,
    keys,
    values,
    residual,
    out_weight,
    norm_gain,
    cand_len,
    head_w1,
    head_b1,
    head_w2,
    head_b2,
    head_w3,
    head_b3,
):
    z = lax.axis_index("z")
    xl = lax.axis_index("xl")
    core = lax.axis_index("core")
    y = lax.axis_index("y")
    xh = lax.axis_index("xh")
    cand_count = cand_len.shape[0]

    lock = lax.optimization_barrier
    rows_half = out_weight.shape[0] // 2
    moved = [
        lax.ppermute(out_weight[v * rows_half : (v + 1) * rows_half], ALL, spread_moves(v))
        for v in range(2)
    ]
    attn_out = attention(query, keys, values, cand_len)
    here = lax.all_gather(attn_out, "y", axis=0, tiled=False)

    last_rows = jnp.arange(cand_count, dtype=jnp.int32) * SEQUENCE_SLOTS + cand_len - 1
    picked = jnp.concatenate(
        [jnp.take(attn_out, last_rows, axis=0), jnp.take(residual, last_rows, axis=0)], axis=1
    )
    depth = attn_out.shape[1]
    width = out_weight.shape[1]
    near = lax.all_gather(picked, ("xl", "core"), axis=0, tiled=True)
    near, held, *moved = lock((near, attn_out, *moved))
    across = from_ahead(held, "xh", XH, 1)
    moved = [lax.ppermute(m, ALL, column_moves(v)) for v, m in enumerate(moved)]
    rows = jnp.concatenate([near] + [from_ahead(near, "z", Z, s) for s in (1, 2, 3)], axis=0)
    own = jnp.dot(rows[:, :depth], out_weight, preferred_element_type=jnp.float32)
    res = rows[:, depth:]
    res = jnp.where(core == 0, res[:, :width], res[:, width:]).astype(jnp.float32)
    own = jnp.where((y == z) & (xh == xl), own + res, own).astype(jnp.bfloat16)
    pair = jnp.stack([own, from_ahead(own, "xh", XH, 1)])
    pair, across, *moved = lock((pair, across, *moved))
    there = lax.all_gather(across, "y", axis=0, tiled=False)
    w, swapped = {}, {}
    w[0, 0] = jnp.stack(moved)
    w[1, 0] = from_ahead(w[0, 0], "z", Z, 1)
    w[3, 0] = from_ahead(w[0, 0], "z", Z, 3)
    w[0, 1] = from_ahead(w[0, 0], "xl", XL, 1)
    parts = [pair] + [from_ahead(pair, "y", Y, s) for s in (1, 2, 3)]
    pooled = sum(jnp.sum(p.astype(jnp.float32), axis=0) for p in parts).astype(jnp.bfloat16)
    near = lax.all_gather(pooled, ("xl", "core"), axis=0, tiled=False)
    near, w[1, 0], w[3, 0], w[0, 1] = lock((near, w[1, 0], w[3, 0], w[0, 1]))
    pieces = [near] + [from_ahead(near, "z", Z, s) for s in (1, 2, 3)]
    swapped[0, 0] = from_ahead(w[0, 0], "core", CORE, 1)
    w[2, 0, 0] = from_ahead(w[1, 0][0], "z", Z, 1)
    w[2, 0, 1] = from_ahead(w[3, 0][1], "z", Z, 3)
    for n in ((1, 0), (3, 0)):
        swapped[n] = from_ahead(w[n], "core", CORE, 1)
    features = normalize(pieces, norm_gain, z)
    features, w[2, 0, 0], w[2, 0, 1], swapped[0, 0], w[0, 1] = lock(
        (features, w[2, 0, 0], w[2, 0, 1], swapped[0, 0], w[0, 1])
    )
    w[1, 1] = from_ahead(w[0, 1], "z", Z, 1)
    w[3, 1] = from_ahead(w[0, 1], "z", Z, 3)
    for n in ((2, 0, 0), (2, 0, 1), (0, 1)):
        swapped[n] = from_ahead(w[n], "core", CORE, 1)
    first = jax.nn.silu(
        jnp.dot(features, head_w1[0], preferred_element_type=jnp.float32) + head_b1[0]
    ).astype(jnp.bfloat16)
    terms = jnp.dot(first, head_w2[0], preferred_element_type=jnp.float32).astype(jnp.bfloat16)
    names = [(1, 0), (3, 0), (2, 0, 0), (2, 0, 1)]
    terms, *early = lock((terms, *[swapped[n] for n in names]))
    swapped.update(zip(names, early))
    count = terms.shape[0] // Y
    terms = lax.all_to_all(
        terms.reshape(Y, count, terms.shape[1]), "y", split_axis=0, concat_axis=0, tiled=True
    )

    def product(e, trunk, dtype, *names):
        items = [
            (n[0], v, w[n], swapped[n])
            for n in names
            for v in ((0, 1) if len(n) == 2 else n[2:])
        ]
        place = jnp.stack([lax.rem(y - z + Y, Y), lax.rem(xl + e, XH), core])
        return trunk_part(place, here, there, items, trunk, dtype)

    trunk = product(0, residual, jnp.float32, (0, 0), (1, 0), (3, 0), (2, 0, 0), (2, 0, 1))
    terms, w[1, 1], w[3, 1], swapped[0, 1], trunk = lock(
        (terms, w[1, 1], w[3, 1], swapped[0, 1], trunk)
    )
    w[2, 1, 0] = from_ahead(w[1, 1][0], "z", Z, 1)
    w[2, 1, 1] = from_ahead(w[3, 1][1], "z", Z, 3)
    for n in ((1, 1), (3, 1)):
        swapped[n] = from_ahead(w[n], "core", CORE, 1)
    half = jnp.sum(terms.astype(jnp.float32), axis=0).astype(jnp.bfloat16)
    other = from_ahead(half, "xh", XH, 1)
    trunk = product(1, trunk, jnp.float32, (0, 1), (1, 1), (3, 1))
    other, w[2, 1, 0], w[2, 1, 1], trunk = lock((other, w[2, 1, 0], w[2, 1, 1], trunk))
    second = jax.nn.silu(half.astype(jnp.float32) + other.astype(jnp.float32) + head_b2[0])
    mine = jnp.sum(second * head_w3[0].astype(jnp.float32), axis=-1) + head_b3[0]
    for n in ((2, 1, 0), (2, 1, 1)):
        swapped[n] = from_ahead(w[n], "core", CORE, 1)
    scores = jnp.stack([mine] + [from_ahead(mine, "y", Y, s) for s in (1, 2, 3)])
    scores = jnp.roll(scores, lax.rem(y + z, Y), axis=0).reshape(1, Y * count)
    trunk_out = product(1, trunk, jnp.bfloat16, (2, 1, 0), (2, 1, 1))
    return (trunk_out, scores)


def solution(mesh):
    fine = Mesh(mesh.devices.reshape(Z, XL, CORE, Y, XH), ALL)
    in_specs = (
        P(MEMBER, TENSOR),
        P(MEMBER, TENSOR),
        P(MEMBER, TENSOR),
        P(MEMBER, TENSOR),
        P(TENSOR, MEMBER),
        P(),
        P(MEMBER),
        P(MEMBER, None, TENSOR),
        P(MEMBER, TENSOR),
        P(MEMBER, TENSOR, None),
        P(MEMBER, None),
        P(MEMBER, None),
        P(MEMBER),
    )
    out_specs = (P(MEMBER, TENSOR), P(MEMBER, None))
    return jax.shard_map(local, mesh=fine, in_specs=in_specs, out_specs=out_specs, check_vma=False)
```

```python
import functools
import itertools

import jax
import jax.numpy as jnp
from jax import lax
from jax.experimental import pallas as pl
from jax.experimental.pallas import tpu as pltpu
from jax.sharding import Mesh, PartitionSpec as P

HEAD_WIDTH = 128
SEQUENCE_SLOTS = 128
Z, XL, CORE, Y, XH = 4, 2, 2, 4, 2
MEMBER = ("z", "xl", "core")
TENSOR = ("y", "xh")
ALL = MEMBER + TENSOR


def flat(z, xl, core, y, xh):
    return (((z % Z) * XL + xl % XL) * CORE + core) * Y * XH + (y % Y) * XH + xh % XH


def places():
    return itertools.product(range(Z), range(XL), range(CORE), range(Y), range(XH))


def spread_moves(v):
    return [
        (flat(z, xl, core, y, xh), flat(z - y - 2 * v, xl, core, y, xh))
        for z, xl, core, y, xh in places()
    ]


def column_moves(v):
    return [
        (flat(z, xl, core, y, xh), flat(z, xh, core, y + z + 2 * v, xl))
        for z, xl, core, y, xh in places()
    ]


def from_ahead(x, axis, size, step):
    return lax.ppermute(x, axis, [(i, (i - step) % size) for i in range(size)])


def attention(query, keys, values, cand_len):
    row_count = query.shape[0]
    cand_count = row_count // SEQUENCE_SLOTS
    heads_here = query.shape[1] // HEAD_WIDTH
    kv_here = keys.shape[1] // HEAD_WIDTH
    group_width = heads_here // kv_here
    query_tiles = query.reshape(cand_count, SEQUENCE_SLOTS, kv_here, group_width, HEAD_WIDTH)
    key_tiles = keys.reshape(cand_count, SEQUENCE_SLOTS, kv_here, HEAD_WIDTH)
    value_tiles = values.reshape(cand_count, SEQUENCE_SLOTS, kv_here, HEAD_WIDTH)
    logits = jnp.einsum(
        "cskgd,ctkd->ckgst", query_tiles, key_tiles, preferred_element_type=jnp.float32
    ) * HEAD_WIDTH ** (-0.5)
    places = jnp.arange(SEQUENCE_SLOTS, dtype=jnp.int32)
    allowed = (places[None, :, None] >= places[None, None, :]) & (
        places[None, None, :] < cand_len[:, None, None]
    )
    allowed = allowed[:, None, None]
    logits = jnp.where(allowed, logits, jnp.float32(-1e30))
    row_max = jnp.max(logits, axis=-1, keepdims=True)
    probs = jnp.where(allowed, jnp.exp(logits - row_max), jnp.float32(0.0))
    totals = jnp.sum(probs, axis=-1, keepdims=True)
    attn_weights = (probs / totals).astype(jnp.bfloat16)
    attn_out = jnp.einsum(
        "ckgst,ctkd->cskgd", attn_weights, value_tiles, preferred_element_type=jnp.float32
    )
    return attn_out.astype(jnp.bfloat16).reshape(row_count, heads_here * HEAD_WIDTH)


def trunk_kernel(picks, has_base, place_ref, *refs):
    count = len(picks)
    sources, blocks = refs[:4], refs[4 : 4 + count]
    base_ref = refs[4 + count] if has_base else None
    out_ref, acts, sems = refs[-3:]
    j = pl.program_id(0)

    def copies(which):
        for r in range(CORE):
            for i, (s, v) in enumerate(picks):
                depth = acts.shape[3]
                group = lax.rem(place_ref[0] + 2 * Y - s - 2 * v, Y)
                yield pltpu.make_async_copy(
                    sources[2 * which + r].at[group, :, pl.ds(v * depth, depth)],
                    acts.at[r, i],
                    sems.at[r, i],
                )

    @pl.when(j == 0)
    def _():
        for which in range(2):

            @pl.when(place_ref[1] == which)
            def _():
                for copy in copies(which):
                    copy.start()

        for copy in copies(0):
            copy.wait()

    if has_base:
        total = base_ref[...]
    else:
        total = jnp.zeros(out_ref.shape, jnp.float32)
    r = j // 2
    for i, block in enumerate(blocks):
        total = total + jnp.dot(acts[r, i], block[...], preferred_element_type=jnp.float32)
    out_ref[...] = total.astype(out_ref.dtype)


def trunk_part(place, sources, terms, base, dtype):
    rows = sources[0].shape[1]
    depth = sources[0].shape[2] // 2
    width = terms[0][2].shape[-1]
    count = len(terms)

    def weight_spec(v):
        return pl.BlockSpec((None, depth, width // 2), lambda j, p: (v, 0, lax.rem(j, 2)))

    tile = pl.BlockSpec((rows, width // 2), lambda j, p: (j // 2, lax.rem(j, 2)))
    return pl.pallas_call(
        functools.partial(trunk_kernel, [(s, v) for s, v, _ in terms], base is not None),
        grid_spec=pltpu.PrefetchScalarGridSpec(
            num_scalar_prefetch=1,
            grid=(2 * CORE,),
            in_specs=[pl.BlockSpec(memory_space=pltpu.HBM)] * 4
            + [weight_spec(v) for _, v, _ in terms]
            + ([] if base is None else [tile]),
            out_specs=tile,
            scratch_shapes=[
                pltpu.VMEM((CORE, count, rows, depth), sources[0].dtype),
                pltpu.SemaphoreType.DMA((CORE, count)),
            ],
        ),
        out_shape=jax.ShapeDtypeStruct((CORE * rows, width), dtype),
        compiler_params=pltpu.CompilerParams(vmem_limit_bytes=32 * 2**20),
        cost_estimate=pl.CostEstimate(
            flops=2 * CORE * rows * count * depth * width,
            bytes_accessed=2 * count * depth * (CORE * rows + width) + 8 * CORE * rows * width,
            transcendentals=0,
        ),
        name="trunk_part",
    )(
        place,
        *[pltpu.with_memory_space_constraint(x, pltpu.HBM) for x in sources],
        *[t[2] for t in terms],
        *([] if base is None else [base]),
    )


def norm_kernel(place_ref, p0, p1, p2, p3, gain_ref, out_ref):
    pieces = (p0, p1, p2, p3)
    z = place_ref[0]
    group = p0.shape[1] // Z
    width = p0.shape[2]
    per_z = p0.shape[0]
    scales = []
    for r in range(Z):
        square = jnp.zeros((group, 1), jnp.float32)
        for s in range(Z):
            for q in range(per_z):
                rows = pieces[s][q, pl.ds(((r - s) % Z) * group, group), :].astype(jnp.float32)
                square = square + jnp.sum(rows * rows, axis=-1, keepdims=True)
        scales.append(lax.rsqrt(square / (Z * per_z * width) + 1e-05))
    for s in range(Z):
        for q in range(per_z):
            start = pl.multiple_of((lax.rem(z + s, Z) * per_z + q) * width, width)
            gain = gain_ref[:, pl.ds(start, width)]
            for r in range(Z):
                rows = pieces[s][q, pl.ds(((r - s) % Z) * group, group), :].astype(jnp.float32)
                out_ref[pl.ds(r * group, group), pl.ds(start, width)] = (
                    rows * scales[r] * gain
                ).astype(jnp.bfloat16)


def normalize(pieces, gain, z):
    per_z, rows, width = pieces[0].shape
    total = Z * per_z * width
    return pl.pallas_call(
        norm_kernel,
        in_specs=[pl.BlockSpec(memory_space=pltpu.SMEM)]
        + [pl.BlockSpec(memory_space=pltpu.VMEM)] * 5,
        out_specs=pl.BlockSpec(memory_space=pltpu.VMEM),
        out_shape=jax.ShapeDtypeStruct((rows, total), jnp.bfloat16),
        cost_estimate=pl.CostEstimate(
            flops=8 * rows * total, bytes_accessed=4 * rows * total, transcendentals=rows
        ),
        name="normalize",
    )(z[None], *pieces, gain[None, :])


def local(
    query,
    keys,
    values,
    residual,
    out_weight,
    norm_gain,
    cand_len,
    head_w1,
    head_b1,
    head_w2,
    head_b2,
    head_w3,
    head_b3,
):
    z = lax.axis_index("z")
    xl = lax.axis_index("xl")
    core = lax.axis_index("core")
    y = lax.axis_index("y")
    xh = lax.axis_index("xh")
    cand_count = cand_len.shape[0]

    lock = lax.optimization_barrier
    rows_half = out_weight.shape[0] // 2
    moved = [
        lax.ppermute(out_weight[v * rows_half : (v + 1) * rows_half], ALL, spread_moves(v))
        for v in range(2)
    ]
    attn_out = attention(query, keys, values, cand_len)
    here = lax.all_gather(attn_out, "y", axis=0, tiled=False)

    last_rows = jnp.arange(cand_count, dtype=jnp.int32) * SEQUENCE_SLOTS + cand_len - 1
    picked = jnp.concatenate(
        [jnp.take(attn_out, last_rows, axis=0), jnp.take(residual, last_rows, axis=0)], axis=1
    )
    depth = attn_out.shape[1]
    width = out_weight.shape[1]
    near = lax.all_gather(picked, ("xl", "core"), axis=0, tiled=True)
    near, *moved = lock((near, *moved))
    moved = [lax.ppermute(m, ALL, column_moves(v)) for v, m in enumerate(moved)]
    rows = jnp.concatenate([near] + [from_ahead(near, "z", Z, s) for s in (1, 2, 3)], axis=0)
    own = jnp.dot(rows[:, :depth], out_weight, preferred_element_type=jnp.float32)
    res = rows[:, depth:]
    res = jnp.where(core == 0, res[:, :width], res[:, width:]).astype(jnp.float32)
    own = jnp.where((y == z) & (xh == xl), own + res, own).astype(jnp.bfloat16)
    pair = jnp.stack([own, from_ahead(own, "xh", XH, 1)])
    pair, held, *moved = lock((pair, attn_out, *moved))
    w = {(0, 0): jnp.stack(moved)}
    w[1, 0] = from_ahead(w[0, 0], "z", Z, 1)
    w[3, 0] = from_ahead(w[0, 0], "z", Z, 3)
    across = from_ahead(held, "xh", XH, 1)
    parts = [pair] + [from_ahead(pair, "y", Y, s) for s in (1, 2, 3)]
    pooled = sum(jnp.sum(p.astype(jnp.float32), axis=0) for p in parts).astype(jnp.bfloat16)
    near = lax.all_gather(pooled, ("xl", "core"), axis=0, tiled=False)
    near, w[1, 0], w[3, 0], w[0, 0], across, here = lock(
        (near, w[1, 0], w[3, 0], w[0, 0], across, here)
    )
    there = lax.all_gather(across, "y", axis=0, tiled=False)
    pieces = [near] + [from_ahead(near, "z", Z, s) for s in (1, 2, 3)]
    w[0, 1] = from_ahead(w[0, 0], "xl", XL, 1)
    features = normalize(pieces, norm_gain, z)
    features, w[0, 0], here = lock((features, w[0, 0], here))
    w[2, 0] = from_ahead(w[0, 0], "z", Z, 2)
    here_other = from_ahead(here, "core", CORE, 1)
    first = jax.nn.silu(
        jnp.dot(features, head_w1[0], preferred_element_type=jnp.float32) + head_b1[0]
    ).astype(jnp.bfloat16)
    terms = jnp.dot(first, head_w2[0], preferred_element_type=jnp.float32).astype(jnp.bfloat16)
    terms, w[0, 1] = lock((terms, w[0, 1]))
    w[1, 1] = from_ahead(w[0, 1], "z", Z, 1)
    w[3, 1] = from_ahead(w[0, 1], "z", Z, 3)
    count = terms.shape[0] // Y
    terms = lax.all_to_all(
        terms.reshape(Y, count, terms.shape[1]), "y", split_axis=0, concat_axis=0, tiled=True
    )
    terms, w[2, 0], w[0, 1], here_other = lock((terms, w[2, 0], w[0, 1], here_other))
    w[2, 1] = from_ahead(w[0, 1], "z", Z, 2)
    half = jnp.sum(terms.astype(jnp.float32), axis=0).astype(jnp.bfloat16)
    other = from_ahead(half, "xh", XH, 1)
    second = jax.nn.silu(half.astype(jnp.float32) + other.astype(jnp.float32) + head_b2[0])
    mine = jnp.sum(second * head_w3[0].astype(jnp.float32), axis=-1) + head_b3[0]
    scores = jnp.stack([mine] + [from_ahead(mine, "y", Y, s) for s in (1, 2, 3)])
    scores = jnp.roll(scores, lax.rem(y + z, Y), axis=0).reshape(1, Y * count)

    scores, w[1, 1], w[3, 1], there = lock((scores, w[1, 1], w[3, 1], there))
    sources = (here, here_other, there, from_ahead(there, "core", CORE, 1))

    def product(e, trunk, dtype):
        items = [(s, v, w[s, e]) for s in range(Z) for v in range(2)]
        place = jnp.stack([lax.rem(y - z + Y, Y), lax.rem(xl + e + xh, XH)])
        return trunk_part(place, sources, items, trunk, dtype)

    trunk = product(0, None, jnp.float32)
    trunk = product(1, trunk, jnp.bfloat16)
    row_count = residual.shape[0]
    mine = trunk[:row_count]
    other = from_ahead(trunk[row_count:], "core", CORE, 1)
    left, right = jnp.where(core == 0, mine, other), jnp.where(core == 0, other, mine)
    trunk = jnp.concatenate([left, right], axis=1).astype(jnp.float32)
    trunk_out = (trunk + residual.astype(jnp.float32)).astype(jnp.bfloat16)
    return (trunk_out, scores)


def solution(mesh):
    fine = Mesh(mesh.devices.reshape(Z, XL, CORE, Y, XH), ALL)
    in_specs = (
        P(MEMBER, TENSOR),
        P(MEMBER, TENSOR),
        P(MEMBER, TENSOR),
        P(MEMBER, TENSOR),
        P(TENSOR, MEMBER),
        P(),
        P(MEMBER),
        P(MEMBER, None, TENSOR),
        P(MEMBER, TENSOR),
        P(MEMBER, TENSOR, None),
        P(MEMBER, None),
        P(MEMBER, None),
        P(MEMBER),
    )
    out_specs = (P(MEMBER, TENSOR), P(MEMBER, None))
    return jax.shard_map(local, mesh=fine, in_specs=in_specs, out_specs=out_specs, check_vma=False)
```

```python
import functools
import itertools

import jax
import jax.numpy as jnp
from jax import lax
from jax.experimental import pallas as pl
from jax.experimental.pallas import tpu as pltpu
from jax.sharding import Mesh, PartitionSpec as P

HEAD_WIDTH = 128
SEQUENCE_SLOTS = 128
Z, XL, CORE, Y, XH = 4, 2, 2, 4, 2
MEMBER = ("z", "xl", "core")
TENSOR = ("y", "xh")
ALL = MEMBER + TENSOR


def flat(z, xl, core, y, xh):
    return (((z % Z) * XL + xl % XL) * CORE + core) * Y * XH + (y % Y) * XH + xh % XH


def places():
    return itertools.product(range(Z), range(XL), range(CORE), range(Y), range(XH))


def spread_moves(v):
    return [
        (flat(z, xl, core, y, xh), flat(z - y - 2 * v, xl, core, y, xh))
        for z, xl, core, y, xh in places()
    ]


def column_moves(v):
    return [
        (flat(z, xl, core, y, xh), flat(z, xh, core, y + z + 2 * v, xl))
        for z, xl, core, y, xh in places()
    ]


def from_ahead(x, axis, size, step):
    return lax.ppermute(x, axis, [(i, (i - step) % size) for i in range(size)])


def attention(query, keys, values, cand_len):
    row_count = query.shape[0]
    cand_count = row_count // SEQUENCE_SLOTS
    heads_here = query.shape[1] // HEAD_WIDTH
    kv_here = keys.shape[1] // HEAD_WIDTH
    group_width = heads_here // kv_here
    query_tiles = query.reshape(cand_count, SEQUENCE_SLOTS, kv_here, group_width, HEAD_WIDTH)
    key_tiles = keys.reshape(cand_count, SEQUENCE_SLOTS, kv_here, HEAD_WIDTH)
    value_tiles = values.reshape(cand_count, SEQUENCE_SLOTS, kv_here, HEAD_WIDTH)
    logits = jnp.einsum(
        "cskgd,ctkd->ckgst", query_tiles, key_tiles, preferred_element_type=jnp.float32
    ) * HEAD_WIDTH ** (-0.5)
    places = jnp.arange(SEQUENCE_SLOTS, dtype=jnp.int32)
    allowed = (places[None, :, None] >= places[None, None, :]) & (
        places[None, None, :] < cand_len[:, None, None]
    )
    allowed = allowed[:, None, None]
    logits = jnp.where(allowed, logits, jnp.float32(-1e30))
    row_max = jnp.max(logits, axis=-1, keepdims=True)
    probs = jnp.where(allowed, jnp.exp(logits - row_max), jnp.float32(0.0))
    totals = jnp.sum(probs, axis=-1, keepdims=True)
    attn_weights = (probs / totals).astype(jnp.bfloat16)
    attn_out = jnp.einsum(
        "ckgst,ctkd->cskgd", attn_weights, value_tiles, preferred_element_type=jnp.float32
    )
    return attn_out.astype(jnp.bfloat16).reshape(row_count, heads_here * HEAD_WIDTH)


def trunk_kernel(picks, has_base, place_ref, *refs):
    count = len(picks)
    sources, blocks = refs[:4], refs[4 : 4 + count]
    base_ref = refs[4 + count] if has_base else None
    out_ref, acts, sems = refs[-3:]
    j = pl.program_id(0)

    def copies(which):
        for r in range(CORE):
            for i, (s, v) in enumerate(picks):
                depth = acts.shape[3]
                group = lax.rem(place_ref[0] + 2 * Y - s - 2 * v, Y)
                yield pltpu.make_async_copy(
                    sources[2 * which + r].at[group, :, pl.ds(v * depth, depth)],
                    acts.at[r, i],
                    sems.at[r, i],
                )

    @pl.when(j == 0)
    def _():
        for which in range(2):

            @pl.when(place_ref[1] == which)
            def _():
                for copy in copies(which):
                    copy.start()

        for copy in copies(0):
            copy.wait()

    if has_base:
        total = base_ref[...]
    else:
        total = jnp.zeros(out_ref.shape, jnp.float32)
    r = j // 2
    for i, block in enumerate(blocks):
        total = total + jnp.dot(acts[r, i], block[...], preferred_element_type=jnp.float32)
    out_ref[...] = total.astype(out_ref.dtype)


def trunk_part(place, sources, terms, base, dtype):
    rows = sources[0].shape[1]
    depth = sources[0].shape[2] // 2
    width = terms[0][2].shape[-1]
    count = len(terms)

    def weight_spec(v):
        return pl.BlockSpec((None, depth, width // 2), lambda j, p: (v, 0, lax.rem(j, 2)))

    tile = pl.BlockSpec((rows, width // 2), lambda j, p: (j // 2, lax.rem(j, 2)))
    return pl.pallas_call(
        functools.partial(trunk_kernel, [(s, v) for s, v, _ in terms], base is not None),
        grid_spec=pltpu.PrefetchScalarGridSpec(
            num_scalar_prefetch=1,
            grid=(2 * CORE,),
            in_specs=[pl.BlockSpec(memory_space=pltpu.HBM)] * 4
            + [weight_spec(v) for _, v, _ in terms]
            + ([] if base is None else [tile]),
            out_specs=tile,
            scratch_shapes=[
                pltpu.VMEM((CORE, count, rows, depth), sources[0].dtype),
                pltpu.SemaphoreType.DMA((CORE, count)),
            ],
        ),
        out_shape=jax.ShapeDtypeStruct((CORE * rows, width), dtype),
        compiler_params=pltpu.CompilerParams(vmem_limit_bytes=32 * 2**20),
        cost_estimate=pl.CostEstimate(
            flops=CORE * rows * width, bytes_accessed=CORE * rows * width, transcendentals=0
        ),
        name="trunk_part",
    )(
        place,
        *[pltpu.with_memory_space_constraint(x, pltpu.HBM) for x in sources],
        *[t[2] for t in terms],
        *([] if base is None else [base]),
    )


def norm_kernel(place_ref, p0, p1, p2, p3, gain_ref, out_ref):
    pieces = (p0, p1, p2, p3)
    z = place_ref[0]
    group = p0.shape[1] // Z
    width = p0.shape[2]
    per_z = p0.shape[0]
    scales = []
    for r in range(Z):
        square = jnp.zeros((group, 1), jnp.float32)
        for s in range(Z):
            for q in range(per_z):
                rows = pieces[s][q, pl.ds(((r - s) % Z) * group, group), :].astype(jnp.float32)
                square = square + jnp.sum(rows * rows, axis=-1, keepdims=True)
        scales.append(lax.rsqrt(square / (Z * per_z * width) + 1e-05))
    for s in range(Z):
        for q in range(per_z):
            start = pl.multiple_of((lax.rem(z + s, Z) * per_z + q) * width, width)
            gain = gain_ref[:, pl.ds(start, width)]
            for r in range(Z):
                rows = pieces[s][q, pl.ds(((r - s) % Z) * group, group), :].astype(jnp.float32)
                out_ref[pl.ds(r * group, group), pl.ds(start, width)] = (
                    rows * scales[r] * gain
                ).astype(jnp.bfloat16)


def normalize(pieces, gain, z):
    per_z, rows, width = pieces[0].shape
    total = Z * per_z * width
    return pl.pallas_call(
        norm_kernel,
        in_specs=[pl.BlockSpec(memory_space=pltpu.SMEM)]
        + [pl.BlockSpec(memory_space=pltpu.VMEM)] * 5,
        out_specs=pl.BlockSpec(memory_space=pltpu.VMEM),
        out_shape=jax.ShapeDtypeStruct((rows, total), jnp.bfloat16),
        cost_estimate=pl.CostEstimate(
            flops=8 * rows * total, bytes_accessed=4 * rows * total, transcendentals=rows
        ),
        name="normalize",
    )(z[None], *pieces, gain[None, :])


def local(
    query,
    keys,
    values,
    residual,
    out_weight,
    norm_gain,
    cand_len,
    head_w1,
    head_b1,
    head_w2,
    head_b2,
    head_w3,
    head_b3,
):
    z = lax.axis_index("z")
    xl = lax.axis_index("xl")
    core = lax.axis_index("core")
    y = lax.axis_index("y")
    xh = lax.axis_index("xh")
    cand_count = cand_len.shape[0]

    lock = lax.optimization_barrier
    rows_half = out_weight.shape[0] // 2
    moved = [
        lax.ppermute(out_weight[v * rows_half : (v + 1) * rows_half], ALL, spread_moves(v))
        for v in range(2)
    ]
    attn_out = attention(query, keys, values, cand_len)
    here = lax.all_gather(attn_out, "y", axis=0, tiled=False)

    last_rows = jnp.arange(cand_count, dtype=jnp.int32) * SEQUENCE_SLOTS + cand_len - 1
    picked = jnp.concatenate(
        [jnp.take(attn_out, last_rows, axis=0), jnp.take(residual, last_rows, axis=0)], axis=1
    )
    depth = attn_out.shape[1]
    width = out_weight.shape[1]
    near = lax.all_gather(picked, ("xl", "core"), axis=0, tiled=True)
    near, *moved = lock((near, *moved))
    moved = [lax.ppermute(m, ALL, column_moves(v)) for v, m in enumerate(moved)]
    rows = jnp.concatenate([near] + [from_ahead(near, "z", Z, s) for s in (1, 2, 3)], axis=0)
    own = jnp.dot(rows[:, :depth], out_weight, preferred_element_type=jnp.float32)
    res = rows[:, depth:]
    res = jnp.where(core == 0, res[:, :width], res[:, width:]).astype(jnp.float32)
    own = jnp.where((y == z) & (xh == xl), own + res, own).astype(jnp.bfloat16)
    pair = jnp.stack([own, from_ahead(own, "xh", XH, 1)])
    pair, held, *moved = lock((pair, attn_out, *moved))
    w = {(0, 0): jnp.stack(moved)}
    w[1, 0] = from_ahead(w[0, 0], "z", Z, 1)
    w[3, 0] = from_ahead(w[0, 0], "z", Z, 3)
    w[2, 0] = from_ahead(w[0, 0], "z", Z, 2)
    across = from_ahead(held, "xh", XH, 1)
    parts = [pair] + [from_ahead(pair, "y", Y, s) for s in (1, 2, 3)]
    pooled = sum(jnp.sum(p.astype(jnp.float32), axis=0) for p in parts).astype(jnp.bfloat16)
    pooled, across = lock((pooled, across))
    there = lax.all_gather(across, "y", axis=0, tiled=False)
    near = lax.all_gather(pooled, ("xl", "core"), axis=0, tiled=False)
    near, w[1, 0], w[3, 0], w[2, 0], w[0, 0], here = lock(
        (near, w[1, 0], w[3, 0], w[2, 0], w[0, 0], here)
    )
    pieces = [near] + [from_ahead(near, "z", Z, s) for s in (1, 2, 3)]
    w[0, 1] = from_ahead(w[0, 0], "xl", XL, 1)
    features = normalize(pieces, norm_gain, z)
    features, w[0, 1], here = lock((features, w[0, 1], here))
    w[1, 1] = from_ahead(w[0, 1], "z", Z, 1)
    w[3, 1] = from_ahead(w[0, 1], "z", Z, 3)
    here_other = from_ahead(here, "core", CORE, 1)
    first = jax.nn.silu(
        jnp.dot(features, head_w1[0], preferred_element_type=jnp.float32) + head_b1[0]
    ).astype(jnp.bfloat16)
    terms = jnp.dot(first, head_w2[0], preferred_element_type=jnp.float32).astype(jnp.bfloat16)
    count = terms.shape[0] // Y
    terms = lax.all_to_all(
        terms.reshape(Y, count, terms.shape[1]), "y", split_axis=0, concat_axis=0, tiled=True
    )
    terms, there, w[0, 1], w[1, 1], w[3, 1], here_other = lock(
        (terms, there, w[0, 1], w[1, 1], w[3, 1], here_other)
    )
    there_other = from_ahead(there, "core", CORE, 1)
    w[2, 1] = from_ahead(w[0, 1], "z", Z, 2)
    half = jnp.sum(terms.astype(jnp.float32), axis=0).astype(jnp.bfloat16)
    other = from_ahead(half, "xh", XH, 1)
    second = jax.nn.silu(half.astype(jnp.float32) + other.astype(jnp.float32) + head_b2[0])
    mine = jnp.sum(second * head_w3[0].astype(jnp.float32), axis=-1) + head_b3[0]
    scores = jnp.stack([mine] + [from_ahead(mine, "y", Y, s) for s in (1, 2, 3)])
    scores = jnp.roll(scores, lax.rem(y + z, Y), axis=0).reshape(1, Y * count)


    def product(e, trunk, dtype):
        items = [(s, v, w[s, e]) for s in range(Z) for v in range(2)]
        place = jnp.stack([lax.rem(y - z + Y, Y), lax.rem(xl + e + xh, XH)])
        return trunk_part(place, sources, items, trunk, dtype)

    scores, there_other = lock((scores, there_other))
    sources = (here, here_other, there, there_other)
    trunk = product(0, None, jnp.float32)
    trunk = product(1, trunk, jnp.bfloat16)
    row_count = residual.shape[0]
    mine = trunk[:row_count]
    other = from_ahead(trunk[row_count:], "core", CORE, 1)
    left, right = jnp.where(core == 0, mine, other), jnp.where(core == 0, other, mine)
    trunk = jnp.concatenate([left, right], axis=1).astype(jnp.float32)
    trunk_out = (trunk + residual.astype(jnp.float32)).astype(jnp.bfloat16)
    return (trunk_out, scores)


def solution(mesh):
    fine = Mesh(mesh.devices.reshape(Z, XL, CORE, Y, XH), ALL)
    in_specs = (
        P(MEMBER, TENSOR),
        P(MEMBER, TENSOR),
        P(MEMBER, TENSOR),
        P(MEMBER, TENSOR),
        P(TENSOR, MEMBER),
        P(),
        P(MEMBER),
        P(MEMBER, None, TENSOR),
        P(MEMBER, TENSOR),
        P(MEMBER, TENSOR, None),
        P(MEMBER, None),
        P(MEMBER, None),
        P(MEMBER),
    )
    out_specs = (P(MEMBER, TENSOR), P(MEMBER, None))
    return jax.shard_map(local, mesh=fine, in_specs=in_specs, out_specs=out_specs, check_vma=False)
```

```python
import functools
import itertools

import jax
import jax.numpy as jnp
from jax import lax
from jax.experimental import pallas as pl
from jax.experimental.pallas import tpu as pltpu
from jax.sharding import Mesh, PartitionSpec as P

HEAD_WIDTH = 128
SEQUENCE_SLOTS = 128
Z, XL, CORE, Y, XH = 4, 2, 2, 4, 2
MEMBER = ("z", "xl", "core")
TENSOR = ("y", "xh")
ALL = MEMBER + TENSOR


def flat(z, xl, core, y, xh):
    return (((z % Z) * XL + xl % XL) * CORE + core) * Y * XH + (y % Y) * XH + xh % XH


def places():
    return itertools.product(range(Z), range(XL), range(CORE), range(Y), range(XH))


def spread_moves(v):
    return [
        (flat(z, xl, core, y, xh), flat(z - y - 2 * v, xl, core, y, xh))
        for z, xl, core, y, xh in places()
    ]


def column_moves(v):
    return [
        (flat(z, xl, core, y, xh), flat(z, xh, core, y + z + 2 * v, xl))
        for z, xl, core, y, xh in places()
    ]


def from_ahead(x, axis, size, step):
    return lax.ppermute(x, axis, [(i, (i - step) % size) for i in range(size)])


def attention(query, keys, values, cand_len):
    row_count = query.shape[0]
    cand_count = row_count // SEQUENCE_SLOTS
    heads_here = query.shape[1] // HEAD_WIDTH
    kv_here = keys.shape[1] // HEAD_WIDTH
    group_width = heads_here // kv_here
    query_tiles = query.reshape(cand_count, SEQUENCE_SLOTS, kv_here, group_width, HEAD_WIDTH)
    key_tiles = keys.reshape(cand_count, SEQUENCE_SLOTS, kv_here, HEAD_WIDTH)
    value_tiles = values.reshape(cand_count, SEQUENCE_SLOTS, kv_here, HEAD_WIDTH)
    logits = jnp.einsum(
        "cskgd,ctkd->ckgst", query_tiles, key_tiles, preferred_element_type=jnp.float32
    ) * HEAD_WIDTH ** (-0.5)
    places = jnp.arange(SEQUENCE_SLOTS, dtype=jnp.int32)
    allowed = (places[None, :, None] >= places[None, None, :]) & (
        places[None, None, :] < cand_len[:, None, None]
    )
    allowed = allowed[:, None, None]
    logits = jnp.where(allowed, logits, jnp.float32(-1e30))
    row_max = jnp.max(logits, axis=-1, keepdims=True)
    probs = jnp.where(allowed, jnp.exp(logits - row_max), jnp.float32(0.0))
    totals = jnp.sum(probs, axis=-1, keepdims=True)
    attn_weights = (probs / totals).astype(jnp.bfloat16)
    attn_out = jnp.einsum(
        "ckgst,ctkd->cskgd", attn_weights, value_tiles, preferred_element_type=jnp.float32
    )
    return attn_out.astype(jnp.bfloat16).reshape(row_count, heads_here * HEAD_WIDTH)


def trunk_kernel(picks, has_base, place_ref, *refs):
    count = len(picks)
    sources, blocks = refs[:4], refs[4 : 4 + count]
    base_ref = refs[4 + count] if has_base else None
    out_ref, acts, sems = refs[-3:]
    j = pl.program_id(0)

    def copies(which):
        for r in range(CORE):
            for i, (s, v) in enumerate(picks):
                depth = acts.shape[3]
                group = lax.rem(place_ref[0] + 2 * Y - s - 2 * v, Y)
                yield pltpu.make_async_copy(
                    sources[2 * which + r].at[group, :, pl.ds(v * depth, depth)],
                    acts.at[r, i],
                    sems.at[r, i],
                )

    @pl.when(j == 0)
    def _():
        for which in range(2):

            @pl.when(place_ref[1] == which)
            def _():
                for copy in copies(which):
                    copy.start()

        for copy in copies(0):
            copy.wait()

    if has_base:
        total = base_ref[...]
    else:
        total = jnp.zeros(out_ref.shape, jnp.float32)
    r = j // 2
    for i, block in enumerate(blocks):
        total = total + jnp.dot(acts[r, i], block[...], preferred_element_type=jnp.float32)
    out_ref[...] = total.astype(out_ref.dtype)


def trunk_part(place, sources, terms, base, dtype):
    rows = sources[0].shape[1]
    depth = sources[0].shape[2] // 2
    width = terms[0][2].shape[-1]
    count = len(terms)

    def weight_spec(v, w):
        if w.ndim == 2:
            return pl.BlockSpec((depth, width // 2), lambda j, p: (0, lax.rem(j, 2)))
        return pl.BlockSpec((None, depth, width // 2), lambda j, p: (v, 0, lax.rem(j, 2)))

    tile = pl.BlockSpec((rows, width // 2), lambda j, p: (j // 2, lax.rem(j, 2)))
    return pl.pallas_call(
        functools.partial(trunk_kernel, [(s, v) for s, v, _ in terms], base is not None),
        grid_spec=pltpu.PrefetchScalarGridSpec(
            num_scalar_prefetch=1,
            grid=(2 * CORE,),
            in_specs=[pl.BlockSpec(memory_space=pltpu.HBM)] * 4
            + [weight_spec(v, w) for _, v, w in terms]
            + ([] if base is None else [tile]),
            out_specs=tile,
            scratch_shapes=[
                pltpu.VMEM((CORE, count, rows, depth), sources[0].dtype),
                pltpu.SemaphoreType.DMA((CORE, count)),
            ],
        ),
        out_shape=jax.ShapeDtypeStruct((CORE * rows, width), dtype),
        compiler_params=pltpu.CompilerParams(vmem_limit_bytes=32 * 2**20),
        cost_estimate=pl.CostEstimate(
            flops=CORE * rows * width, bytes_accessed=CORE * rows * width, transcendentals=0
        ),
        name="trunk_part",
    )(
        place,
        *[pltpu.with_memory_space_constraint(x, pltpu.HBM) for x in sources],
        *[t[2] for t in terms],
        *([] if base is None else [base]),
    )


def norm_kernel(place_ref, p0, p1, p2, p3, gain_ref, out_ref):
    pieces = (p0, p1, p2, p3)
    z = place_ref[0]
    group = p0.shape[1] // Z
    width = p0.shape[2]
    per_z = p0.shape[0]
    scales = []
    for r in range(Z):
        square = jnp.zeros((group, 1), jnp.float32)
        for s in range(Z):
            for q in range(per_z):
                rows = pieces[s][q, pl.ds(((r - s) % Z) * group, group), :].astype(jnp.float32)
                square = square + jnp.sum(rows * rows, axis=-1, keepdims=True)
        scales.append(lax.rsqrt(square / (Z * per_z * width) + 1e-05))
    for s in range(Z):
        for q in range(per_z):
            start = pl.multiple_of((lax.rem(z + s, Z) * per_z + q) * width, width)
            gain = gain_ref[:, pl.ds(start, width)]
            for r in range(Z):
                rows = pieces[s][q, pl.ds(((r - s) % Z) * group, group), :].astype(jnp.float32)
                out_ref[pl.ds(r * group, group), pl.ds(start, width)] = (
                    rows * scales[r] * gain
                ).astype(jnp.bfloat16)


def normalize(pieces, gain, z):
    per_z, rows, width = pieces[0].shape
    total = Z * per_z * width
    return pl.pallas_call(
        norm_kernel,
        in_specs=[pl.BlockSpec(memory_space=pltpu.SMEM)]
        + [pl.BlockSpec(memory_space=pltpu.VMEM)] * 5,
        out_specs=pl.BlockSpec(memory_space=pltpu.VMEM),
        out_shape=jax.ShapeDtypeStruct((rows, total), jnp.bfloat16),
        cost_estimate=pl.CostEstimate(
            flops=8 * rows * total, bytes_accessed=4 * rows * total, transcendentals=rows
        ),
        name="normalize",
    )(z[None], *pieces, gain[None, :])


def local(
    query,
    keys,
    values,
    residual,
    out_weight,
    norm_gain,
    cand_len,
    head_w1,
    head_b1,
    head_w2,
    head_b2,
    head_w3,
    head_b3,
):
    z = lax.axis_index("z")
    xl = lax.axis_index("xl")
    core = lax.axis_index("core")
    y = lax.axis_index("y")
    xh = lax.axis_index("xh")
    cand_count = cand_len.shape[0]

    lock = lax.optimization_barrier
    rows_half = out_weight.shape[0] // 2
    moved = [
        lax.ppermute(out_weight[v * rows_half : (v + 1) * rows_half], ALL, spread_moves(v))
        for v in range(2)
    ]
    attn_out = attention(query, keys, values, cand_len)
    here = lax.all_gather(attn_out, "y", axis=0, tiled=False)

    last_rows = jnp.arange(cand_count, dtype=jnp.int32) * SEQUENCE_SLOTS + cand_len - 1
    picked = jnp.concatenate(
        [jnp.take(attn_out, last_rows, axis=0), jnp.take(residual, last_rows, axis=0)], axis=1
    )
    depth = attn_out.shape[1]
    width = out_weight.shape[1]
    near = lax.all_gather(picked, ("xl", "core"), axis=0, tiled=True)
    near, *moved = lock((near, *moved))
    moved = [lax.ppermute(m, ALL, column_moves(v)) for v, m in enumerate(moved)]
    rows = jnp.concatenate([near] + [from_ahead(near, "z", Z, s) for s in (1, 2, 3)], axis=0)
    own = jnp.dot(rows[:, :depth], out_weight, preferred_element_type=jnp.float32)
    res = rows[:, depth:]
    res = jnp.where(core == 0, res[:, :width], res[:, width:]).astype(jnp.float32)
    own = jnp.where((y == z) & (xh == xl), own + res, own).astype(jnp.bfloat16)
    pair = jnp.stack([own, from_ahead(own, "xh", XH, 1)])
    pair, held, *moved = lock((pair, attn_out, *moved))
    w = {(0, 0): jnp.stack(moved)}
    w[1, 0] = from_ahead(w[0, 0], "z", Z, 1)
    w[3, 0] = from_ahead(w[0, 0], "z", Z, 3)
    across = from_ahead(held, "xh", XH, 1)
    parts = [pair] + [from_ahead(pair, "y", Y, s) for s in (1, 2, 3)]
    pooled = sum(jnp.sum(p.astype(jnp.float32), axis=0) for p in parts).astype(jnp.bfloat16)
    pooled, across = lock((pooled, across))
    there = lax.all_gather(across, "y", axis=0, tiled=False)
    near = lax.all_gather(pooled, ("xl", "core"), axis=0, tiled=False)
    near, w[1, 0], w[3, 0], w[0, 0], here = lock((near, w[1, 0], w[3, 0], w[0, 0], here))
    pieces = [near] + [from_ahead(near, "z", Z, s) for s in (1, 2, 3)]
    w[0, 1] = from_ahead(w[0, 0], "xl", XL, 1)
    pieces[1], w[1, 0], w[3, 0] = lock((pieces[1], w[1, 0], w[3, 0]))
    w[2, 0] = [from_ahead(w[1, 0][0], "z", Z, 1), from_ahead(w[3, 0][1], "z", Z, 3)]
    features = normalize(pieces, norm_gain, z)
    features, w[0, 1], here, *w[2, 0] = lock((features, w[0, 1], here, *w[2, 0]))
    w[1, 1] = from_ahead(w[0, 1], "z", Z, 1)
    w[3, 1] = from_ahead(w[0, 1], "z", Z, 3)
    here_other = from_ahead(here, "core", CORE, 1)
    first = jax.nn.silu(
        jnp.dot(features, head_w1[0], preferred_element_type=jnp.float32) + head_b1[0]
    ).astype(jnp.bfloat16)
    terms = jnp.dot(first, head_w2[0], preferred_element_type=jnp.float32).astype(jnp.bfloat16)
    count = terms.shape[0] // Y
    terms = lax.all_to_all(
        terms.reshape(Y, count, terms.shape[1]), "y", split_axis=0, concat_axis=0, tiled=True
    )
    terms, w[0, 1], w[1, 1], w[3, 1], here_other = lock(
        (terms, w[0, 1], w[1, 1], w[3, 1], here_other)
    )
    w[2, 1] = from_ahead(w[0, 1], "z", Z, 2)
    half = jnp.sum(terms.astype(jnp.float32), axis=0).astype(jnp.bfloat16)
    other = from_ahead(half, "xh", XH, 1)
    second = jax.nn.silu(half.astype(jnp.float32) + other.astype(jnp.float32) + head_b2[0])
    second, there = lock((second, there))
    there_other = from_ahead(there, "core", CORE, 1)
    mine = jnp.sum(second * head_w3[0].astype(jnp.float32), axis=-1) + head_b3[0]
    scores = jnp.stack([mine] + [from_ahead(mine, "y", Y, s) for s in (1, 2, 3)])
    scores = jnp.roll(scores, lax.rem(y + z, Y), axis=0).reshape(1, Y * count)


    def product(e, trunk, dtype):
        items = [
            (s, v, w[s, e][v] if isinstance(w[s, e], list) else w[s, e])
            for s in range(Z)
            for v in range(2)
        ]
        place = jnp.stack([lax.rem(y - z + Y, Y), lax.rem(xl + e + xh, XH)])
        return trunk_part(place, sources, items, trunk, dtype)

    scores, there_other = lock((scores, there_other))
    sources = (here, here_other, there, there_other)
    trunk = product(0, None, jnp.float32)
    trunk = product(1, trunk, jnp.bfloat16)
    row_count = residual.shape[0]
    mine = trunk[:row_count]
    other = from_ahead(trunk[row_count:], "core", CORE, 1)
    left, right = jnp.where(core == 0, mine, other), jnp.where(core == 0, other, mine)
    trunk = jnp.concatenate([left, right], axis=1).astype(jnp.float32)
    trunk_out = (trunk + residual.astype(jnp.float32)).astype(jnp.bfloat16)
    return (trunk_out, scores)


def solution(mesh):
    fine = Mesh(mesh.devices.reshape(Z, XL, CORE, Y, XH), ALL)
    in_specs = (
        P(MEMBER, TENSOR),
        P(MEMBER, TENSOR),
        P(MEMBER, TENSOR),
        P(MEMBER, TENSOR),
        P(TENSOR, MEMBER),
        P(),
        P(MEMBER),
        P(MEMBER, None, TENSOR),
        P(MEMBER, TENSOR),
        P(MEMBER, TENSOR, None),
        P(MEMBER, None),
        P(MEMBER, None),
        P(MEMBER),
    )
    out_specs = (P(MEMBER, TENSOR), P(MEMBER, None))
    return jax.shard_map(local, mesh=fine, in_specs=in_specs, out_specs=out_specs, check_vma=False)
```

```python
import functools
import itertools

import jax
import jax.numpy as jnp
from jax import lax
from jax.experimental import pallas as pl
from jax.experimental.pallas import tpu as pltpu
from jax.sharding import Mesh, PartitionSpec as P

HEAD_WIDTH = 128
Z, XL, CORE, Y, XH = 4, 2, 2, 4, 2
MEMBER = ("z", "xl", "core")
TENSOR = ("y", "xh")
ALL = MEMBER + TENSOR


def flat(z, xl, core, y, xh):
    return (((z % Z) * XL + xl % XL) * CORE + core) * Y * XH + (y % Y) * XH + xh % XH


def places():
    return itertools.product(range(Z), range(XL), range(CORE), range(Y), range(XH))


def spread_moves(v):
    return [
        (flat(z, xl, core, y, xh), flat(z - y - 2 * v, xl, core, y, xh))
        for z, xl, core, y, xh in places()
    ]


def column_moves(v):
    return [
        (flat(z, xl, core, y, xh), flat(z, xh, core, y + z + 2 * v, xl))
        for z, xl, core, y, xh in places()
    ]


def from_ahead(x, axis, size, step):
    return lax.ppermute(x, axis, [(i, (i - step) % size) for i in range(size)])


def attention_kernel(len_ref, query_ref, keys_ref, values_ref, residual_ref, out_ref, picked_ref):
    length = len_ref[pl.program_id(0)]
    slots, width = query_ref.shape
    heads = width // HEAD_WIDTH
    queries = jnp.concatenate(
        [query_ref[:, h * HEAD_WIDTH : (h + 1) * HEAD_WIDTH] for h in range(heads)], axis=0
    )
    logits = lax.dot_general(
        queries, keys_ref[...], (((1,), (1,)), ((), ())), preferred_element_type=jnp.float32
    ) * HEAD_WIDTH ** (-0.5)
    row = lax.rem(lax.broadcasted_iota(jnp.int32, logits.shape, 0), slots)
    column = lax.broadcasted_iota(jnp.int32, logits.shape, 1)
    allowed = (row >= column) & (column < length)
    logits = jnp.where(allowed, logits, jnp.float32(-1e30))
    row_max = jnp.max(logits, axis=-1, keepdims=True)
    probs = jnp.where(allowed, jnp.exp(logits - row_max), jnp.float32(0.0))
    totals = jnp.sum(probs, axis=-1, keepdims=True)
    weights = (probs / totals).astype(jnp.bfloat16)
    result = jnp.dot(weights, values_ref[...], preferred_element_type=jnp.float32)
    result = result.astype(jnp.bfloat16)
    scored = lax.broadcasted_iota(jnp.int32, (slots, 1), 0) == length - 1
    for h in range(heads):
        part = result[h * slots : (h + 1) * slots]
        out_ref[:, h * HEAD_WIDTH : (h + 1) * HEAD_WIDTH] = part
        picked_ref[0, :, h * HEAD_WIDTH : (h + 1) * HEAD_WIDTH] = jnp.sum(
            jnp.where(scored, part.astype(jnp.float32), 0.0), axis=0, keepdims=True
        ).astype(jnp.bfloat16)
    picked_ref[0, :, width:] = jnp.sum(
        jnp.where(scored, residual_ref[...].astype(jnp.float32), 0.0), axis=0, keepdims=True
    ).astype(jnp.bfloat16)


def attention(query, keys, values, residual, cand_len):
    count = cand_len.shape[0]
    slots = query.shape[0] // count
    wide = pl.BlockSpec((slots, query.shape[1]), lambda c, n: (c, 0))
    narrow = pl.BlockSpec((slots, keys.shape[1]), lambda c, n: (c, 0))
    picked_width = query.shape[1] + residual.shape[1]
    out, picked = pl.pallas_call(
        attention_kernel,
        grid_spec=pltpu.PrefetchScalarGridSpec(
            num_scalar_prefetch=1,
            grid=(count,),
            in_specs=[wide, narrow, narrow, wide],
            out_specs=[wide, pl.BlockSpec((1, 1, picked_width), lambda c, n: (c, 0, 0))],
        ),
        out_shape=[
            jax.ShapeDtypeStruct(query.shape, jnp.bfloat16),
            jax.ShapeDtypeStruct((count, 1, picked_width), jnp.bfloat16),
        ],
        cost_estimate=pl.CostEstimate(
            flops=4 * query.size * slots,
            bytes_accessed=6 * query.size,
            transcendentals=query.size,
        ),
        name="attention",
    )(cand_len, query, keys, values, residual)
    return out, picked.reshape(count, picked_width)


def trunk_kernel(picks, has_base, place_ref, *refs):
    count = len(picks)
    sources, blocks = refs[:4], refs[4 : 4 + count]
    base_ref = refs[4 + count] if has_base else None
    out_ref, acts, sems = refs[-3:]
    j = pl.program_id(0)

    def copies(which):
        for r in range(CORE):
            for i, (s, v) in enumerate(picks):
                depth = acts.shape[3]
                group = lax.rem(place_ref[0] + 2 * Y - s - 2 * v, Y)
                yield pltpu.make_async_copy(
                    sources[2 * which + r].at[group, :, pl.ds(v * depth, depth)],
                    acts.at[r, i],
                    sems.at[r, i],
                )

    @pl.when(j == 0)
    def _():
        for which in range(2):

            @pl.when(place_ref[1] == which)
            def _():
                for copy in copies(which):
                    copy.start()

        for copy in copies(0):
            copy.wait()

    if has_base:
        total = base_ref[...]
    else:
        total = jnp.zeros(out_ref.shape, jnp.float32)
    r = j // 2
    for i, block in enumerate(blocks):
        total = total + jnp.dot(acts[r, i], block[...], preferred_element_type=jnp.float32)
    out_ref[...] = total.astype(out_ref.dtype)


def trunk_part(place, sources, terms, base, dtype):
    rows = sources[0].shape[1]
    depth = sources[0].shape[2] // 2
    width = terms[0][2].shape[-1]
    count = len(terms)

    def weight_spec(v, w):
        if w.ndim == 2:
            return pl.BlockSpec((depth, width // 2), lambda j, p: (0, lax.rem(j, 2)))
        return pl.BlockSpec((None, depth, width // 2), lambda j, p: (v, 0, lax.rem(j, 2)))

    tile = pl.BlockSpec((rows, width // 2), lambda j, p: (j // 2, lax.rem(j, 2)))
    return pl.pallas_call(
        functools.partial(trunk_kernel, [(s, v) for s, v, _ in terms], base is not None),
        grid_spec=pltpu.PrefetchScalarGridSpec(
            num_scalar_prefetch=1,
            grid=(2 * CORE,),
            in_specs=[pl.BlockSpec(memory_space=pltpu.HBM)] * 4
            + [weight_spec(v, w) for _, v, w in terms]
            + ([] if base is None else [tile]),
            out_specs=tile,
            scratch_shapes=[
                pltpu.VMEM((CORE, count, rows, depth), sources[0].dtype),
                pltpu.SemaphoreType.DMA((CORE, count)),
            ],
        ),
        out_shape=jax.ShapeDtypeStruct((CORE * rows, width), dtype),
        compiler_params=pltpu.CompilerParams(vmem_limit_bytes=32 * 2**20),
        cost_estimate=pl.CostEstimate(
            flops=CORE * rows * width, bytes_accessed=CORE * rows * width, transcendentals=0
        ),
        name="trunk_part",
    )(
        place,
        *[pltpu.with_memory_space_constraint(x, pltpu.HBM) for x in sources],
        *[t[2] for t in terms],
        *([] if base is None else [base]),
    )


def norm_kernel(place_ref, p0, p1, p2, p3, gain_ref, out_ref):
    pieces = (p0, p1, p2, p3)
    z = place_ref[0]
    group = p0.shape[1] // Z
    width = p0.shape[2]
    per_z = p0.shape[0]
    scales = []
    for r in range(Z):
        square = jnp.zeros((group, 1), jnp.float32)
        for s in range(Z):
            for q in range(per_z):
                rows = pieces[s][q, pl.ds(((r - s) % Z) * group, group), :].astype(jnp.float32)
                square = square + jnp.sum(rows * rows, axis=-1, keepdims=True)
        scales.append(lax.rsqrt(square / (Z * per_z * width) + 1e-05))
    for s in range(Z):
        for q in range(per_z):
            start = pl.multiple_of((lax.rem(z + s, Z) * per_z + q) * width, width)
            gain = gain_ref[:, pl.ds(start, width)]
            for r in range(Z):
                rows = pieces[s][q, pl.ds(((r - s) % Z) * group, group), :].astype(jnp.float32)
                out_ref[pl.ds(r * group, group), pl.ds(start, width)] = (
                    rows * scales[r] * gain
                ).astype(jnp.bfloat16)


def normalize(pieces, gain, z):
    per_z, rows, width = pieces[0].shape
    total = Z * per_z * width
    return pl.pallas_call(
        norm_kernel,
        in_specs=[pl.BlockSpec(memory_space=pltpu.SMEM)]
        + [pl.BlockSpec(memory_space=pltpu.VMEM)] * 5,
        out_specs=pl.BlockSpec(memory_space=pltpu.VMEM),
        out_shape=jax.ShapeDtypeStruct((rows, total), jnp.bfloat16),
        cost_estimate=pl.CostEstimate(
            flops=8 * rows * total, bytes_accessed=4 * rows * total, transcendentals=rows
        ),
        name="normalize",
    )(z[None], *pieces, gain[None, :])


def local(
    query,
    keys,
    values,
    residual,
    out_weight,
    norm_gain,
    cand_len,
    head_w1,
    head_b1,
    head_w2,
    head_b2,
    head_w3,
    head_b3,
):
    z = lax.axis_index("z")
    xl = lax.axis_index("xl")
    core = lax.axis_index("core")
    y = lax.axis_index("y")
    xh = lax.axis_index("xh")

    lock = lax.optimization_barrier
    rows_half = out_weight.shape[0] // 2
    moved = [
        lax.ppermute(out_weight[v * rows_half : (v + 1) * rows_half], ALL, spread_moves(v))
        for v in range(2)
    ]
    attn_out, picked = attention(query, keys, values, residual, cand_len)
    here = lax.all_gather(attn_out, "y", axis=0, tiled=False)

    depth = attn_out.shape[1]
    width = out_weight.shape[1]
    near = lax.all_gather(picked, ("xl", "core"), axis=0, tiled=True)
    near, *moved = lock((near, *moved))
    moved = [lax.ppermute(m, ALL, column_moves(v)) for v, m in enumerate(moved)]
    rows = jnp.concatenate([near] + [from_ahead(near, "z", Z, s) for s in (1, 2, 3)], axis=0)
    own = jnp.dot(rows[:, :depth], out_weight, preferred_element_type=jnp.float32)
    res = rows[:, depth:]
    res = jnp.where(core == 0, res[:, :width], res[:, width:]).astype(jnp.float32)
    own = jnp.where((y == z) & (xh == xl), own + res, own).astype(jnp.bfloat16)
    pair = jnp.stack([own, from_ahead(own, "xh", XH, 1)])
    pair, held, *moved = lock((pair, attn_out, *moved))
    w = {(0, 0): jnp.stack(moved)}
    w[1, 0] = from_ahead(w[0, 0], "z", Z, 1)
    w[3, 0] = from_ahead(w[0, 0], "z", Z, 3)
    across = from_ahead(held, "xh", XH, 1)
    parts = [pair] + [from_ahead(pair, "y", Y, s) for s in (1, 2, 3)]
    pooled = sum(jnp.sum(p.astype(jnp.float32), axis=0) for p in parts).astype(jnp.bfloat16)
    pooled, across = lock((pooled, across))
    there = lax.all_gather(across, "y", axis=0, tiled=False)
    near = lax.all_gather(pooled, ("xl", "core"), axis=0, tiled=False)
    near, w[1, 0], w[3, 0], w[0, 0], here = lock((near, w[1, 0], w[3, 0], w[0, 0], here))
    pieces = [near] + [from_ahead(near, "z", Z, s) for s in (1, 2, 3)]
    w[0, 1] = from_ahead(w[0, 0], "xl", XL, 1)
    *pieces, w[1, 0], w[3, 0] = lock((*pieces, w[1, 0], w[3, 0]))
    w[2, 0] = [from_ahead(w[1, 0][0], "z", Z, 1), from_ahead(w[3, 0][1], "z", Z, 3)]
    features = normalize(pieces, norm_gain, z)
    features, w[0, 1], here, *w[2, 0] = lock((features, w[0, 1], here, *w[2, 0]))
    w[1, 1] = from_ahead(w[0, 1], "z", Z, 1)
    w[3, 1] = from_ahead(w[0, 1], "z", Z, 3)
    here_other = from_ahead(here, "core", CORE, 1)
    first = jax.nn.silu(
        jnp.dot(features, head_w1[0], preferred_element_type=jnp.float32) + head_b1[0]
    ).astype(jnp.bfloat16)
    terms = jnp.dot(first, head_w2[0], preferred_element_type=jnp.float32).astype(jnp.bfloat16)
    count = terms.shape[0] // Y
    terms = lax.all_to_all(
        terms.reshape(Y, count, terms.shape[1]), "y", split_axis=0, concat_axis=0, tiled=True
    )
    terms, there, w[0, 1], w[1, 1], w[3, 1], here_other = lock(
        (terms, there, w[0, 1], w[1, 1], w[3, 1], here_other)
    )
    there_other = from_ahead(there, "core", CORE, 1)
    w[2, 1] = from_ahead(w[0, 1], "z", Z, 2)
    half = jnp.sum(terms.astype(jnp.float32), axis=0).astype(jnp.bfloat16)
    other = from_ahead(half, "xh", XH, 1)
    second = jax.nn.silu(half.astype(jnp.float32) + other.astype(jnp.float32) + head_b2[0])
    mine = jnp.sum(second * head_w3[0].astype(jnp.float32), axis=-1) + head_b3[0]
    scores = jnp.stack([mine] + [from_ahead(mine, "y", Y, s) for s in (1, 2, 3)])
    scores = jnp.roll(scores, lax.rem(y + z, Y), axis=0).reshape(1, Y * count)


    def product(e, trunk, dtype):
        items = [
            (s, v, w[s, e][v] if isinstance(w[s, e], list) else w[s, e])
            for s in range(Z)
            for v in range(2)
        ]
        place = jnp.stack([lax.rem(y - z + Y, Y), lax.rem(xl + e + xh, XH)])
        return trunk_part(place, sources, items, trunk, dtype)

    scores, there_other = lock((scores, there_other))
    sources = (here, here_other, there, there_other)
    trunk = product(0, None, jnp.float32)
    trunk = product(1, trunk, jnp.bfloat16)
    row_count = residual.shape[0]
    mine = trunk[:row_count]
    other = from_ahead(trunk[row_count:], "core", CORE, 1)
    left, right = jnp.where(core == 0, mine, other), jnp.where(core == 0, other, mine)
    trunk = jnp.concatenate([left, right], axis=1).astype(jnp.float32)
    trunk_out = (trunk + residual.astype(jnp.float32)).astype(jnp.bfloat16)
    return (trunk_out, scores)


def solution(mesh):
    fine = Mesh(mesh.devices.reshape(Z, XL, CORE, Y, XH), ALL)
    in_specs = (
        P(MEMBER, TENSOR),
        P(MEMBER, TENSOR),
        P(MEMBER, TENSOR),
        P(MEMBER, TENSOR),
        P(TENSOR, MEMBER),
        P(),
        P(MEMBER),
        P(MEMBER, None, TENSOR),
        P(MEMBER, TENSOR),
        P(MEMBER, TENSOR, None),
        P(MEMBER, None),
        P(MEMBER, None),
        P(MEMBER),
    )
    out_specs = (P(MEMBER, TENSOR), P(MEMBER, None))
    return jax.shard_map(local, mesh=fine, in_specs=in_specs, out_specs=out_specs, check_vma=False)
```

```python
import functools
import itertools

import jax
import jax.numpy as jnp
from jax import lax
from jax.experimental import pallas as pl
from jax.experimental.pallas import tpu as pltpu
from jax.sharding import Mesh, PartitionSpec as P

HEAD_WIDTH = 128
Z, XL, CORE, Y, XH = 4, 2, 2, 4, 2
MEMBER = ("z", "xl", "core")
TENSOR = ("y", "xh")
ALL = MEMBER + TENSOR


def flat(z, xl, core, y, xh):
    return (((z % Z) * XL + xl % XL) * CORE + core) * Y * XH + (y % Y) * XH + xh % XH


def places():
    return itertools.product(range(Z), range(XL), range(CORE), range(Y), range(XH))


def spread_moves(v):
    return [
        (flat(z, xl, core, y, xh), flat(z - y - 2 * v, xl, core, y, xh))
        for z, xl, core, y, xh in places()
    ]


def column_moves(v):
    return [
        (flat(z, xl, core, y, xh), flat(z, xh, core, y + z + 2 * v, xl))
        for z, xl, core, y, xh in places()
    ]


def from_ahead(x, axis, size, step):
    return lax.ppermute(x, axis, [(i, (i - step) % size) for i in range(size)])


def attention_kernel(len_ref, query_ref, keys_ref, values_ref, residual_ref, out_ref, picked_ref):
    length = len_ref[pl.program_id(0)]
    slots, width = query_ref.shape
    heads = width // HEAD_WIDTH
    queries = jnp.concatenate(
        [query_ref[:, h * HEAD_WIDTH : (h + 1) * HEAD_WIDTH] for h in range(heads)], axis=0
    )
    logits = lax.dot_general(
        queries, keys_ref[...], (((1,), (1,)), ((), ())), preferred_element_type=jnp.float32
    ) * HEAD_WIDTH ** (-0.5)
    row = lax.rem(lax.broadcasted_iota(jnp.int32, logits.shape, 0), slots)
    column = lax.broadcasted_iota(jnp.int32, logits.shape, 1)
    allowed = (row >= column) & (column < length)
    logits = jnp.where(allowed, logits, jnp.float32(-1e30))
    row_max = jnp.max(logits, axis=-1, keepdims=True)
    probs = jnp.where(allowed, jnp.exp(logits - row_max), jnp.float32(0.0))
    totals = jnp.sum(probs, axis=-1, keepdims=True)
    weights = (probs / totals).astype(jnp.bfloat16)
    result = jnp.dot(weights, values_ref[...], preferred_element_type=jnp.float32)
    result = result.astype(jnp.bfloat16)
    scored = lax.broadcasted_iota(jnp.int32, (slots, 1), 0) == length - 1
    for h in range(heads):
        part = result[h * slots : (h + 1) * slots]
        out_ref[:, h * HEAD_WIDTH : (h + 1) * HEAD_WIDTH] = part
        picked_ref[0, :, h * HEAD_WIDTH : (h + 1) * HEAD_WIDTH] = jnp.sum(
            jnp.where(scored, part.astype(jnp.float32), 0.0), axis=0, keepdims=True
        ).astype(jnp.bfloat16)
    picked_ref[0, :, width:] = jnp.sum(
        jnp.where(scored, residual_ref[...].astype(jnp.float32), 0.0), axis=0, keepdims=True
    ).astype(jnp.bfloat16)


def attention(query, keys, values, residual, cand_len):
    count = cand_len.shape[0]
    slots = query.shape[0] // count
    wide = pl.BlockSpec((slots, query.shape[1]), lambda c, n: (c, 0))
    narrow = pl.BlockSpec((slots, keys.shape[1]), lambda c, n: (c, 0))
    picked_width = query.shape[1] + residual.shape[1]
    out, picked = pl.pallas_call(
        attention_kernel,
        grid_spec=pltpu.PrefetchScalarGridSpec(
            num_scalar_prefetch=1,
            grid=(count,),
            in_specs=[wide, narrow, narrow, wide],
            out_specs=[wide, pl.BlockSpec((1, 1, picked_width), lambda c, n: (c, 0, 0))],
        ),
        out_shape=[
            jax.ShapeDtypeStruct(query.shape, jnp.bfloat16),
            jax.ShapeDtypeStruct((count, 1, picked_width), jnp.bfloat16),
        ],
        cost_estimate=pl.CostEstimate(
            flops=4 * query.size * slots,
            bytes_accessed=6 * query.size,
            transcendentals=query.size,
        ),
        name="attention",
    )(cand_len, query, keys, values, residual)
    return out, picked.reshape(count, picked_width)


def trunk_kernel(picks, has_base, place_ref, *refs):
    count = len(picks)
    sources, blocks = refs[:4], refs[4 : 4 + count]
    base_ref = refs[4 + count] if has_base else None
    out_ref, acts, sems = refs[-3:]
    j = pl.program_id(0)

    def copies(which):
        for r in range(CORE):
            for i, (s, v) in enumerate(picks):
                depth = acts.shape[3]
                group = lax.rem(place_ref[0] + 2 * Y - s - 2 * v, Y)
                yield pltpu.make_async_copy(
                    sources[2 * which + r].at[group, :, pl.ds(v * depth, depth)],
                    acts.at[r, i],
                    sems.at[r, i],
                )

    @pl.when(j == 0)
    def _():
        for which in range(2):

            @pl.when(place_ref[1] == which)
            def _():
                for copy in copies(which):
                    copy.start()

        for copy in copies(0):
            copy.wait()

    if has_base:
        total = base_ref[...]
    else:
        total = jnp.zeros(out_ref.shape, jnp.float32)
    r = j // 2
    for i, block in enumerate(blocks):
        total = total + jnp.dot(acts[r, i], block[...], preferred_element_type=jnp.float32)
    out_ref[...] = total.astype(out_ref.dtype)


def trunk_part(place, sources, terms, base, dtype):
    rows = sources[0].shape[1]
    depth = sources[0].shape[2] // 2
    width = terms[0][2].shape[-1]
    count = len(terms)

    def weight_spec(v, w):
        if w.ndim == 2:
            return pl.BlockSpec((depth, width // 2), lambda j, p: (0, lax.rem(j, 2)))
        return pl.BlockSpec((None, depth, width // 2), lambda j, p: (v, 0, lax.rem(j, 2)))

    tile = pl.BlockSpec((rows, width // 2), lambda j, p: (j // 2, lax.rem(j, 2)))
    return pl.pallas_call(
        functools.partial(trunk_kernel, [(s, v) for s, v, _ in terms], base is not None),
        grid_spec=pltpu.PrefetchScalarGridSpec(
            num_scalar_prefetch=1,
            grid=(2 * CORE,),
            in_specs=[pl.BlockSpec(memory_space=pltpu.HBM)] * 4
            + [weight_spec(v, w) for _, v, w in terms]
            + ([] if base is None else [tile]),
            out_specs=tile,
            scratch_shapes=[
                pltpu.VMEM((CORE, count, rows, depth), sources[0].dtype),
                pltpu.SemaphoreType.DMA((CORE, count)),
            ],
        ),
        out_shape=jax.ShapeDtypeStruct((CORE * rows, width), dtype),
        compiler_params=pltpu.CompilerParams(vmem_limit_bytes=32 * 2**20),
        cost_estimate=pl.CostEstimate(
            flops=CORE * rows * width, bytes_accessed=CORE * rows * width, transcendentals=0
        ),
        name="trunk_part",
    )(
        place,
        *[pltpu.with_memory_space_constraint(x, pltpu.HBM) for x in sources],
        *[t[2] for t in terms],
        *([] if base is None else [base]),
    )


def norm_kernel(place_ref, p0, p1, p2, p3, gain_ref, out_ref):
    pieces = (p0, p1, p2, p3)
    z = place_ref[0]
    group = p0.shape[1] // Z
    width = p0.shape[2]
    per_z = p0.shape[0]
    scales = []
    for r in range(Z):
        square = jnp.zeros((group, 1), jnp.float32)
        for s in range(Z):
            for q in range(per_z):
                rows = pieces[s][q, pl.ds(((r - s) % Z) * group, group), :].astype(jnp.float32)
                square = square + jnp.sum(rows * rows, axis=-1, keepdims=True)
        scales.append(lax.rsqrt(square / (Z * per_z * width) + 1e-05))
    for s in range(Z):
        for q in range(per_z):
            start = pl.multiple_of((lax.rem(z + s, Z) * per_z + q) * width, width)
            gain = gain_ref[:, pl.ds(start, width)]
            for r in range(Z):
                rows = pieces[s][q, pl.ds(((r - s) % Z) * group, group), :].astype(jnp.float32)
                out_ref[pl.ds(r * group, group), pl.ds(start, width)] = (
                    rows * scales[r] * gain
                ).astype(jnp.bfloat16)


def normalize(pieces, gain, z):
    per_z, rows, width = pieces[0].shape
    total = Z * per_z * width
    return pl.pallas_call(
        norm_kernel,
        in_specs=[pl.BlockSpec(memory_space=pltpu.SMEM)]
        + [pl.BlockSpec(memory_space=pltpu.VMEM)] * 5,
        out_specs=pl.BlockSpec(memory_space=pltpu.VMEM),
        out_shape=jax.ShapeDtypeStruct((rows, total), jnp.bfloat16),
        cost_estimate=pl.CostEstimate(
            flops=8 * rows * total, bytes_accessed=4 * rows * total, transcendentals=rows
        ),
        name="normalize",
    )(z[None], *pieces, gain[None, :])


def local(
    query,
    keys,
    values,
    residual,
    out_weight,
    norm_gain,
    cand_len,
    head_w1,
    head_b1,
    head_w2,
    head_b2,
    head_w3,
    head_b3,
):
    z = lax.axis_index("z")
    xl = lax.axis_index("xl")
    core = lax.axis_index("core")
    y = lax.axis_index("y")
    xh = lax.axis_index("xh")

    lock = lax.optimization_barrier
    rows_half = out_weight.shape[0] // 2
    moved = [
        lax.ppermute(out_weight[v * rows_half : (v + 1) * rows_half], ALL, spread_moves(v))
        for v in range(2)
    ]
    attn_out, picked = attention(query, keys, values, residual, cand_len)
    here = lax.all_gather(attn_out, "y", axis=0, tiled=False)

    depth = attn_out.shape[1]
    width = out_weight.shape[1]
    near = lax.all_gather(picked, ("xl", "core"), axis=0, tiled=True)
    near, *moved = lock((near, *moved))
    moved = [lax.ppermute(m, ALL, column_moves(v)) for v, m in enumerate(moved)]
    rows = jnp.concatenate([near] + [from_ahead(near, "z", Z, s) for s in (1, 2, 3)], axis=0)
    rows, *moved = lock((rows, *moved))
    w = {(0, 0): jnp.stack(moved)}
    w[1, 0] = from_ahead(w[0, 0], "z", Z, 1)
    w[3, 0] = from_ahead(w[0, 0], "z", Z, 3)
    own = jnp.dot(rows[:, :depth], out_weight, preferred_element_type=jnp.float32)
    res = rows[:, depth:]
    res = jnp.where(core == 0, res[:, :width], res[:, width:]).astype(jnp.float32)
    own = jnp.where((y == z) & (xh == xl), own + res, own).astype(jnp.bfloat16)
    pair = jnp.stack([own, from_ahead(own, "xh", XH, 1)])
    pair, held = lock((pair, attn_out))
    across = from_ahead(held, "xh", XH, 1)
    parts = [pair] + [from_ahead(pair, "y", Y, s) for s in (1, 2, 3)]
    pooled = sum(jnp.sum(p.astype(jnp.float32), axis=0) for p in parts).astype(jnp.bfloat16)
    pooled, across = lock((pooled, across))
    there = lax.all_gather(across, "y", axis=0, tiled=False)
    near = lax.all_gather(pooled, ("xl", "core"), axis=0, tiled=False)
    near, w[1, 0], w[3, 0], w[0, 0], here = lock((near, w[1, 0], w[3, 0], w[0, 0], here))
    pieces = [near] + [from_ahead(near, "z", Z, s) for s in (1, 2, 3)]
    w[0, 1] = from_ahead(w[0, 0], "xl", XL, 1)
    *pieces, w[1, 0], w[3, 0] = lock((*pieces, w[1, 0], w[3, 0]))
    w[2, 0] = [from_ahead(w[1, 0][0], "z", Z, 1), from_ahead(w[3, 0][1], "z", Z, 3)]
    features = normalize(pieces, norm_gain, z)
    features, w[0, 1], here = lock((features, w[0, 1], here))
    w[1, 1] = from_ahead(w[0, 1], "z", Z, 1)
    w[3, 1] = from_ahead(w[0, 1], "z", Z, 3)
    here_other = from_ahead(here, "core", CORE, 1)
    first = jax.nn.silu(
        jnp.dot(features, head_w1[0], preferred_element_type=jnp.float32) + head_b1[0]
    ).astype(jnp.bfloat16)
    terms = jnp.dot(first, head_w2[0], preferred_element_type=jnp.float32).astype(jnp.bfloat16)
    count = terms.shape[0] // Y
    terms = lax.all_to_all(
        terms.reshape(Y, count, terms.shape[1]), "y", split_axis=0, concat_axis=0, tiled=True
    )
    terms, there, w[0, 1], w[1, 1], w[3, 1], here_other, *w[2, 0] = lock(
        (terms, there, w[0, 1], w[1, 1], w[3, 1], here_other, *w[2, 0])
    )
    there_other = from_ahead(there, "core", CORE, 1)
    w[2, 1] = from_ahead(w[0, 1], "z", Z, 2)
    half = jnp.sum(terms.astype(jnp.float32), axis=0).astype(jnp.bfloat16)
    other = from_ahead(half, "xh", XH, 1)
    second = jax.nn.silu(half.astype(jnp.float32) + other.astype(jnp.float32) + head_b2[0])
    mine = jnp.sum(second * head_w3[0].astype(jnp.float32), axis=-1) + head_b3[0]

    def product(e, trunk, dtype):
        items = [
            (s, v, w[s, e][v] if isinstance(w[s, e], list) else w[s, e])
            for s in range(Z)
            for v in range(2)
        ]
        place = jnp.stack([lax.rem(y - z + Y, Y), lax.rem(xl + e + xh, XH)])
        return trunk_part(place, sources, items, trunk, dtype)

    sources = (here, here_other, there, there_other)
    trunk = product(0, None, jnp.float32)
    scores = [mine] + [from_ahead(mine, "y", Y, s) for s in (1, 2, 3)]
    *scores, trunk = lock((*scores, trunk))
    scores = jnp.roll(jnp.stack(scores), lax.rem(y + z, Y), axis=0).reshape(1, Y * count)
    trunk = product(1, trunk, jnp.bfloat16)
    row_count = residual.shape[0]
    mine = trunk[:row_count]
    other = from_ahead(trunk[row_count:], "core", CORE, 1)
    left, right = jnp.where(core == 0, mine, other), jnp.where(core == 0, other, mine)
    trunk = jnp.concatenate([left, right], axis=1).astype(jnp.float32)
    trunk_out = (trunk + residual.astype(jnp.float32)).astype(jnp.bfloat16)
    return (trunk_out, scores)


def solution(mesh):
    fine = Mesh(mesh.devices.reshape(Z, XL, CORE, Y, XH), ALL)
    in_specs = (
        P(MEMBER, TENSOR),
        P(MEMBER, TENSOR),
        P(MEMBER, TENSOR),
        P(MEMBER, TENSOR),
        P(TENSOR, MEMBER),
        P(),
        P(MEMBER),
        P(MEMBER, None, TENSOR),
        P(MEMBER, TENSOR),
        P(MEMBER, TENSOR, None),
        P(MEMBER, None),
        P(MEMBER, None),
        P(MEMBER),
    )
    out_specs = (P(MEMBER, TENSOR), P(MEMBER, None))
    return jax.shard_map(local, mesh=fine, in_specs=in_specs, out_specs=out_specs, check_vma=False)
```

```python
import functools
import itertools

import jax
import jax.numpy as jnp
from jax import lax
from jax.experimental import pallas as pl
from jax.experimental.pallas import tpu as pltpu
from jax.sharding import Mesh, PartitionSpec as P

HEAD_WIDTH = 128
Z, XL, CORE, Y, XH = 4, 2, 2, 4, 2
MEMBER = ("z", "xl", "core")
TENSOR = ("y", "xh")
ALL = MEMBER + TENSOR


def flat(z, xl, core, y, xh):
    return (((z % Z) * XL + xl % XL) * CORE + core) * Y * XH + (y % Y) * XH + xh % XH


def places():
    return itertools.product(range(Z), range(XL), range(CORE), range(Y), range(XH))


def spread_moves(v):
    return [
        (flat(z, xl, core, y, xh), flat(z - y - 2 * v, xl, core, y, xh))
        for z, xl, core, y, xh in places()
    ]


def column_moves(v):
    return [
        (flat(z, xl, core, y, xh), flat(z, xh, core, y + z + 2 * v, xl))
        for z, xl, core, y, xh in places()
    ]


def from_ahead(x, axis, size, step):
    return lax.ppermute(x, axis, [(i, (i - step) % size) for i in range(size)])


def attention_kernel(len_ref, query_ref, keys_ref, values_ref, residual_ref, out_ref, picked_ref):
    length = len_ref[pl.program_id(0)]
    slots, width = query_ref.shape
    heads = width // HEAD_WIDTH
    queries = jnp.concatenate(
        [query_ref[:, h * HEAD_WIDTH : (h + 1) * HEAD_WIDTH] for h in range(heads)], axis=0
    )
    logits = lax.dot_general(
        queries, keys_ref[...], (((1,), (1,)), ((), ())), preferred_element_type=jnp.float32
    ) * HEAD_WIDTH ** (-0.5)
    row = lax.rem(lax.broadcasted_iota(jnp.int32, logits.shape, 0), slots)
    column = lax.broadcasted_iota(jnp.int32, logits.shape, 1)
    allowed = (row >= column) & (column < length)
    logits = jnp.where(allowed, logits, jnp.float32(-1e30))
    row_max = jnp.max(logits, axis=-1, keepdims=True)
    probs = jnp.where(allowed, jnp.exp(logits - row_max), jnp.float32(0.0))
    totals = jnp.sum(probs, axis=-1, keepdims=True)
    weights = (probs / totals).astype(jnp.bfloat16)
    result = jnp.dot(weights, values_ref[...], preferred_element_type=jnp.float32)
    result = result.astype(jnp.bfloat16)
    scored = lax.broadcasted_iota(jnp.int32, (slots, 1), 0) == length - 1
    for h in range(heads):
        part = result[h * slots : (h + 1) * slots]
        out_ref[:, h * HEAD_WIDTH : (h + 1) * HEAD_WIDTH] = part
        picked_ref[0, :, h * HEAD_WIDTH : (h + 1) * HEAD_WIDTH] = jnp.sum(
            jnp.where(scored, part.astype(jnp.float32), 0.0), axis=0, keepdims=True
        ).astype(jnp.bfloat16)
    picked_ref[0, :, width:] = jnp.sum(
        jnp.where(scored, residual_ref[...].astype(jnp.float32), 0.0), axis=0, keepdims=True
    ).astype(jnp.bfloat16)


def attention(query, keys, values, residual, cand_len):
    count = cand_len.shape[0]
    slots = query.shape[0] // count
    wide = pl.BlockSpec((slots, query.shape[1]), lambda c, n: (c, 0))
    narrow = pl.BlockSpec((slots, keys.shape[1]), lambda c, n: (c, 0))
    picked_width = query.shape[1] + residual.shape[1]
    out, picked = pl.pallas_call(
        attention_kernel,
        grid_spec=pltpu.PrefetchScalarGridSpec(
            num_scalar_prefetch=1,
            grid=(count,),
            in_specs=[wide, narrow, narrow, wide],
            out_specs=[wide, pl.BlockSpec((1, 1, picked_width), lambda c, n: (c, 0, 0))],
        ),
        out_shape=[
            jax.ShapeDtypeStruct(query.shape, jnp.bfloat16),
            jax.ShapeDtypeStruct((count, 1, picked_width), jnp.bfloat16),
        ],
        cost_estimate=pl.CostEstimate(
            flops=4 * query.size * slots,
            bytes_accessed=6 * query.size,
            transcendentals=query.size,
        ),
        name="attention",
    )(cand_len, query, keys, values, residual)
    return out, picked.reshape(count, picked_width)


def trunk_kernel(picks, has_base, place_ref, *refs):
    count = len(picks)
    sources, blocks = refs[:4], refs[4 : 4 + count]
    base_ref = refs[4 + count] if has_base else None
    out_ref, acts, sems = refs[-3:]
    j = pl.program_id(0)

    depth = acts.shape[2] // count

    def copies(which, r):
        for i, (s, v) in enumerate(picks):
            group = lax.rem(place_ref[0] + 2 * Y - s - 2 * v, Y)
            yield pltpu.make_async_copy(
                sources[2 * which + r].at[group, :, pl.ds(v * depth, depth)],
                acts.at[r, :, pl.ds(i * depth, depth)],
                sems.at[r, i],
            )

    @pl.when(j == 0)
    def _():
        for which in range(2):

            @pl.when(place_ref[1] == which)
            def _():
                for r in range(CORE):
                    for copy in copies(which, r):
                        copy.start()

    for r in range(CORE):

        @pl.when(j == 2 * r)
        def _():
            for copy in copies(0, r):
                copy.wait()

    total = jnp.dot(
        acts[j // 2],
        jnp.concatenate([block[...] for block in blocks], axis=0),
        preferred_element_type=jnp.float32,
    )
    if has_base:
        total = total + base_ref[...]
    out_ref[...] = total.astype(out_ref.dtype)


def trunk_part(place, sources, terms, base, dtype):
    rows = sources[0].shape[1]
    depth = sources[0].shape[2] // 2
    width = terms[0][2].shape[-1]
    count = len(terms)

    def weight_spec(v, w):
        if w.ndim == 2:
            return pl.BlockSpec((depth, width // 2), lambda j, p: (0, lax.rem(j, 2)))
        return pl.BlockSpec((None, depth, width // 2), lambda j, p: (v, 0, lax.rem(j, 2)))

    tile = pl.BlockSpec((rows, width // 2), lambda j, p: (j // 2, lax.rem(j, 2)))
    return pl.pallas_call(
        functools.partial(trunk_kernel, [(s, v) for s, v, _ in terms], base is not None),
        grid_spec=pltpu.PrefetchScalarGridSpec(
            num_scalar_prefetch=1,
            grid=(2 * CORE,),
            in_specs=[pl.BlockSpec(memory_space=pltpu.HBM)] * 4
            + [weight_spec(v, w) for _, v, w in terms]
            + ([] if base is None else [tile]),
            out_specs=tile,
            scratch_shapes=[
                pltpu.VMEM((CORE, rows, count * depth), sources[0].dtype),
                pltpu.SemaphoreType.DMA((CORE, count)),
            ],
        ),
        out_shape=jax.ShapeDtypeStruct((CORE * rows, width), dtype),
        compiler_params=pltpu.CompilerParams(vmem_limit_bytes=32 * 2**20),
        cost_estimate=pl.CostEstimate(
            flops=CORE * rows * width, bytes_accessed=CORE * rows * width, transcendentals=0
        ),
        name="trunk_part",
    )(
        place,
        *[pltpu.with_memory_space_constraint(x, pltpu.HBM) for x in sources],
        *[t[2] for t in terms],
        *([] if base is None else [base]),
    )


def norm_kernel(place_ref, p0, p1, p2, p3, gain_ref, out_ref):
    pieces = (p0, p1, p2, p3)
    z = place_ref[0]
    group = p0.shape[1] // Z
    width = p0.shape[2]
    per_z = p0.shape[0]
    scales = []
    for r in range(Z):
        square = jnp.zeros((group, 1), jnp.float32)
        for s in range(Z):
            for q in range(per_z):
                rows = pieces[s][q, pl.ds(((r - s) % Z) * group, group), :].astype(jnp.float32)
                square = square + jnp.sum(rows * rows, axis=-1, keepdims=True)
        scales.append(lax.rsqrt(square / (Z * per_z * width) + 1e-05))
    for s in range(Z):
        for q in range(per_z):
            start = pl.multiple_of((lax.rem(z + s, Z) * per_z + q) * width, width)
            gain = gain_ref[:, pl.ds(start, width)]
            for r in range(Z):
                rows = pieces[s][q, pl.ds(((r - s) % Z) * group, group), :].astype(jnp.float32)
                out_ref[pl.ds(r * group, group), pl.ds(start, width)] = (
                    rows * scales[r] * gain
                ).astype(jnp.bfloat16)


def normalize(pieces, gain, z):
    per_z, rows, width = pieces[0].shape
    total = Z * per_z * width
    return pl.pallas_call(
        norm_kernel,
        in_specs=[pl.BlockSpec(memory_space=pltpu.SMEM)]
        + [pl.BlockSpec(memory_space=pltpu.VMEM)] * 5,
        out_specs=pl.BlockSpec(memory_space=pltpu.VMEM),
        out_shape=jax.ShapeDtypeStruct((rows, total), jnp.bfloat16),
        cost_estimate=pl.CostEstimate(
            flops=8 * rows * total, bytes_accessed=4 * rows * total, transcendentals=rows
        ),
        name="normalize",
    )(z[None], *pieces, gain[None, :])


def local(
    query,
    keys,
    values,
    residual,
    out_weight,
    norm_gain,
    cand_len,
    head_w1,
    head_b1,
    head_w2,
    head_b2,
    head_w3,
    head_b3,
):
    z = lax.axis_index("z")
    xl = lax.axis_index("xl")
    core = lax.axis_index("core")
    y = lax.axis_index("y")
    xh = lax.axis_index("xh")

    lock = lax.optimization_barrier
    rows_half = out_weight.shape[0] // 2
    moved = [
        lax.ppermute(out_weight[v * rows_half : (v + 1) * rows_half], ALL, spread_moves(v))
        for v in range(2)
    ]
    attn_out, picked = attention(query, keys, values, residual, cand_len)
    here = lax.all_gather(attn_out, "y", axis=0, tiled=False)

    depth = attn_out.shape[1]
    width = out_weight.shape[1]
    near = lax.all_gather(picked, ("xl", "core"), axis=0, tiled=True)
    near, *moved = lock((near, *moved))
    moved = [lax.ppermute(m, ALL, column_moves(v)) for v, m in enumerate(moved)]
    rows = jnp.concatenate([near] + [from_ahead(near, "z", Z, s) for s in (1, 2, 3)], axis=0)
    own = jnp.dot(rows[:, :depth], out_weight, preferred_element_type=jnp.float32)
    res = rows[:, depth:]
    res = jnp.where(core == 0, res[:, :width], res[:, width:]).astype(jnp.float32)
    own = jnp.where((y == z) & (xh == xl), own + res, own).astype(jnp.bfloat16)
    pair = jnp.stack([own, from_ahead(own, "xh", XH, 1)])
    pair, held, *moved = lock((pair, attn_out, *moved))
    w = {(0, 0): jnp.stack(moved)}
    w[1, 0] = from_ahead(w[0, 0], "z", Z, 1)
    w[3, 0] = from_ahead(w[0, 0], "z", Z, 3)
    across = from_ahead(held, "xh", XH, 1)
    parts = [pair] + [from_ahead(pair, "y", Y, s) for s in (1, 2, 3)]
    pooled = sum(jnp.sum(p.astype(jnp.float32), axis=0) for p in parts).astype(jnp.bfloat16)
    pooled, across = lock((pooled, across))
    there = lax.all_gather(across, "y", axis=0, tiled=False)
    near = lax.all_gather(pooled, ("xl", "core"), axis=0, tiled=False)
    near, w[1, 0], w[3, 0], w[0, 0], here = lock((near, w[1, 0], w[3, 0], w[0, 0], here))
    pieces = [near] + [from_ahead(near, "z", Z, s) for s in (1, 2, 3)]
    w[0, 1] = from_ahead(w[0, 0], "xl", XL, 1)
    *pieces, w[1, 0], w[3, 0] = lock((*pieces, w[1, 0], w[3, 0]))
    w[2, 0] = [from_ahead(w[1, 0][0], "z", Z, 1), from_ahead(w[3, 0][1], "z", Z, 3)]
    features = normalize(pieces, norm_gain, z)
    features, w[0, 1], here, *w[2, 0] = lock((features, w[0, 1], here, *w[2, 0]))
    w[1, 1] = from_ahead(w[0, 1], "z", Z, 1)
    w[3, 1] = from_ahead(w[0, 1], "z", Z, 3)
    here_other = from_ahead(here, "core", CORE, 1)
    first = jax.nn.silu(
        jnp.dot(features, head_w1[0], preferred_element_type=jnp.float32) + head_b1[0]
    ).astype(jnp.bfloat16)
    terms = jnp.dot(first, head_w2[0], preferred_element_type=jnp.float32).astype(jnp.bfloat16)
    count = terms.shape[0] // Y
    terms = lax.all_to_all(
        terms.reshape(Y, count, terms.shape[1]), "y", split_axis=0, concat_axis=0, tiled=True
    )
    terms, there, w[0, 1], w[1, 1], w[3, 1], here_other = lock(
        (terms, there, w[0, 1], w[1, 1], w[3, 1], here_other)
    )
    there_other = from_ahead(there, "core", CORE, 1)
    w[2, 1] = from_ahead(w[0, 1], "z", Z, 2)
    half = jnp.sum(terms.astype(jnp.float32), axis=0).astype(jnp.bfloat16)
    other = from_ahead(half, "xh", XH, 1)
    second = jax.nn.silu(half.astype(jnp.float32) + other.astype(jnp.float32) + head_b2[0])
    mine = jnp.sum(second * head_w3[0].astype(jnp.float32), axis=-1) + head_b3[0]

    def product(e, steps, trunk, dtype):
        items = [
            (s, v, w[s, e][v] if isinstance(w[s, e], list) else w[s, e])
            for s in steps
            for v in range(2)
        ]
        place = jnp.stack([lax.rem(y - z + Y, Y), lax.rem(xl + e + xh, XH)])
        return trunk_part(place, sources, items, trunk, dtype)

    sources = (here, here_other, there, there_other)
    trunk = product(0, range(Z), None, jnp.float32)
    scores = [mine] + [from_ahead(mine, "y", Y, s) for s in (1, 2, 3)]
    *scores, trunk = lock((*scores, trunk))
    scores = jnp.roll(jnp.stack(scores), lax.rem(y + z, Y), axis=0).reshape(1, Y * count)
    trunk = product(1, (0, 1, 3), trunk, jnp.float32)
    trunk = product(1, (2,), trunk, jnp.bfloat16)
    row_count = residual.shape[0]
    mine = trunk[:row_count]
    other = from_ahead(trunk[row_count:], "core", CORE, 1)
    left, right = jnp.where(core == 0, mine, other), jnp.where(core == 0, other, mine)
    trunk = jnp.concatenate([left, right], axis=1).astype(jnp.float32)
    trunk_out = (trunk + residual.astype(jnp.float32)).astype(jnp.bfloat16)
    return (trunk_out, scores)


def solution(mesh):
    fine = Mesh(mesh.devices.reshape(Z, XL, CORE, Y, XH), ALL)
    in_specs = (
        P(MEMBER, TENSOR),
        P(MEMBER, TENSOR),
        P(MEMBER, TENSOR),
        P(MEMBER, TENSOR),
        P(TENSOR, MEMBER),
        P(),
        P(MEMBER),
        P(MEMBER, None, TENSOR),
        P(MEMBER, TENSOR),
        P(MEMBER, TENSOR, None),
        P(MEMBER, None),
        P(MEMBER, None),
        P(MEMBER),
    )
    out_specs = (P(MEMBER, TENSOR), P(MEMBER, None))
    return jax.shard_map(local, mesh=fine, in_specs=in_specs, out_specs=out_specs, check_vma=False)
```

```python
import functools
import itertools

import jax
import jax.numpy as jnp
from jax import lax
from jax.experimental import pallas as pl
from jax.experimental.pallas import tpu as pltpu
from jax.sharding import Mesh, PartitionSpec as P

HEAD_WIDTH = 128
Z, XL, CORE, Y, XH = 4, 2, 2, 4, 2
MEMBER = ("z", "xl", "core")
TENSOR = ("y", "xh")
ALL = MEMBER + TENSOR


def flat(z, xl, core, y, xh):
    return (((z % Z) * XL + xl % XL) * CORE + core) * Y * XH + (y % Y) * XH + xh % XH


def places():
    return itertools.product(range(Z), range(XL), range(CORE), range(Y), range(XH))


def spread_moves(v):
    return [
        (flat(z, xl, core, y, xh), flat(z - y - 2 * v, xl, core, y, xh))
        for z, xl, core, y, xh in places()
    ]


def column_moves(v):
    return [
        (flat(z, xl, core, y, xh), flat(z, xh, core, y + z + 2 * v, xl))
        for z, xl, core, y, xh in places()
    ]


def from_ahead(x, axis, size, step):
    return lax.ppermute(x, axis, [(i, (i - step) % size) for i in range(size)])


def attention_kernel(len_ref, query_ref, keys_ref, values_ref, residual_ref, out_ref, picked_ref):
    length = len_ref[pl.program_id(0)]
    slots, width = query_ref.shape
    heads = width // HEAD_WIDTH
    queries = jnp.concatenate(
        [query_ref[:, h * HEAD_WIDTH : (h + 1) * HEAD_WIDTH] for h in range(heads)], axis=0
    )
    logits = lax.dot_general(
        queries, keys_ref[...], (((1,), (1,)), ((), ())), preferred_element_type=jnp.float32
    ) * HEAD_WIDTH ** (-0.5)
    row = lax.rem(lax.broadcasted_iota(jnp.int32, logits.shape, 0), slots)
    column = lax.broadcasted_iota(jnp.int32, logits.shape, 1)
    allowed = (row >= column) & (column < length)
    logits = jnp.where(allowed, logits, jnp.float32(-1e30))
    row_max = jnp.max(logits, axis=-1, keepdims=True)
    probs = jnp.where(allowed, jnp.exp(logits - row_max), jnp.float32(0.0))
    totals = jnp.sum(probs, axis=-1, keepdims=True)
    weights = (probs / totals).astype(jnp.bfloat16)
    result = jnp.dot(weights, values_ref[...], preferred_element_type=jnp.float32)
    result = result.astype(jnp.bfloat16)
    scored = lax.broadcasted_iota(jnp.int32, (slots, 1), 0) == length - 1
    for h in range(heads):
        part = result[h * slots : (h + 1) * slots]
        out_ref[:, h * HEAD_WIDTH : (h + 1) * HEAD_WIDTH] = part
        picked_ref[0, :, h * HEAD_WIDTH : (h + 1) * HEAD_WIDTH] = jnp.sum(
            jnp.where(scored, part.astype(jnp.float32), 0.0), axis=0, keepdims=True
        ).astype(jnp.bfloat16)
    picked_ref[0, :, width:] = jnp.sum(
        jnp.where(scored, residual_ref[...].astype(jnp.float32), 0.0), axis=0, keepdims=True
    ).astype(jnp.bfloat16)


def attention(query, keys, values, residual, cand_len):
    count = cand_len.shape[0]
    slots = query.shape[0] // count
    wide = pl.BlockSpec((slots, query.shape[1]), lambda c, n: (c, 0))
    narrow = pl.BlockSpec((slots, keys.shape[1]), lambda c, n: (c, 0))
    picked_width = query.shape[1] + residual.shape[1]
    out, picked = pl.pallas_call(
        attention_kernel,
        grid_spec=pltpu.PrefetchScalarGridSpec(
            num_scalar_prefetch=1,
            grid=(count,),
            in_specs=[wide, narrow, narrow, wide],
            out_specs=[wide, pl.BlockSpec((1, 1, picked_width), lambda c, n: (c, 0, 0))],
        ),
        out_shape=[
            jax.ShapeDtypeStruct(query.shape, jnp.bfloat16),
            jax.ShapeDtypeStruct((count, 1, picked_width), jnp.bfloat16),
        ],
        cost_estimate=pl.CostEstimate(
            flops=4 * query.size * slots,
            bytes_accessed=6 * query.size,
            transcendentals=query.size,
        ),
        name="attention",
    )(cand_len, query, keys, values, residual)
    return out, picked.reshape(count, picked_width)


def trunk_kernel(picks, has_base, place_ref, *refs):
    count = len(picks)
    sources, blocks = refs[:4], refs[4 : 4 + count]
    base_ref = refs[4 + count] if has_base else None
    out_ref, acts, sems = refs[-3:]
    j = pl.program_id(0)

    depth = acts.shape[2] // count

    def copies(which, r):
        for i, (s, v) in enumerate(picks):
            group = lax.rem(place_ref[0] + 2 * Y - s - 2 * v, Y)
            yield pltpu.make_async_copy(
                sources[2 * which + r].at[group, :, pl.ds(v * depth, depth)],
                acts.at[r, :, pl.ds(i * depth, depth)],
                sems.at[r, i],
            )

    @pl.when(j == 0)
    def _():
        for which in range(2):

            @pl.when(place_ref[1] == which)
            def _():
                for r in range(CORE):
                    for copy in copies(which, r):
                        copy.start()

    for r in range(CORE):

        @pl.when(j == 2 * r)
        def _():
            for copy in copies(0, r):
                copy.wait()

    total = jnp.dot(
        acts[j // 2],
        jnp.concatenate([block[...] for block in blocks], axis=0),
        preferred_element_type=jnp.float32,
    )
    if has_base:
        total = total + base_ref[...]
    out_ref[...] = total.astype(out_ref.dtype)


def trunk_part(place, sources, terms, base, dtype):
    rows = sources[0].shape[1]
    depth = sources[0].shape[2] // 2
    width = terms[0][2].shape[-1]
    count = len(terms)

    def weight_spec(v, w):
        if w.ndim == 2:
            return pl.BlockSpec((depth, width // 2), lambda j, p: (0, lax.rem(j, 2)))
        return pl.BlockSpec((None, depth, width // 2), lambda j, p: (v, 0, lax.rem(j, 2)))

    tile = pl.BlockSpec((rows, width // 2), lambda j, p: (j // 2, lax.rem(j, 2)))
    return pl.pallas_call(
        functools.partial(trunk_kernel, [(s, v) for s, v, _ in terms], base is not None),
        grid_spec=pltpu.PrefetchScalarGridSpec(
            num_scalar_prefetch=1,
            grid=(2 * CORE,),
            in_specs=[pl.BlockSpec(memory_space=pltpu.HBM)] * 4
            + [weight_spec(v, w) for _, v, w in terms]
            + ([] if base is None else [tile]),
            out_specs=tile,
            scratch_shapes=[
                pltpu.VMEM((CORE, rows, count * depth), sources[0].dtype),
                pltpu.SemaphoreType.DMA((CORE, count)),
            ],
        ),
        out_shape=jax.ShapeDtypeStruct((CORE * rows, width), dtype),
        compiler_params=pltpu.CompilerParams(vmem_limit_bytes=32 * 2**20),
        cost_estimate=pl.CostEstimate(
            flops=CORE * rows * width, bytes_accessed=CORE * rows * width, transcendentals=0
        ),
        name="trunk_part",
    )(
        place,
        *[pltpu.with_memory_space_constraint(x, pltpu.HBM) for x in sources],
        *[t[2] for t in terms],
        *([] if base is None else [base]),
    )


def norm_kernel(place_ref, p0, p1, p2, p3, gain_ref, out_ref):
    pieces = (p0, p1, p2, p3)
    z = place_ref[0]
    group = p0.shape[1] // Z
    width = p0.shape[2]
    per_z = p0.shape[0]
    scales = []
    for r in range(Z):
        square = jnp.zeros((group, 1), jnp.float32)
        for s in range(Z):
            for q in range(per_z):
                rows = pieces[s][q, pl.ds(((r - s) % Z) * group, group), :].astype(jnp.float32)
                square = square + jnp.sum(rows * rows, axis=-1, keepdims=True)
        scales.append(lax.rsqrt(square / (Z * per_z * width) + 1e-05))
    for s in range(Z):
        for q in range(per_z):
            start = pl.multiple_of((lax.rem(z + s, Z) * per_z + q) * width, width)
            gain = gain_ref[:, pl.ds(start, width)]
            for r in range(Z):
                rows = pieces[s][q, pl.ds(((r - s) % Z) * group, group), :].astype(jnp.float32)
                out_ref[pl.ds(r * group, group), pl.ds(start, width)] = (
                    rows * scales[r] * gain
                ).astype(jnp.bfloat16)


def normalize(pieces, gain, z):
    per_z, rows, width = pieces[0].shape
    total = Z * per_z * width
    return pl.pallas_call(
        norm_kernel,
        in_specs=[pl.BlockSpec(memory_space=pltpu.SMEM)]
        + [pl.BlockSpec(memory_space=pltpu.VMEM)] * 5,
        out_specs=pl.BlockSpec(memory_space=pltpu.VMEM),
        out_shape=jax.ShapeDtypeStruct((rows, total), jnp.bfloat16),
        cost_estimate=pl.CostEstimate(
            flops=8 * rows * total, bytes_accessed=4 * rows * total, transcendentals=rows
        ),
        name="normalize",
    )(z[None], *pieces, gain[None, :])


def local(
    query,
    keys,
    values,
    residual,
    out_weight,
    norm_gain,
    cand_len,
    head_w1,
    head_b1,
    head_w2,
    head_b2,
    head_w3,
    head_b3,
):
    z = lax.axis_index("z")
    xl = lax.axis_index("xl")
    core = lax.axis_index("core")
    y = lax.axis_index("y")
    xh = lax.axis_index("xh")

    lock = lax.optimization_barrier
    rows_half = out_weight.shape[0] // 2
    moved = [
        lax.ppermute(out_weight[v * rows_half : (v + 1) * rows_half], ALL, spread_moves(v))
        for v in range(2)
    ]
    attn_out, picked = attention(query, keys, values, residual, cand_len)
    here = lax.all_gather(attn_out, "y", axis=0, tiled=False)

    depth = attn_out.shape[1]
    width = out_weight.shape[1]
    near = lax.all_gather(picked, ("xl", "core"), axis=0, tiled=True)
    near, *moved = lock((near, *moved))
    moved = [lax.ppermute(m, ALL, column_moves(v)) for v, m in enumerate(moved)]
    rows = jnp.concatenate([near] + [from_ahead(near, "z", Z, s) for s in (1, 2, 3)], axis=0)
    own = jnp.dot(rows[:, :depth], out_weight, preferred_element_type=jnp.float32)
    res = rows[:, depth:]
    res = jnp.where(core == 0, res[:, :width], res[:, width:]).astype(jnp.float32)
    own = jnp.where((y == z) & (xh == xl), own + res, own).astype(jnp.bfloat16)
    pair = jnp.stack([own, from_ahead(own, "xh", XH, 1)])
    pair, held, *moved = lock((pair, attn_out, *moved))
    w = {(0, 0): jnp.stack(moved)}
    w[1, 0] = from_ahead(w[0, 0], "z", Z, 1)
    w[3, 0] = from_ahead(w[0, 0], "z", Z, 3)
    across = from_ahead(held, "xh", XH, 1)
    parts = [pair] + [from_ahead(pair, "y", Y, s) for s in (1, 2, 3)]
    pooled = sum(jnp.sum(p.astype(jnp.float32), axis=0) for p in parts).astype(jnp.bfloat16)
    pooled, across = lock((pooled, across))
    there = lax.all_gather(across, "y", axis=0, tiled=False)
    near = lax.all_gather(pooled, ("xl", "core"), axis=0, tiled=False)
    near, w[1, 0], w[3, 0], w[0, 0], here = lock((near, w[1, 0], w[3, 0], w[0, 0], here))
    pieces = [near] + [from_ahead(near, "z", Z, s) for s in (1, 2, 3)]
    w[0, 1] = from_ahead(w[0, 0], "xl", XL, 1)
    *pieces, w[1, 0], w[3, 0] = lock((*pieces, w[1, 0], w[3, 0]))
    w[2, 0] = [from_ahead(w[1, 0][0], "z", Z, 1), from_ahead(w[3, 0][1], "z", Z, 3)]
    features = normalize(pieces, norm_gain, z)
    features, w[0, 1], here, *w[2, 0] = lock((features, w[0, 1], here, *w[2, 0]))
    w[1, 1] = from_ahead(w[0, 1], "z", Z, 1)
    w[3, 1] = from_ahead(w[0, 1], "z", Z, 3)
    here_other = from_ahead(here, "core", CORE, 1)
    first = jax.nn.silu(
        jnp.dot(features, head_w1[0], preferred_element_type=jnp.float32) + head_b1[0]
    ).astype(jnp.bfloat16)
    terms = jnp.dot(first, head_w2[0], preferred_element_type=jnp.float32).astype(jnp.bfloat16)
    count = terms.shape[0] // Y
    terms = lax.all_to_all(
        terms.reshape(Y, count, terms.shape[1]), "y", split_axis=0, concat_axis=0, tiled=True
    )
    terms, there, w[0, 1], w[1, 1], w[3, 1], here_other = lock(
        (terms, there, w[0, 1], w[1, 1], w[3, 1], here_other)
    )
    there_other = from_ahead(there, "core", CORE, 1)
    w[2, 1] = [from_ahead(w[1, 1][0], "z", Z, 1), from_ahead(w[3, 1][1], "z", Z, 3)]
    half = jnp.sum(terms.astype(jnp.float32), axis=0).astype(jnp.bfloat16)
    other = from_ahead(half, "xh", XH, 1)

    sources = (here, here_other, there, there_other)

    def product(e, steps, trunk, dtype):
        items = [
            (s, v, w[s, e][v] if isinstance(w[s, e], list) else w[s, e])
            for s in steps
            for v in range(2)
        ]
        place = jnp.stack([lax.rem(y - z + Y, Y), lax.rem(xl + e + xh, XH)])
        return trunk_part(place, sources, items, trunk, dtype)

    trunk = product(0, range(Z), None, jnp.float32)
    other, trunk = lock((other, trunk))
    second = jax.nn.silu(half.astype(jnp.float32) + other.astype(jnp.float32) + head_b2[0])
    mine = jnp.sum(second * head_w3[0].astype(jnp.float32), axis=-1) + head_b3[0]
    scores = [mine] + [from_ahead(mine, "y", Y, s) for s in (1, 2, 3)]
    trunk = product(1, range(Z), trunk, jnp.bfloat16)
    *scores, trunk = lock((*scores, trunk))
    scores = jnp.roll(jnp.stack(scores), lax.rem(y + z, Y), axis=0).reshape(1, Y * count)
    row_count = residual.shape[0]
    mine = trunk[:row_count]
    other = from_ahead(trunk[row_count:], "core", CORE, 1)
    left, right = jnp.where(core == 0, mine, other), jnp.where(core == 0, other, mine)
    trunk = jnp.concatenate([left, right], axis=1).astype(jnp.float32)
    trunk_out = (trunk + residual.astype(jnp.float32)).astype(jnp.bfloat16)
    return (trunk_out, scores)


def solution(mesh):
    fine = Mesh(mesh.devices.reshape(Z, XL, CORE, Y, XH), ALL)
    in_specs = (
        P(MEMBER, TENSOR),
        P(MEMBER, TENSOR),
        P(MEMBER, TENSOR),
        P(MEMBER, TENSOR),
        P(TENSOR, MEMBER),
        P(),
        P(MEMBER),
        P(MEMBER, None, TENSOR),
        P(MEMBER, TENSOR),
        P(MEMBER, TENSOR, None),
        P(MEMBER, None),
        P(MEMBER, None),
        P(MEMBER),
    )
    out_specs = (P(MEMBER, TENSOR), P(MEMBER, None))
    return jax.shard_map(local, mesh=fine, in_specs=in_specs, out_specs=out_specs, check_vma=False)
```

```python
import functools
import itertools

import jax
import jax.numpy as jnp
from jax import lax
from jax.experimental import pallas as pl
from jax.experimental.pallas import tpu as pltpu
from jax.sharding import Mesh, PartitionSpec as P

HEAD_WIDTH = 128
Z, XL, CORE, Y, XH = 4, 2, 2, 4, 2
MEMBER = ("z", "xl", "core")
TENSOR = ("y", "xh")
ALL = MEMBER + TENSOR


def flat(z, xl, core, y, xh):
    return (((z % Z) * XL + xl % XL) * CORE + core) * Y * XH + (y % Y) * XH + xh % XH


def places():
    return itertools.product(range(Z), range(XL), range(CORE), range(Y), range(XH))


def spread_moves(v):
    return [
        (flat(z, xl, core, y, xh), flat(z - y - 2 * v, xl, core, y, xh))
        for z, xl, core, y, xh in places()
    ]


def column_moves(v):
    return [
        (flat(z, xl, core, y, xh), flat(z, xh, core, y + z + 2 * v, xl))
        for z, xl, core, y, xh in places()
    ]


def from_ahead(x, axis, size, step):
    return lax.ppermute(x, axis, [(i, (i - step) % size) for i in range(size)])


def attention_kernel(len_ref, query_ref, keys_ref, values_ref, residual_ref, out_ref, picked_ref):
    length = len_ref[pl.program_id(0)]
    slots, width = query_ref.shape
    heads = width // HEAD_WIDTH
    queries = jnp.concatenate(
        [query_ref[:, h * HEAD_WIDTH : (h + 1) * HEAD_WIDTH] for h in range(heads)], axis=0
    )
    logits = lax.dot_general(
        queries, keys_ref[...], (((1,), (1,)), ((), ())), preferred_element_type=jnp.float32
    ) * HEAD_WIDTH ** (-0.5)
    row = lax.rem(lax.broadcasted_iota(jnp.int32, logits.shape, 0), slots)
    column = lax.broadcasted_iota(jnp.int32, logits.shape, 1)
    allowed = (row >= column) & (column < length)
    logits = jnp.where(allowed, logits, jnp.float32(-1e30))
    row_max = jnp.max(logits, axis=-1, keepdims=True)
    probs = jnp.where(allowed, jnp.exp(logits - row_max), jnp.float32(0.0))
    totals = jnp.sum(probs, axis=-1, keepdims=True)
    weights = (probs / totals).astype(jnp.bfloat16)
    result = jnp.dot(weights, values_ref[...], preferred_element_type=jnp.float32)
    result = result.astype(jnp.bfloat16)
    scored = lax.broadcasted_iota(jnp.int32, (slots, 1), 0) == length - 1
    for h in range(heads):
        part = result[h * slots : (h + 1) * slots]
        out_ref[:, h * HEAD_WIDTH : (h + 1) * HEAD_WIDTH] = part
        picked_ref[0, :, h * HEAD_WIDTH : (h + 1) * HEAD_WIDTH] = jnp.sum(
            jnp.where(scored, part.astype(jnp.float32), 0.0), axis=0, keepdims=True
        ).astype(jnp.bfloat16)
    picked_ref[0, :, width:] = jnp.sum(
        jnp.where(scored, residual_ref[...].astype(jnp.float32), 0.0), axis=0, keepdims=True
    ).astype(jnp.bfloat16)


def attention(query, keys, values, residual, cand_len):
    count = cand_len.shape[0]
    slots = query.shape[0] // count
    wide = pl.BlockSpec((slots, query.shape[1]), lambda c, n: (c, 0))
    narrow = pl.BlockSpec((slots, keys.shape[1]), lambda c, n: (c, 0))
    picked_width = query.shape[1] + residual.shape[1]
    out, picked = pl.pallas_call(
        attention_kernel,
        grid_spec=pltpu.PrefetchScalarGridSpec(
            num_scalar_prefetch=1,
            grid=(count,),
            in_specs=[wide, narrow, narrow, wide],
            out_specs=[wide, pl.BlockSpec((1, 1, picked_width), lambda c, n: (c, 0, 0))],
        ),
        out_shape=[
            jax.ShapeDtypeStruct(query.shape, jnp.bfloat16),
            jax.ShapeDtypeStruct((count, 1, picked_width), jnp.bfloat16),
        ],
        cost_estimate=pl.CostEstimate(
            flops=4 * query.size * slots,
            bytes_accessed=6 * query.size,
            transcendentals=query.size,
        ),
        name="attention",
    )(cand_len, query, keys, values, residual)
    return out, picked.reshape(count, picked_width)


def trunk_kernel(picks, has_base, place_ref, *refs):
    count = len(picks)
    sources, blocks = refs[:4], refs[4 : 4 + count]
    base_ref = refs[4 + count] if has_base else None
    out_ref, acts, sems = refs[-3:]
    j = pl.program_id(0)

    depth = acts.shape[2] // count

    def copies(which, r):
        for i, (s, v) in enumerate(picks):
            group = lax.rem(place_ref[0] + 2 * Y - s - 2 * v, Y)
            yield pltpu.make_async_copy(
                sources[2 * which + r].at[group, :, pl.ds(v * depth, depth)],
                acts.at[r, :, pl.ds(i * depth, depth)],
                sems.at[r, i],
            )

    @pl.when(j == 0)
    def _():
        for which in range(2):

            @pl.when(place_ref[1] == which)
            def _():
                for r in range(CORE):
                    for copy in copies(which, r):
                        copy.start()

    for r in range(CORE):

        @pl.when(j == 2 * r)
        def _():
            for copy in copies(0, r):
                copy.wait()

    total = jnp.dot(
        acts[j // 2],
        jnp.concatenate([block[...] for block in blocks], axis=0),
        preferred_element_type=jnp.float32,
    )
    if has_base:
        total = total + base_ref[...]
    out_ref[...] = total.astype(out_ref.dtype)


def trunk_part(place, sources, terms, base, dtype):
    rows = sources[0].shape[1]
    depth = sources[0].shape[2] // 2
    width = terms[0][2].shape[-1]
    count = len(terms)

    def weight_spec(v, w):
        if w.ndim == 2:
            return pl.BlockSpec((depth, width // 2), lambda j, p: (0, lax.rem(j, 2)))
        return pl.BlockSpec((None, depth, width // 2), lambda j, p: (v, 0, lax.rem(j, 2)))

    tile = pl.BlockSpec((rows, width // 2), lambda j, p: (j // 2, lax.rem(j, 2)))
    return pl.pallas_call(
        functools.partial(trunk_kernel, [(s, v) for s, v, _ in terms], base is not None),
        grid_spec=pltpu.PrefetchScalarGridSpec(
            num_scalar_prefetch=1,
            grid=(2 * CORE,),
            in_specs=[pl.BlockSpec(memory_space=pltpu.HBM)] * 4
            + [weight_spec(v, w) for _, v, w in terms]
            + ([] if base is None else [tile]),
            out_specs=tile,
            scratch_shapes=[
                pltpu.VMEM((CORE, rows, count * depth), sources[0].dtype),
                pltpu.SemaphoreType.DMA((CORE, count)),
            ],
        ),
        out_shape=jax.ShapeDtypeStruct((CORE * rows, width), dtype),
        compiler_params=pltpu.CompilerParams(vmem_limit_bytes=32 * 2**20),
        cost_estimate=pl.CostEstimate(
            flops=CORE * rows * width, bytes_accessed=CORE * rows * width, transcendentals=0
        ),
        name="trunk_part",
    )(
        place,
        *[pltpu.with_memory_space_constraint(x, pltpu.HBM) for x in sources],
        *[t[2] for t in terms],
        *([] if base is None else [base]),
    )


def norm_kernel(place_ref, p0, p1, p2, p3, gain_ref, out_ref):
    pieces = (p0, p1, p2, p3)
    z = place_ref[0]
    group = p0.shape[1] // Z
    width = p0.shape[2]
    per_z = p0.shape[0]
    scales = []
    for r in range(Z):
        square = jnp.zeros((group, 1), jnp.float32)
        for s in range(Z):
            for q in range(per_z):
                rows = pieces[s][q, pl.ds(((r - s) % Z) * group, group), :].astype(jnp.float32)
                square = square + jnp.sum(rows * rows, axis=-1, keepdims=True)
        scales.append(lax.rsqrt(square / (Z * per_z * width) + 1e-05))
    for s in range(Z):
        for q in range(per_z):
            start = pl.multiple_of((lax.rem(z + s, Z) * per_z + q) * width, width)
            gain = gain_ref[:, pl.ds(start, width)]
            for r in range(Z):
                rows = pieces[s][q, pl.ds(((r - s) % Z) * group, group), :].astype(jnp.float32)
                out_ref[pl.ds(r * group, group), pl.ds(start, width)] = (
                    rows * scales[r] * gain
                ).astype(jnp.bfloat16)


def normalize(pieces, gain, z):
    per_z, rows, width = pieces[0].shape
    total = Z * per_z * width
    return pl.pallas_call(
        norm_kernel,
        in_specs=[pl.BlockSpec(memory_space=pltpu.SMEM)]
        + [pl.BlockSpec(memory_space=pltpu.VMEM)] * 5,
        out_specs=pl.BlockSpec(memory_space=pltpu.VMEM),
        out_shape=jax.ShapeDtypeStruct((rows, total), jnp.bfloat16),
        cost_estimate=pl.CostEstimate(
            flops=8 * rows * total, bytes_accessed=4 * rows * total, transcendentals=rows
        ),
        name="normalize",
    )(z[None], *pieces, gain[None, :])


def local(
    query,
    keys,
    values,
    residual,
    out_weight,
    norm_gain,
    cand_len,
    head_w1,
    head_b1,
    head_w2,
    head_b2,
    head_w3,
    head_b3,
):
    z = lax.axis_index("z")
    xl = lax.axis_index("xl")
    core = lax.axis_index("core")
    y = lax.axis_index("y")
    xh = lax.axis_index("xh")

    lock = lax.optimization_barrier
    rows_half = out_weight.shape[0] // 2
    moved = [
        lax.ppermute(out_weight[v * rows_half : (v + 1) * rows_half], ALL, spread_moves(v))
        for v in range(2)
    ]
    attn_out, picked = attention(query, keys, values, residual, cand_len)
    here = lax.all_gather(attn_out, "y", axis=0, tiled=False)

    depth = attn_out.shape[1]
    width = out_weight.shape[1]
    near = lax.all_gather(picked, ("xl", "core"), axis=0, tiled=True)
    near, *moved = lock((near, *moved))
    moved = [lax.ppermute(m, ALL, column_moves(v)) for v, m in enumerate(moved)]
    rows = jnp.concatenate([near] + [from_ahead(near, "z", Z, s) for s in (1, 2, 3)], axis=0)
    own = jnp.dot(rows[:, :depth], out_weight, preferred_element_type=jnp.float32)
    res = rows[:, depth:]
    res = jnp.where(core == 0, res[:, :width], res[:, width:]).astype(jnp.float32)
    own = jnp.where((y == z) & (xh == xl), own + res, own).astype(jnp.bfloat16)
    pair = jnp.stack([own, from_ahead(own, "xh", XH, 1)])
    pair, held, *moved = lock((pair, attn_out, *moved))
    w = {(0, 0): jnp.stack(moved)}
    w[1, 0] = from_ahead(w[0, 0], "z", Z, 1)
    w[3, 0] = from_ahead(w[0, 0], "z", Z, 3)
    across = from_ahead(held, "xh", XH, 1)
    parts = [pair] + [from_ahead(pair, "y", Y, s) for s in (1, 2, 3)]
    pooled = sum(jnp.sum(p.astype(jnp.float32), axis=0) for p in parts).astype(jnp.bfloat16)
    pooled, across = lock((pooled, across))
    there = lax.all_gather(across, "y", axis=0, tiled=False)
    near = lax.all_gather(pooled, ("xl", "core"), axis=0, tiled=False)
    near, w[1, 0], w[3, 0], w[0, 0], here = lock((near, w[1, 0], w[3, 0], w[0, 0], here))
    pieces = [near] + [from_ahead(near, "z", Z, s) for s in (1, 2, 3)]
    w[0, 1] = from_ahead(w[0, 0], "xl", XL, 1)
    here_other = from_ahead(here, "core", CORE, 1)
    *pieces, w[1, 0], w[3, 0] = lock((*pieces, w[1, 0], w[3, 0]))
    w[2, 0] = [from_ahead(w[1, 0][0], "z", Z, 1), from_ahead(w[3, 0][1], "z", Z, 3)]
    features = normalize(pieces, norm_gain, z)
    features, w[0, 1], here_other, *w[2, 0] = lock(
        (features, w[0, 1], here_other, *w[2, 0])
    )
    w[1, 1] = from_ahead(w[0, 1], "z", Z, 1)
    w[3, 1] = from_ahead(w[0, 1], "z", Z, 3)
    first = jax.nn.silu(
        jnp.dot(features, head_w1[0], preferred_element_type=jnp.float32) + head_b1[0]
    ).astype(jnp.bfloat16)
    terms = jnp.dot(first, head_w2[0], preferred_element_type=jnp.float32).astype(jnp.bfloat16)
    count = terms.shape[0] // Y
    terms = lax.all_to_all(
        terms.reshape(Y, count, terms.shape[1]), "y", split_axis=0, concat_axis=0, tiled=True
    )
    terms, there, w[1, 1], w[3, 1] = lock((terms, there, w[1, 1], w[3, 1]))
    there_other = from_ahead(there, "core", CORE, 1)
    w[2, 1] = [from_ahead(w[1, 1][0], "z", Z, 1), from_ahead(w[3, 1][1], "z", Z, 3)]
    half = jnp.sum(terms.astype(jnp.float32), axis=0).astype(jnp.bfloat16)
    other = from_ahead(half, "xh", XH, 1)

    sources = (here, here_other, there, there_other)

    def product(e, steps, trunk, dtype):
        items = [
            (s, v, w[s, e][v] if isinstance(w[s, e], list) else w[s, e])
            for s in steps
            for v in range(2)
        ]
        place = jnp.stack([lax.rem(y - z + Y, Y), lax.rem(xl + e + xh, XH)])
        return trunk_part(place, sources, items, trunk, dtype)

    trunk = product(0, range(Z), None, jnp.float32)
    other, trunk = lock((other, trunk))
    second = jax.nn.silu(half.astype(jnp.float32) + other.astype(jnp.float32) + head_b2[0])
    mine = jnp.sum(second * head_w3[0].astype(jnp.float32), axis=-1) + head_b3[0]
    scores = [mine] + [from_ahead(mine, "y", Y, s) for s in (1, 2, 3)]
    trunk = product(1, range(Z), trunk, jnp.bfloat16)
    *scores, trunk = lock((*scores, trunk))
    scores = jnp.roll(jnp.stack(scores), lax.rem(y + z, Y), axis=0).reshape(1, Y * count)
    row_count = residual.shape[0]
    mine = trunk[:row_count]
    other = from_ahead(trunk[row_count:], "core", CORE, 1)
    left, right = jnp.where(core == 0, mine, other), jnp.where(core == 0, other, mine)
    trunk = jnp.concatenate([left, right], axis=1).astype(jnp.float32)
    trunk_out = (trunk + residual.astype(jnp.float32)).astype(jnp.bfloat16)
    return (trunk_out, scores)


def solution(mesh):
    fine = Mesh(mesh.devices.reshape(Z, XL, CORE, Y, XH), ALL)
    in_specs = (
        P(MEMBER, TENSOR),
        P(MEMBER, TENSOR),
        P(MEMBER, TENSOR),
        P(MEMBER, TENSOR),
        P(TENSOR, MEMBER),
        P(),
        P(MEMBER),
        P(MEMBER, None, TENSOR),
        P(MEMBER, TENSOR),
        P(MEMBER, TENSOR, None),
        P(MEMBER, None),
        P(MEMBER, None),
        P(MEMBER),
    )
    out_specs = (P(MEMBER, TENSOR), P(MEMBER, None))
    return jax.shard_map(local, mesh=fine, in_specs=in_specs, out_specs=out_specs, check_vma=False)
```
